32 devices in a mesh: req: 16 (over z, y, x), blk: 2 (over core).
Axes of the slice: x: 2, y: 2, z: 4, core: 2. Of those that a mesh axis runs over, the one named last changes fastest.
Arguments:
- residual: bfloat16 [16, 48, 2048], P('req'), may hold values from -6 to 6
- queries: bfloat16 [16, 48, 16, 576], P('req', None, 'blk'), may hold values from -60 to 60, as said below
- new_latents: bfloat16 [16, 48, 576], P('req'), may hold values from -5 to 5
- latent_cache: bfloat16 [16, 768, 576], P('req', 'blk'), may hold values from -5 to 5
- lengths: int32 [16], replicated, may hold values from 1 to 760, as said below
- placement: int32 [16], replicated, may hold values from 0 to 15, each once
- parents: int32 [16, 48], replicated, may hold values from -1 to 46, as said below
- accepted: int32 [16, 8], replicated, may hold values from 0 to 47
- expert_ids: int32 [16, 48, 6], replicated, may hold values from 0 to 15, all different within a row; in each aligned block of 24 rows (0 to 23, 24 to 47, ..., all dimensions but the last counted through in order) at most 18 rows name the same one
- value_weight: bfloat16 [16, 512, 128], P('blk'), may hold values from -0.25 to 0.25
- out_weight: bfloat16 [2048, 2048], P('blk'), may hold values from -0.125 to 0.125
- norm_gain: bfloat16 [2048], replicated, may hold values from 0.25 to 1.75
- router_weight: bfloat16 [2048, 16], replicated, may hold values from -0.125 to 0.125
- gate_weight: bfloat16 [16, 2048, 1408], P('req', None, 'blk'), may hold values from -0.125 to 0.125
- up_weight: bfloat16 [16, 2048, 1408], P('req', None, 'blk'), may hold values from -0.125 to 0.125
- down_weight: bfloat16 [16, 1408, 2048], P('req', 'blk'), may hold values from -0.15625 to 0.15625
Outputs:
- layer_out: bfloat16 [16, 48, 2048], P('req', 'blk')
- updated_cache: bfloat16 [16, 768, 576], P('req', 'blk')
The draws below stay inside these ranges and needn't reach their ends.
Inputs may be any that keep to these rules, and one draw needn't show every extreme that they name: `lengths`: each request reads at least one and at most 760 cache positions; some request reads exactly that many. `parents`: draft 0 has parent -1; every other draft's parent is an earlier draft. `expert_ids`: the 6 experts of a draft differ. Split each request's drafts into aligned blocks of 24: no expert is named by more than 18 drafts of one block, and some expert reaches that in some block. `queries`: queries are of order one, except that some may be large multiples of a cache latent of their slot.
All inputs are finite; a program needn't handle non-finite values.
Results may differ from the reference program's by a relative error of at most 0.012.
Values may be sent and summed in bfloat16 or wider, within the bound.
A program may use at most 64 MiB of HBM per device.

```python
import math
import jax
import jax.numpy as jnp
import numpy as np
from jax import lax

D = 2048
HEADS = 16
LATENT = 512
ROPE = 64
VDIM = 128
EFF = 1408
TOP = 6
DRAFTS = 48
ACCEPT = 8
EXPERTS = 16
REQS = 16
CAP = 768
ROW_DEV = 24
LOCAL_CAP = 18
SLOT_CAP = 36
N_BLK = 2


def draw_latent_cache(key, part):
    values = jnp.clip(jax.random.normal(jax.random.fold_in(key, 7), (REQS, CAP, LATENT + ROPE), jnp.float32), -5.0, 5.0)
    return values.astype(jnp.bfloat16)


def draw_queries(key, part):
    values = jnp.clip(jax.random.normal(jax.random.fold_in(key, 5), (REQS, DRAFTS, HEADS, LATENT + ROPE), jnp.float32), -5.0, 5.0)
    return values.astype(jnp.bfloat16)


def draw_lengths(key, part):
    limit = CAP - ACCEPT
    values = jax.random.randint(jax.random.fold_in(key, 3), (REQS,), 1, limit + 1)
    where = jax.random.randint(jax.random.fold_in(key, 4), (), 0, REQS)
    return values.at[where].set(limit).astype(jnp.int32)


def draw_parents(key, part):
    index = jnp.arange(DRAFTS, dtype=jnp.int32)
    upper = jnp.maximum(index, 1)
    values = jax.random.randint(jax.random.fold_in(key, 21), (REQS, DRAFTS), 0, upper[None, :])
    values = jnp.where(index[None, :] == 0, -1, values)
    where = jax.random.randint(jax.random.fold_in(key, 22), (), 0, REQS)
    values = values.at[where, DRAFTS - 1].set(DRAFTS - 2)
    return values.astype(jnp.int32)


def touch_ends(values, rng, low, largest):
    dims = values.shape
    index_at = [jax.random.randint(jax.random.fold_in(rng, axis), (), 0, dims[axis]) for axis in range(len(dims))]
    values = values.at[tuple(index_at)].set(low)
    longest = dims.index(max(dims))
    index_at[longest] = (index_at[longest] + 1) % dims[longest]
    return values.at[tuple(index_at)].set(largest)


def levels(stream_key, dims, pieces, least, top_value):
    loudness, own = 1.0, jax.random.fold_in(stream_key, 6)
    for axis_at, blocks in pieces:
        steps = jnp.exp(jax.random.uniform(jax.random.fold_in(own, axis_at), (blocks,), jnp.float32, least / len(pieces), top_value / len(pieces)))
        loudness = loudness * jnp.repeat(steps, dims[axis_at] // blocks).reshape([-1 if axis == axis_at else 1 for axis in range(len(dims))])
    return loudness


def assign_block(rng, own, number, rows, amount, top, most, skew):
    order = jax.random.permutation(rng, amount)
    heavy_load, ordinary = load_shares(amount, rows * top, most, skew, True), load_shares(amount, rows * top, most, skew, False)
    places = jnp.arange(amount)

    def named(sizes, rotation):
        used = int((sizes > 0).sum())
        fixed = max(1, used // 4)
        moved = fixed + (places - fixed + rotation * (used - fixed)) % max(1, amount - fixed)
        return jnp.zeros((amount,), jnp.int32).at[order[jnp.where(places < fixed, places, moved)]].set(jnp.asarray(sizes, jnp.int32))

    sizes = jnp.where(number % 4 == 0, named(heavy_load, number // 4), named(ordinary, number - number // 4 - 1))
    mixed = jax.random.permutation(jax.random.fold_in(own, 3), amount)
    giver, receiver = mixed[0:amount // 2 * 2:2], mixed[1:amount // 2 * 2:2]
    slack = jnp.minimum(sizes[giver] - 1, most - sizes[receiver]) // 2
    slack = jnp.where((giver == order[0]) | (receiver == order[0]) | (sizes[receiver] == 0), 0, jnp.maximum(slack, 0))
    moved = jax.random.randint(jax.random.fold_in(own, 4), (amount // 2,), 0, 1 << 20) % (slack + 1)
    sizes = sizes.at[giver].add(-moved).at[receiver].add(moved)
    members = jnp.searchsorted(jnp.cumsum(sizes), jnp.arange(rows * top), side="right").astype(jnp.int32)
    listing = members.reshape(top, rows).T
    listing = listing[jax.random.permutation(jax.random.fold_in(own, 1), rows)]
    rotation = jax.random.randint(jax.random.fold_in(own, 2), (rows, 1), 0, top)
    return jnp.take_along_axis(listing, (jnp.arange(top)[None, :] + rotation) % top, axis=1)


def load_shares(amount, total, bound, slope, full):
    weights = [(1 << 20) // math.isqrt(rank ** slope) + 1 for rank in range(1, amount + 1)]
    largest = bound if full else min(bound, max(-(-total // amount), total * weights[0] // sum(weights)))
    least = 1 if total - largest >= amount - 1 else 0
    counts, spare = [largest] + [least] * (amount - 1), total - largest - least * (amount - 1)
    while spare > 0:
        free = [i for i in range(1, amount) if counts[i] < largest] or [i for i in range(1, amount) if counts[i] < bound]
        pool, left = sum([weights[i] for i in free]), spare
        for i in free:
            more = min(bound - counts[i], max(1, left * weights[i] // pool), spare)
            counts[i] = counts[i] + more
            spare = spare - more
    return np.array(counts)


def centred(key, extent, spread, most, pieces=(), kind=jnp.bfloat16):
    entries = jax.random.normal(key, extent, jnp.float32) * spread
    if len(pieces) > 0:
        entries = levels(key, extent, pieces, -0.22, 0.18) * entries
    return jnp.clip(entries, min=-most, max=most).astype(kind)


def setup_inputs(seed: int = 0) -> dict:
    key_of = jax.random.split(jax.random.key(seed), 17)
    residual = centred(key_of[0], (REQS, DRAFTS, D), 1.0, 6.0, ((0, 16),))
    queries = draw_queries(jax.random.fold_in(key_of[16], 71), 0)
    new_latents = centred(key_of[2], (REQS, DRAFTS, LATENT + ROPE), 1.0, 5.0, ((0, 16),))
    latent_cache = draw_latent_cache(jax.random.fold_in(key_of[16], 71), 0)
    lengths = draw_lengths(jax.random.fold_in(key_of[16], 71), 0)
    placement = jax.random.permutation(key_of[5], REQS).astype(jnp.int32)
    parents = draw_parents(jax.random.fold_in(key_of[16], 71), 0)
    accepted = touch_ends(jax.random.randint(key_of[7], (REQS, ACCEPT), 0, DRAFTS), jax.random.fold_in(key_of[7], 1), 0, DRAFTS - 1).astype(jnp.int32)
    expert_ids_keys = jax.random.split(jax.random.fold_in(key_of[8], 1), REQS * DRAFTS // ROW_DEV)
    expert_ids_turns = jax.random.permutation(jax.random.fold_in(key_of[8], 3), REQS * DRAFTS // ROW_DEV)
    expert_ids = jax.vmap(lambda own, number: assign_block(jax.random.fold_in(key_of[8], 2), own, number, ROW_DEV, EXPERTS, TOP, LOCAL_CAP, 2))(expert_ids_keys, expert_ids_turns).reshape((REQS, DRAFTS, TOP))
    value_weight = centred(key_of[9], (HEADS, LATENT, VDIM), LATENT ** -0.5, 0.25, ((0, 2),))
    out_weight = centred(key_of[10], (HEADS * VDIM, D), (HEADS * VDIM) ** -0.5, 0.125, ((0, 2),))
    norm_gain = jnp.clip(1.0 + 0.15 * jax.random.normal(key_of[11], (D,), jnp.float32), 0.25, 1.75).astype(jnp.bfloat16)
    router_weight = centred(key_of[12], (D, EXPERTS), D ** -0.5, 0.125)
    gate_weight = centred(key_of[13], (EXPERTS, D, EFF), D ** -0.5, 0.125, ((0, 16), (2, 2)))
    up_weight = centred(key_of[14], (EXPERTS, D, EFF), D ** -0.5, 0.125, ((0, 16), (2, 2)))
    down_weight = centred(key_of[15], (EXPERTS, EFF, D), EFF ** -0.5, 0.15625, ((0, 16), (1, 2)))
    return dict(residual=residual, queries=queries, new_latents=new_latents, latent_cache=latent_cache, lengths=lengths, placement=placement, parents=parents, accepted=accepted, expert_ids=expert_ids, value_weight=value_weight, out_weight=out_weight, norm_gain=norm_gain, router_weight=router_weight, gate_weight=gate_weight, up_weight=up_weight, down_weight=down_weight)


score_scale = 0.07216878364870322
route_scale = 2.446
norm_eps = 1e-06

def ancestors(parent_row):
    span = parent_row.shape[0]
    links = (parent_row[:, None] == jnp.arange(span, dtype=jnp.int32)[None, :]).astype(jnp.float32)
    reach = jnp.eye(span, dtype=jnp.float32) + links
    for _ in range(span.bit_length()):
        reach = jnp.minimum(jnp.dot(reach, reach, precision=lax.Precision.HIGHEST), 1.0)
    return reach

def attend(items):
    query, fresh, stored, length, parent_row = items
    query_f = query.astype(jnp.float32)
    cached = jnp.einsum('thc,jc->thj', query_f, stored.astype(jnp.float32), precision=lax.Precision.HIGHEST) * score_scale
    valid = jnp.arange(stored.shape[0], dtype=jnp.int32) < length
    cached = jnp.where(valid[None, None, :], cached, -jnp.inf)
    own = jnp.einsum('thc,uc->thu', query_f, fresh.astype(jnp.float32), precision=lax.Precision.HIGHEST) * score_scale
    reach = ancestors(parent_row)
    own = jnp.where(reach[:, None, :] > 0.5, own, -jnp.inf)
    top = jnp.maximum(lax.optimization_barrier(jnp.max(cached, axis=2)), lax.optimization_barrier(jnp.max(own, axis=2)))
    exp_cache = jnp.exp(cached - top[:, :, None])
    exp_own = jnp.exp(own - top[:, :, None])
    total = lax.optimization_barrier(jnp.sum(exp_cache, axis=2)) + lax.optimization_barrier(jnp.sum(exp_own, axis=2))
    prob_cache = exp_cache.astype(jnp.bfloat16).astype(jnp.float32)
    prob_own = exp_own.astype(jnp.bfloat16).astype(jnp.float32)
    acc = jnp.einsum('thj,jc->thc', prob_cache, stored[:, :LATENT].astype(jnp.float32), precision=lax.Precision.HIGHEST)
    acc = acc + jnp.einsum('thu,uc->thc', prob_own, fresh[:, :LATENT].astype(jnp.float32), precision=lax.Precision.HIGHEST)
    return (acc / total[:, :, None]).astype(jnp.bfloat16)

def reference(residual, queries, new_latents, latent_cache, lengths, placement, parents, accepted, expert_ids, value_weight, out_weight, norm_gain, router_weight, gate_weight, up_weight, down_weight):
    slot_len = lengths[placement]
    slot_par = parents[placement]
    slot_acc = accepted[placement]
    slot_ids = expert_ids[placement]
    context = lax.map(attend, (queries, new_latents, latent_cache, slot_len, slot_par))
    head_out = jnp.einsum('sthc,hcv->sthv', context.astype(jnp.float32), value_weight.astype(jnp.float32), precision=lax.Precision.HIGHEST).astype(jnp.bfloat16)
    attn = jnp.dot(head_out.reshape(REQS * DRAFTS, HEADS * VDIM), out_weight, preferred_element_type=jnp.float32)
    mid = residual.reshape(REQS * DRAFTS, D).astype(jnp.float32) + attn
    normed = (mid * lax.rsqrt(lax.optimization_barrier(jnp.mean(mid * mid, axis=1, keepdims=True)) + norm_eps) * norm_gain.astype(jnp.float32)).astype(jnp.bfloat16)
    score_e = jax.nn.sigmoid(jnp.dot(normed, router_weight, preferred_element_type=jnp.float32))
    ids = slot_ids.reshape(REQS * DRAFTS, TOP)
    pick = ids[:, :, None] == jnp.arange(EXPERTS, dtype=jnp.int32)[None, None, :]
    chosen = lax.optimization_barrier(jnp.sum(jnp.where(pick, score_e[:, None, :], 0.0), axis=2))
    gates = route_scale * chosen / lax.optimization_barrier(jnp.sum(chosen, axis=1, keepdims=True))
    weight_e = lax.optimization_barrier(jnp.sum(jnp.where(pick, gates[:, :, None], 0.0), axis=1)).reshape(REQS, DRAFTS, EXPERTS)
    routed = lax.optimization_barrier(jnp.sum(pick.astype(jnp.int32), axis=1)).reshape(REQS, DRAFTS, EXPERTS)
    position = jnp.cumsum(routed, axis=1) - routed
    normed3 = normed.reshape(REQS, DRAFTS, D).astype(jnp.float32)
    share = EFF // N_BLK
    slots = jnp.arange(SLOT_CAP, dtype=jnp.int32)

    def one_expert(total_moe, expert):
        pos_e = position[:, :, expert]
        hit_e = routed[:, :, expert] > 0
        select = ((pos_e[:, None, :] == slots[None, :, None]) & hit_e[:, None, :]).astype(jnp.float32)
        rows = jnp.einsum('sct,std->scd', select, normed3, precision=lax.Precision.HIGHEST).astype(jnp.bfloat16).reshape(REQS * SLOT_CAP, D)
        gate = jnp.dot(rows, gate_weight[expert], preferred_element_type=jnp.float32)
        upper = jnp.dot(rows, up_weight[expert], preferred_element_type=jnp.float32)
        act = (jax.nn.silu(gate) * upper).astype(jnp.bfloat16)
        shares = jnp.einsum('rbf,bfd->rbd', act.reshape(REQS * SLOT_CAP, N_BLK, share).astype(jnp.float32), down_weight[expert].reshape(N_BLK, share, D).astype(jnp.float32), precision=lax.Precision.HIGHEST).astype(jnp.bfloat16)
        part = lax.optimization_barrier(jnp.sum(shares.astype(jnp.float32), axis=1)).reshape(REQS, SLOT_CAP, D)
        back = jnp.einsum('sct,st,scd->std', select, weight_e[:, :, expert], part, precision=lax.Precision.HIGHEST)
        return (total_moe + back, None)
    moe, _ = lax.scan(one_expert, jnp.zeros((REQS, DRAFTS, D), jnp.float32), jnp.arange(EXPERTS, dtype=jnp.int32))
    layer_out = (mid.reshape(REQS, DRAFTS, D) + moe).astype(jnp.bfloat16)
    targets = slot_len[:, None] + jnp.arange(ACCEPT, dtype=jnp.int32)[None, :]
    rows_new = jnp.take_along_axis(new_latents, slot_acc[:, :, None], axis=1)
    updated_cache = latent_cache.at[jnp.arange(REQS, dtype=jnp.int32)[:, None], targets].set(rows_new)
    return (layer_out, updated_cache)
```

```python
import functools

import jax
import jax.numpy as jnp
from jax import lax
from jax.experimental import pallas as pl
from jax.experimental.pallas import tpu as pltpu
from jax.sharding import PartitionSpec as P

LATENT = 512
TOP = 6
MESH = pl.DeviceIdType.MESH
VMEM_LIMIT = 56 * 1024 * 1024
FUSED_ROWS = 1024
DEPTH = 4

score_scale = 0.07216878364870322
route_scale = 2.446
norm_eps = 1e-06
far_below = -1e30


def ancestors(parent_row):
    span = parent_row.shape[0]
    links = (parent_row[:, None] == jnp.arange(span, dtype=jnp.int32)[None, :]).astype(jnp.float32)
    reach = jnp.eye(span, dtype=jnp.float32) + links
    for _ in range(span.bit_length()):
        reach = jnp.minimum(jnp.dot(reach, reach, precision=lax.Precision.HIGHEST), 1.0)
    return reach


def attend_kernel(length_ref, query_ref, fresh_ref, keys_ref, reach_ref, value_ref, out_weight_ref, attn_ref):
    drafts = fresh_ref.shape[0]
    heads = value_ref.shape[0]
    lines = drafts * heads
    query, fresh, keys = query_ref[...], fresh_ref[...], keys_ref[...]
    line = lax.broadcasted_iota(jnp.int32, (lines, drafts), 0)
    first = lax.broadcasted_iota(jnp.int32, (lines, drafts), 1) * heads
    owner = ((line >= first) & (line < first + heads)).astype(jnp.float32)
    reach = jnp.dot(owner, reach_ref[...], preferred_element_type=jnp.float32)
    stored = jnp.dot(query, keys, preferred_element_type=jnp.float32) * score_scale
    where = lax.broadcasted_iota(jnp.int32, stored.shape, 1)
    stored = jnp.where(where < length_ref[0], stored, far_below)
    own = jnp.where(reach > 0.5, dot_nt(query, fresh) * score_scale, far_below)
    top = jnp.maximum(
        jnp.max(stored, axis=1, keepdims=True), jnp.max(own, axis=1, keepdims=True)
    )
    stored = jnp.exp(stored - top)
    own = jnp.exp(own - top)
    total = jnp.sum(stored, axis=1, keepdims=True) + jnp.sum(own, axis=1, keepdims=True)
    acc = dot_nt(stored.astype(jnp.bfloat16), keys[:LATENT]) + jnp.dot(
        own.astype(jnp.bfloat16), fresh[:, :LATENT], preferred_element_type=jnp.float32
    )
    context = (acc / total).astype(jnp.bfloat16)
    row = lax.broadcasted_iota(jnp.int32, (drafts, lines), 0) * heads
    column = lax.broadcasted_iota(jnp.int32, (drafts, lines), 1)
    outs = []
    for head in range(heads):
        select = (column == row + head).astype(jnp.bfloat16)
        one = jnp.dot(select, context, preferred_element_type=jnp.float32).astype(jnp.bfloat16)
        outs.append(
            jnp.dot(one, value_ref[head], preferred_element_type=jnp.float32).astype(jnp.bfloat16)
        )
    attn_ref[...] = jnp.dot(
        jnp.concatenate(outs, axis=1), out_weight_ref[...], preferred_element_type=jnp.float32
    )


def attend_slot(query, fresh, piece, length, parent_row, value_weight, out_weight):
    drafts, heads, width = query.shape
    vmem = pl.BlockSpec(memory_space=pltpu.VMEM)
    return pl.pallas_call(
        attend_kernel,
        out_shape=jax.ShapeDtypeStruct((drafts, out_weight.shape[1]), jnp.float32),
        in_specs=[pl.BlockSpec(memory_space=pltpu.SMEM)] + [vmem] * 6,
        out_specs=vmem,
        compiler_params=pltpu.CompilerParams(vmem_limit_bytes=VMEM_LIMIT),
    )(
        length.reshape(1),
        query.reshape(drafts * heads, width),
        fresh,
        piece.T,
        ancestors(parent_row),
        value_weight,
        out_weight,
    )


class Place:
    def __init__(self, n_req, n_blk):
        self.depth = n_req // 4
        self.n_blk = n_blk
        req = lax.axis_index("req")
        self.blk = lax.axis_index("blk")
        self.z = req // 4
        self.y = (req // 2) % 2
        self.x = req % 2
        self.swap = self.blk % 2
        self.a = self.y * (1 - self.swap) + self.x * self.swap
        self.b = self.x * (1 - self.swap) + self.y * self.swap
        self.home = self.group(self.a, self.b)

    def group(self, a, b):
        return a * (2 - self.swap) + b * (1 + self.swap)

    def device(self, z, a, b):
        return (z * 4 + self.group(a, b), self.blk)

    def far(self, step):
        return (self.z + step) % self.depth

    def a_side(self):
        return self.device(self.z, 1 - self.a, self.b)

    def b_side(self):
        return self.device(self.z, self.a, 1 - self.b)

    def z_side(self, step):
        return self.device(self.far(step), self.a, self.b)

    def sibling_blk(self, step):
        return (self.blk + step) % self.n_blk

    def sibling(self, step):
        return (self.z * 4 + self.home, self.sibling_blk(step))

    def greet(self):
        barrier = pltpu.get_barrier_semaphore()
        others = [self.a_side(), self.b_side()]
        others += [self.z_side(step) for step in range(1, self.depth)]
        others += [self.sibling(step) for step in range(1, self.n_blk)]
        for other in others:
            pl.semaphore_signal(barrier, inc=1, device_id=other, device_id_type=MESH)
        pl.semaphore_wait(barrier, len(others))


def send(src, dst, send_sem, recv_sem, target):
    return pltpu.make_async_remote_copy(
        src_ref=src,
        dst_ref=dst,
        send_sem=send_sem,
        recv_sem=recv_sem,
        device_id=target,
        device_id_type=MESH,
    )


def gather_kernel(
    n_req,
    n_blk,
    attn_ref,
    res_ref,
    gain_ref,
    mid_ref,
    rows_ref,
    outbox,
    inbox,
    box_send,
    box_recv,
    z_send,
    a_send,
    b_send,
    land,
    sib_send,
    sib_recv,
):
    at = Place(n_req, n_blk)
    depth, blk, home = at.depth, at.blk, at.home
    outbox[...] = attn_ref[...].astype(jnp.bfloat16)
    at.greet()
    swaps = []
    for step in range(1, n_blk):
        copy = send(
            outbox.at[at.sibling_blk(step)],
            inbox.at[step - 1],
            box_send.at[step - 1],
            box_recv.at[step - 1],
            at.sibling(step),
        )
        copy.start()
        swaps.append(copy)
    mid = res_ref[blk].astype(jnp.float32) + attn_ref[blk]
    for step in range(1, n_blk):
        swaps[step - 1].wait_recv()
        mid = mid + inbox[step - 1].astype(jnp.float32)
    mid_ref[...] = mid
    scale = lax.rsqrt(jnp.mean(mid * mid, axis=1, keepdims=True) + norm_eps)
    rows_ref[blk, home, at.z] = (mid * scale * gain_ref[...].astype(jnp.float32)).astype(jnp.bfloat16)

    waits = []

    def forward(group, z, send_sem, target):
        piece = rows_ref.at[blk, group, z]
        copy = send(piece, piece, send_sem, land.at[group, z], target)
        copy.start()
        waits.append(copy)

    def landed(group, z):
        piece = rows_ref.at[blk, group, z]
        send(piece, piece, z_send.at[0], land.at[group, z], at.a_side()).wait_recv()

    def share(group):
        for step in range(1, n_blk):
            block = rows_ref.at[blk, group]
            copy = send(
                block, block, sib_send.at[step - 1, group], sib_recv.at[step - 1, group], at.sibling(step)
            )
            copy.start()
            waits.append(copy)

    for step in range(1, depth):
        forward(home, at.z, z_send.at[step - 1], at.z_side(step))
    forward(home, at.z, b_send.at[0, 0], at.b_side())
    forward(home, at.z, a_send.at[0], at.a_side())
    for step in range(1, depth):
        z = at.far(step)
        landed(home, z)
        forward(home, z, b_send.at[0, step], at.b_side())
        forward(home, z, a_send.at[step], at.a_side())
    share(home)
    over = at.group(1 - at.a, at.b)
    for step in range(depth):
        z = at.far(step)
        landed(over, z)
        forward(over, z, b_send.at[1, step], at.b_side())
    share(over)
    for a in (at.a, 1 - at.a):
        group = at.group(a, 1 - at.b)
        for step in range(depth):
            landed(group, at.far(step))
        share(group)
    for step in range(1, n_blk):
        source = (blk + n_blk - step) % n_blk
        for group in range(4):
            block = rows_ref.at[source, group]
            send(
                block, block, sib_send.at[step - 1, group], sib_recv.at[step - 1, group], at.sibling(step)
            ).wait_recv()
    for copy in waits:
        copy.wait_send()
    for copy in swaps:
        copy.wait_send()


def gather_rows(attn, residual, gain, n_req, n_blk):
    _, rows, width = attn.shape
    depth = n_req // 4
    vmem = pl.BlockSpec(memory_space=pltpu.VMEM)
    dma = pltpu.SemaphoreType.DMA
    sibs = max(n_blk - 1, 1)
    return pl.pallas_call(
        functools.partial(gather_kernel, n_req, n_blk),
        out_shape=(
            jax.ShapeDtypeStruct((rows, width), jnp.float32),
            jax.ShapeDtypeStruct((n_blk, 4, depth, rows, width), jnp.bfloat16),
        ),
        in_specs=[vmem] * 3,
        out_specs=(vmem, vmem),
        scratch_shapes=[
            pltpu.VMEM((n_blk, rows, width), jnp.bfloat16),
            pltpu.VMEM((sibs, rows, width), jnp.bfloat16),
            dma((sibs,)),
            dma((sibs,)),
            dma((depth,)),
            dma((depth,)),
            dma((2, depth)),
            dma((4, depth)),
            dma((sibs, 4)),
            dma((sibs, 4)),
        ],
        compiler_params=pltpu.CompilerParams(
            collective_id=0, has_side_effects=True, vmem_limit_bytes=VMEM_LIMIT
        ),
    )(attn, residual, gain)


def scatter_kernel(
    n_req,
    n_blk,
    part_ref,
    mid_ref,
    out_ref,
    sib_in,
    b_in,
    a_in,
    z_in,
    sums,
    sib_send,
    sib_recv,
    b_send,
    b_recv,
    a_send,
    a_recv,
    z_send,
    z_recv,
):
    at = Place(n_req, n_blk)
    depth, blk = at.depth, at.blk
    at.greet()
    waits = []
    order = [
        at.group(1 - at.a, 1 - at.b),
        at.group(at.a, 1 - at.b),
        at.group(1 - at.a, at.b),
        at.home,
    ]

    def put(src, dst, send_sem, recv_sem, target):
        copy = send(src, dst, send_sem, recv_sem, target)
        copy.start()
        waits.append(copy)

    for k in range(4):
        for step in range(1, n_blk):
            other_swap = at.sibling_blk(step) % 2
            a = at.y * (1 - other_swap) + at.x * other_swap
            b = at.x * (1 - other_swap) + at.y * other_swap
            ta = a if k in (1, 3) else 1 - a
            tb = b if k in (2, 3) else 1 - b
            group = ta * (2 - other_swap) + tb * (1 + other_swap)
            put(
                part_ref.at[at.sibling_blk(step), group],
                sib_in.at[step - 1, k],
                sib_send.at[step - 1, k],
                sib_recv.at[step - 1, k],
                at.sibling(step),
            )

    def wait_sib(k):
        for step in range(1, n_blk):
            box = sib_in.at[step - 1, k]
            send(box, box, sib_send.at[step - 1, k], sib_recv.at[step - 1, k], at.sibling(step)).wait_recv()

    def own(k, z):
        total = part_ref[blk, order[k], z].astype(jnp.float32)
        for step in range(1, n_blk):
            total = total + sib_in[step - 1, k, z].astype(jnp.float32)
        return total

    def await_box(box, send_sem, recv_sem):
        send(box, box, send_sem, recv_sem, at.a_side()).wait_recv()

    steps = list(range(1, depth)) + [0]
    for k in (0, 1):
        wait_sib(k)
        for step in steps:
            z = at.far(step)
            sums[k, step] = own(k, z).astype(jnp.bfloat16)
            put(sums.at[k, step], b_in.at[k, step], b_send.at[k, step], b_recv.at[k, step], at.b_side())
    wait_sib(2)
    for step in steps:
        z = at.far(step)
        total = own(2, z)
        await_box(b_in.at[0, step], b_send.at[0, step], b_recv.at[0, step])
        sums[2, step] = (total + b_in[0, step].astype(jnp.float32)).astype(jnp.bfloat16)
        put(sums.at[2, step], a_in.at[step], a_send.at[step], a_recv.at[step], at.a_side())
    wait_sib(3)
    keep = None
    for step in steps:
        z = at.far(step)
        total = own(3, z)
        await_box(b_in.at[1, step], b_send.at[1, step], b_recv.at[1, step])
        total = total + b_in[1, step].astype(jnp.float32)
        await_box(a_in.at[step], a_send.at[step], a_recv.at[step])
        total = total + a_in[step].astype(jnp.float32)
        if step > 0:
            sums[3, step] = total.astype(jnp.bfloat16)
            put(sums.at[3, step], z_in.at[step - 1], z_send.at[step - 1], z_recv.at[step - 1], at.z_side(step))
        else:
            keep = total
    total = mid_ref[...] + keep
    for step in range(1, depth):
        await_box(z_in.at[step - 1], z_send.at[step - 1], z_recv.at[step - 1])
        total = total + z_in[step - 1].astype(jnp.float32)
    out_ref[...] = total.astype(jnp.bfloat16)
    for copy in waits:
        copy.wait_send()


def scatter_rows(parts, mid, n_req, n_blk):
    _, _, depth, rows, width = parts.shape
    vmem = pl.BlockSpec(memory_space=pltpu.VMEM)
    dma = pltpu.SemaphoreType.DMA
    sibs = max(n_blk - 1, 1)
    far = max(depth - 1, 1)
    box = lambda *dims: pltpu.VMEM(dims + (rows, width), jnp.bfloat16)
    return pl.pallas_call(
        functools.partial(scatter_kernel, n_req, n_blk),
        out_shape=jax.ShapeDtypeStruct((rows, width), jnp.bfloat16),
        in_specs=[vmem] * 2,
        out_specs=vmem,
        scratch_shapes=[
            box(sibs, 4, depth),
            box(2, depth),
            box(depth),
            box(far),
            box(4, depth),
            dma((sibs, 4)),
            dma((sibs, 4)),
            dma((2, depth)),
            dma((2, depth)),
            dma((depth,)),
            dma((depth,)),
            dma((far,)),
            dma((far,)),
        ],
        compiler_params=pltpu.CompilerParams(
            collective_id=1, has_side_effects=True, vmem_limit_bytes=VMEM_LIMIT
        ),
    )(parts, mid)


def dot_nt(left, right):
    return lax.dot_general(left, right, (((1,), (1,)), ((), ())), preferred_element_type=jnp.float32)


def whole_kernel(
    placement_ref,
    lengths_ref,
    accepted_ref,
    parents_hbm,
    ids_hbm,
    gain_hbm,
    router_hbm,
    res_hbm,
    query_hbm,
    fresh_hbm,
    keys_hbm,
    value_hbm,
    out_weight_hbm,
    gate_hbm,
    up_hbm,
    down_hbm,
    out_ref,
    updated_hbm,
    parents_ref,
    ids_ref,
    gain_ref,
    router_ref,
    res_ref,
    query_ref,
    fresh_ref,
    keys_ref,
    value_ref,
    out_weight_ref,
    gate_ref,
    up_ref,
    down_ref,
    gate_t,
    up_t,
    updated_ref,
    attn_ref,
    mid_ref,
    keep_ref,
    outbox,
    inbox,
    rows_ref,
    flat,
    x_ref,
    act_ref,
    named_ref,
    part_ref,
    b_in,
    a_in,
    z_in,
    over_sum,
    home_sum,
    local_sem,
    value_sem,
    swap_send,
    swap_recv,
    gz_send,
    ga_send,
    gb_send,
    land,
    rb_send,
    rb_recv,
    ra_send,
    ra_recv,
    rz_send,
    rz_recv,
):
    at = Place(4 * DEPTH, 2)
    blk, z, home = at.blk, at.z, at.home
    over = at.group(1 - at.a, at.b)
    side = at.group(at.a, 1 - at.b)
    far = at.group(1 - at.a, 1 - at.b)
    req = lax.axis_index("req")
    planes = [z, z + 1 - 2 * (z % 2), 2 - z // 2, 3 - 3 * (z // 2)]
    sibling = at.sibling(1)
    peers = [None] + [at.device(plane, at.a, at.b) for plane in planes[1:]]
    lines = query_ref.shape[0]
    drafts = fresh_ref.shape[0]
    heads = lines // drafts
    rows = mid_ref.shape[0]
    shard = keys_ref.shape[2]
    hidden = gate_ref.shape[1]
    waits = []

    barrier = pltpu.get_barrier_semaphore()
    partners = [sibling, at.a_side(), at.b_side()] + peers[1:]
    for partner in partners:
        pl.semaphore_signal(barrier, inc=1, device_id=partner, device_id_type=MESH)

    moves = [
        (query_hbm, query_ref),
        (keys_hbm, keys_ref.at[0]),
        (fresh_hbm, fresh_ref),
        (parents_hbm, parents_ref),
        (out_weight_hbm, out_weight_ref),
        (res_hbm, res_ref),
        (gain_hbm, gain_ref),
        (ids_hbm, ids_ref),
        (router_hbm, router_ref),
        (gate_hbm, gate_ref.at[0]),
        (up_hbm, up_ref.at[0]),
        (down_hbm, down_ref.at[0]),
    ]
    loads = [pltpu.make_async_copy(src, dst, local_sem.at[i]) for i, (src, dst) in enumerate(moves)]
    (
        query_load,
        keys_load,
        fresh_load,
        parents_load,
        out_weight_load,
        res_load,
        gain_load,
        ids_load,
        router_load,
        gate_load,
        up_load,
        down_load,
    ) = loads
    value_loads = [
        pltpu.make_async_copy(value_hbm.at[head], value_ref.at[:, pl.ds(head * 128, 128)], value_sem.at[head])
        for head in range(heads)
    ]
    for load in loads[:4] + value_loads + loads[4:]:
        load.start()

    def put(src, dst, send_sem, recv_sem, target):
        copy = send(src, dst, send_sem, recv_sem, target)
        copy.start()
        waits.append(copy)

    def await_box(box, send_sem, recv_sem):
        send(box, box, send_sem, recv_sem, sibling).wait_recv()

    swaps = [
        (keys_hbm, keys_ref.at[1]),
        (gate_hbm, gate_ref.at[1]),
        (up_hbm, up_ref.at[1]),
        (down_hbm, down_ref.at[1]),
    ]

    def swap(i):
        put(swaps[i][0], swaps[i][1], swap_send.at[i], swap_recv.at[i], sibling)

    def swapped(i):
        await_box(swaps[i][1], swap_send.at[i], swap_recv.at[i])

    request = placement_ref[req]
    length = lengths_ref[request]

    parents_load.wait()
    parent_row = parents_ref[pl.ds(request, 1), :]
    upper = lax.broadcasted_iota(jnp.int32, (drafts, drafts), 0)
    lower = lax.broadcasted_iota(jnp.int32, (drafts, drafts), 1)
    reach = (parent_row == upper).astype(jnp.float32) + (upper == lower).astype(jnp.float32)
    for _ in range(drafts.bit_length()):
        half = reach.astype(jnp.bfloat16)
        reach = jnp.minimum(jnp.dot(half, half, preferred_element_type=jnp.float32), 1.0)
    line = lax.broadcasted_iota(jnp.int32, (lines, drafts), 0)
    first = lax.broadcasted_iota(jnp.int32, (lines, drafts), 1) * heads
    owner = ((line >= first) & (line < first + heads)).astype(jnp.float32).astype(jnp.bfloat16)
    seen = dot_nt(owner, reach.astype(jnp.bfloat16))

    pl.semaphore_wait(barrier, len(partners))
    for i in range(4):
        swap(i)

    query_load.wait()
    fresh_load.wait()
    query, fresh = query_ref[...], fresh_ref[...]
    own = jnp.where(seen > 0.5, dot_nt(query, fresh) * score_scale, far_below)
    place = lax.broadcasted_iota(jnp.int32, (lines, shard), 1)

    def scores(i, start):
        stored = jnp.dot(query, keys_ref[i], preferred_element_type=jnp.float32) * score_scale
        return jnp.where(place + start < length, stored, far_below)

    keys_load.wait()
    near = scores(0, blk * shard)
    swapped(0)
    apart = scores(1, (1 - blk) * shard)
    top = jnp.maximum(
        jnp.maximum(jnp.max(near, axis=1, keepdims=True), jnp.max(apart, axis=1, keepdims=True)),
        jnp.max(own, axis=1, keepdims=True),
    )
    near, apart, own = jnp.exp(near - top), jnp.exp(apart - top), jnp.exp(own - top)
    total = (
        jnp.sum(near, axis=1, keepdims=True)
        + jnp.sum(apart, axis=1, keepdims=True)
        + jnp.sum(own, axis=1, keepdims=True)
    )
    acc = (
        dot_nt(near.astype(jnp.bfloat16), keys_ref[0, :LATENT])
        + dot_nt(apart.astype(jnp.bfloat16), keys_ref[1, :LATENT])
        + jnp.dot(own.astype(jnp.bfloat16), fresh[:, :LATENT], preferred_element_type=jnp.float32)
    )
    context = (acc * (1.0 / total)).astype(jnp.bfloat16)
    for load in value_loads:
        load.wait()
    every = jnp.dot(context, value_ref[...], preferred_element_type=jnp.float32)
    head_of = lax.broadcasted_iota(jnp.int32, every.shape, 0) % heads
    column_head = lax.broadcasted_iota(jnp.int32, every.shape, 1) // 128
    every = jnp.where(head_of == column_head, every, 0.0).astype(jnp.bfloat16)
    row = lax.broadcasted_iota(jnp.int32, (drafts, lines), 0) * heads
    column = lax.broadcasted_iota(jnp.int32, (drafts, lines), 1)
    gather = ((column >= row) & (column < row + heads)).astype(jnp.float32).astype(jnp.bfloat16)
    head_out = jnp.dot(gather, every, preferred_element_type=jnp.float32).astype(jnp.bfloat16)
    out_weight_load.wait()
    attn = jnp.dot(head_out, out_weight_ref[...], preferred_element_type=jnp.float32)
    attn_ref[0] = attn[:rows]
    attn_ref[1] = attn[rows:]
    outbox[...] = attn_ref[1 - blk].astype(jnp.bfloat16)
    put(outbox, inbox, swap_send.at[4], swap_recv.at[4], sibling)
    res_load.wait()
    gain_load.wait()
    mid = res_ref[blk].astype(jnp.float32) + attn_ref[blk]
    await_box(inbox, swap_send.at[4], swap_recv.at[4])
    mid = mid + inbox[...].astype(jnp.float32)
    mid_ref[...] = mid
    scale = lax.rsqrt(jnp.mean(mid * mid, axis=1, keepdims=True) + norm_eps)
    rows_ref[z, home] = (mid * scale * gain_ref[...].astype(jnp.float32)).astype(jnp.bfloat16)

    def forward(plane, group, send_sem, target):
        piece = rows_ref.at[plane, group]
        put(piece, piece, send_sem, land.at[plane, group], target)

    def landed(plane, group):
        await_box(rows_ref.at[plane, group], gz_send.at[0], land.at[plane, group])

    def spread_home(k):
        if k > 0:
            landed(planes[k], home)
        forward(planes[k], home, gb_send.at[0, k], at.b_side())
        forward(planes[k], home, ga_send.at[k], at.a_side())

    def spread_over(k):
        landed(planes[k], over)
        forward(planes[k], over, gb_send.at[1, k], at.b_side())

    forward(z, home, gz_send.at[1], peers[1])
    spread_home(0)
    forward(z, home, gz_send.at[2], peers[2])
    forward(z, home, gz_send.at[3], peers[3])

    pick_draft = lax.broadcasted_iota(jnp.int32, (drafts, shard), 0)
    pick_place = lax.broadcasted_iota(jnp.int32, (drafts, shard), 1)
    picked = jnp.zeros((drafts, shard), jnp.float32)
    for i in range(accepted_ref.shape[0]):
        target = length + i - blk * shard
        picked = jnp.where((pick_draft == accepted_ref[i, request]) & (pick_place == target), 1.0, picked)
    hit = jnp.max(picked, axis=0, keepdims=True)
    written = lax.dot_general(
        fresh, picked.astype(jnp.bfloat16), (((0,), (0,)), ((), ())), preferred_element_type=jnp.float32
    )
    updated_ref[...] = jnp.where(hit > 0.5, written, keys_ref[0].astype(jnp.float32)).astype(jnp.bfloat16)
    store = pltpu.make_async_copy(updated_ref, updated_hbm, local_sem.at[12])
    store.start()

    ids_load.wait()
    experts = router_ref.shape[0]
    expert_at = lax.broadcasted_iota(jnp.int32, (experts, drafts), 0)
    seat = (
        lax.broadcasted_iota(jnp.int32, (rows, drafts), 1)
        == lax.broadcasted_iota(jnp.int32, (rows, drafts), 0) + blk * rows
    ).astype(jnp.float32).astype(jnp.bfloat16)
    for k in range(DEPTH):
        for group in range(4):
            asked = placement_ref[planes[k] * 4 + group]
            names = jnp.zeros((experts, drafts), jnp.float32)
            for j in range(TOP):
                names = jnp.where(ids_ref[j, pl.ds(asked, 1), :] == expert_at, 1.0, names)
            named_ref[k, pl.ds(group * rows, rows), :] = dot_nt(seat, names.astype(jnp.bfloat16))

    def turn(i):
        for source, dest in ((gate_ref, gate_t), (up_ref, up_t)):
            for c in range(source.shape[2] // 256):
                dest[i, pl.ds(c * 256, 256), :] = source[i, :, pl.ds(c * 256, 256)].T

    def load_rows(k):
        for group in range(4):
            flat[pl.ds(group * rows, rows), :] = rows_ref[planes[k], group].astype(jnp.float32)
        x_ref[...] = flat[...].astype(jnp.bfloat16)

    def gate_of(k):
        chosen = named_ref[k] * jax.nn.sigmoid(dot_nt(x_ref[...], router_ref[...]))
        mine = lax.broadcasted_iota(jnp.int32, chosen.shape, 1) == req
        return (
            route_scale
            * jnp.sum(jnp.where(mine, chosen, 0.0), axis=1, keepdims=True)
            / jnp.sum(chosen, axis=1, keepdims=True)
        )

    def expand(i):
        x = x_ref[...]
        act_ref[i] = (
            jax.nn.silu(jnp.dot(x, gate_t[i], preferred_element_type=jnp.float32))
            * jnp.dot(x, up_t[i], preferred_element_type=jnp.float32)
        ).astype(jnp.bfloat16)

    def contract(k, gate):
        flat[...] = (
            jnp.dot(act_ref[0], down_ref[0], preferred_element_type=jnp.float32)
            + jnp.dot(act_ref[1], down_ref[1], preferred_element_type=jnp.float32)
        ) * gate
        for group in range(4):
            part_ref[k, group] = flat[pl.ds(group * rows, rows), :].astype(jnp.bfloat16)
        put(part_ref.at[k, far], b_in.at[0, k], rb_send.at[0, k], rb_recv.at[0, k], at.b_side())
        put(part_ref.at[k, side], b_in.at[1, k], rb_send.at[1, k], rb_recv.at[1, k], at.b_side())

    def sum_over(k):
        await_box(b_in.at[0, k], rb_send.at[0, k], rb_recv.at[0, k])
        over_sum[k] = (part_ref[k, over].astype(jnp.float32) + b_in[0, k].astype(jnp.float32)).astype(jnp.bfloat16)
        put(over_sum.at[k], a_in.at[k], ra_send.at[k], ra_recv.at[k], at.a_side())

    def sum_home(k):
        await_box(b_in.at[1, k], rb_send.at[1, k], rb_recv.at[1, k])
        here = part_ref[k, home].astype(jnp.float32) + b_in[1, k].astype(jnp.float32)
        await_box(a_in.at[k], ra_send.at[k], ra_recv.at[k])
        here = here + a_in[k].astype(jnp.float32)
        if k > 0:
            home_sum[k] = here.astype(jnp.bfloat16)
            put(home_sum.at[k], z_in.at[z], rz_send.at[k], rz_recv.at[z], peers[k])
        else:
            keep_ref[...] = mid_ref[...] + here

    gate_load.wait()
    up_load.wait()
    turn(0)
    spread_over(0)
    spread_home(1)
    swapped(1)
    swapped(2)
    turn(1)
    router_load.wait()
    spread_over(1)
    landed(z, side)
    landed(z, far)
    load_rows(0)
    gate = gate_of(0)
    expand(0)
    spread_home(2)
    expand(1)
    spread_over(2)
    down_load.wait()
    swapped(3)
    contract(0, gate)
    for k in range(1, DEPTH):
        landed(planes[k], side)
        landed(planes[k], far)
        load_rows(k)
        gate = gate_of(k)
        if k == 1:
            spread_home(3)
        expand(0)
        if k == 1:
            spread_over(3)
        sum_over(k - 1)
        expand(1)
        sum_home(k - 1)
        contract(k, gate)
    sum_over(DEPTH - 1)
    sum_home(DEPTH - 1)
    result = keep_ref[...]
    for k in range(1, DEPTH):
        await_box(z_in.at[planes[k]], rz_send.at[k], rz_recv.at[planes[k]])
        result = result + z_in[planes[k]].astype(jnp.float32)
    out_ref[...] = result.astype(jnp.bfloat16)
    store.wait()
    for copy in waits:
        copy.wait_send()


def whole_layer(
    residual,
    query,
    fresh,
    keys,
    lengths,
    placement,
    parents,
    accepted,
    expert_ids,
    value_weight,
    out_weight,
    gain,
    router_weight,
    gate_weight,
    up_weight,
    down_weight,
):
    n_blk, rows, width = residual.shape
    hidden = gate_weight.shape[0]
    shard = keys.shape[1]
    lines = query.shape[0]
    heads = value_weight.shape[0]
    experts = router_weight.shape[0]
    smem = pl.BlockSpec(memory_space=pltpu.SMEM)
    hbm = pl.BlockSpec(memory_space=pl.ANY)
    vmem = pl.BlockSpec(memory_space=pltpu.VMEM)
    dma = pltpu.SemaphoreType.DMA
    like = lambda a: pltpu.VMEM(a.shape, a.dtype)
    pair = lambda a: pltpu.VMEM((2,) + a.shape, a.dtype)
    box = lambda *dims: pltpu.VMEM(dims + (rows, width), jnp.bfloat16)
    f32 = lambda *dims: pltpu.VMEM(dims, jnp.float32)
    return pl.pallas_call(
        whole_kernel,
        out_shape=(
            jax.ShapeDtypeStruct((rows, width), jnp.bfloat16),
            jax.ShapeDtypeStruct(keys.shape, jnp.bfloat16),
        ),
        in_specs=[smem] * 3 + [hbm] * 13,
        out_specs=(vmem, hbm),
        scratch_shapes=[
            like(parents),
            like(expert_ids),
            like(gain),
            like(router_weight),
            like(residual),
            like(query),
            like(fresh),
            pair(keys),
            pltpu.VMEM((value_weight.shape[1], heads * value_weight.shape[2]), jnp.bfloat16),
            like(out_weight),
            pair(gate_weight),
            pair(up_weight),
            pair(down_weight),
            pltpu.VMEM((2, width, hidden), jnp.bfloat16),
            pltpu.VMEM((2, width, hidden), jnp.bfloat16),
            like(keys),
            f32(n_blk, rows, width),
            f32(rows, width),
            f32(rows, width),
            box(),
            box(),
            box(DEPTH, 4),
            f32(4 * rows, width),
            pltpu.VMEM((4 * rows, width), jnp.bfloat16),
            pltpu.VMEM((2, 4 * rows, hidden), jnp.bfloat16),
            f32(DEPTH, 4 * rows, experts),
            box(DEPTH, 4),
            box(2, DEPTH),
            box(DEPTH),
            box(DEPTH),
            box(DEPTH),
            box(DEPTH),
            dma((13,)),
            dma((heads,)),
            dma((5,)),
            dma((5,)),
            dma((DEPTH,)),
            dma((DEPTH,)),
            dma((2, DEPTH)),
            dma((DEPTH, 4)),
            dma((2, DEPTH)),
            dma((2, DEPTH)),
            dma((DEPTH,)),
            dma((DEPTH,)),
            dma((DEPTH,)),
            dma((DEPTH,)),
        ],
        compiler_params=pltpu.CompilerParams(
            collective_id=2, has_side_effects=True, vmem_limit_bytes=VMEM_LIMIT
        ),
    )(
        placement,
        lengths,
        accepted,
        parents,
        expert_ids,
        gain,
        router_weight,
        residual,
        query,
        fresh,
        keys,
        value_weight,
        out_weight,
        gate_weight,
        up_weight,
        down_weight,
    )


def on_device(
    residual,
    queries,
    new_latents,
    latent_cache,
    lengths,
    placement,
    parents,
    accepted,
    expert_ids,
    value_weight,
    out_weight,
    norm_gain,
    router_weight,
    gate_weight,
    up_weight,
    down_weight,
):
    req = lax.axis_index("req")
    block_index = lax.axis_index("blk")
    n_req = lax.axis_size("req")
    n_blk = lax.axis_size("blk")
    drafts = residual.shape[1]
    width = residual.shape[2]
    shard_len = latent_cache.shape[1]
    experts = router_weight.shape[1]
    rows_here = drafts // n_blk
    depth = n_req // 4
    if n_req == 4 * DEPTH and n_blk == 2 and n_blk * n_req * rows_here <= FUSED_ROWS:
        layer_out, updated = whole_layer(
            residual[0].reshape(n_blk, rows_here, width),
            queries[0].reshape(drafts * queries.shape[2], queries.shape[3]),
            new_latents[0],
            latent_cache[0].T,
            lengths,
            placement,
            parents,
            accepted.T,
            expert_ids.transpose(2, 0, 1),
            value_weight,
            out_weight,
            norm_gain.reshape(1, width),
            router_weight.T,
            gate_weight[0].T,
            up_weight[0].T,
            down_weight[0],
        )
        return (layer_out[None], updated.T[None])

    request = lax.dynamic_index_in_dim(placement, req, 0, keepdims=False)
    length = lax.dynamic_index_in_dim(lengths, request, 0, keepdims=False)
    parent_row = lax.dynamic_index_in_dim(parents, request, 0, keepdims=False)
    taken = lax.dynamic_index_in_dim(accepted, request, 0, keepdims=False)

    named = jnp.any(
        expert_ids[:, :, :, None] == jnp.arange(experts, dtype=jnp.int32), axis=2
    ).astype(jnp.bfloat16)
    seat = (placement[:, None] == jnp.arange(n_req, dtype=jnp.int32)[None, :]).astype(jnp.bfloat16)
    named = jnp.einsum("sr,rte->ste", seat, named, preferred_element_type=jnp.float32)
    named = named.reshape(depth, 4, n_blk, rows_here, experts)

    piece = lax.all_gather(latent_cache[0], "blk", axis=0, tiled=True)
    attn = attend_slot(
        queries[0], new_latents[0], piece, length, parent_row, value_weight, out_weight
    )
    attn = attn.reshape(n_blk, rows_here, width)
    home_rows = residual.reshape(n_blk, rows_here, width)
    gain = norm_gain.reshape(1, width)
    mid, gathered = gather_rows(attn, home_rows, gain, n_req, n_blk)
    rows = gathered.reshape(n_req * drafts, width)
    score_e = jax.nn.sigmoid(jnp.dot(rows, router_weight, preferred_element_type=jnp.float32))
    chosen = named.transpose(2, 1, 0, 3, 4).reshape(n_req * drafts, experts) * score_e
    mine = jnp.arange(experts, dtype=jnp.int32)[None, :] == req
    gate = (
        route_scale
        * jnp.sum(jnp.where(mine, chosen, 0.0), axis=1, keepdims=True)
        / jnp.sum(chosen, axis=1, keepdims=True)
    )
    act = (
        jax.nn.silu(jnp.dot(rows, gate_weight[0], preferred_element_type=jnp.float32))
        * jnp.dot(rows, up_weight[0], preferred_element_type=jnp.float32)
    ).astype(jnp.bfloat16)
    parts = jnp.dot(act, down_weight[0], preferred_element_type=jnp.float32) * gate
    parts = parts.astype(jnp.bfloat16).reshape(n_blk, 4, depth, rows_here, width)
    layer_out = scatter_rows(parts, mid, n_req, n_blk)

    stored = latent_cache[0]
    chosen_rows = new_latents[0][taken]
    targets = length + jnp.arange(taken.shape[0], dtype=jnp.int32) - block_index * shard_len
    hit = jnp.arange(shard_len, dtype=jnp.int32)[:, None] == targets[None, :]
    written = jnp.dot(
        hit.astype(jnp.bfloat16), chosen_rows, preferred_element_type=jnp.float32
    ).astype(jnp.bfloat16)
    updated = jnp.where(jnp.any(hit, axis=1)[:, None], written, stored)
    return (layer_out[None], updated[None])


def solution(mesh):
    return jax.shard_map(
        on_device,
        mesh=mesh,
        in_specs=(
            P("req", None, None),
            P("req", None, "blk", None),
            P("req", None, None),
            P("req", "blk", None),
            P(),
            P(),
            P(),
            P(),
            P(),
            P("blk", None, None),
            P("blk", None),
            P(),
            P(),
            P("req", None, "blk"),
            P("req", None, "blk"),
            P("req", "blk", None),
        ),
        out_specs=(P("req", "blk", None), P("req", "blk", None)),
        check_vma=False,
    )
```

```python
import functools

import jax
import jax.numpy as jnp
from jax import lax
from jax.experimental import pallas as pl
from jax.experimental.pallas import tpu as pltpu
from jax.sharding import PartitionSpec as P

LATENT = 512
TOP = 6
MESH = pl.DeviceIdType.MESH
VMEM_LIMIT = 56 * 1024 * 1024
FUSED_ROWS = 1024
DEPTH = 4

score_scale = 0.07216878364870322
route_scale = 2.446
norm_eps = 1e-06
far_below = -1e30


def ancestors(parent_row):
    span = parent_row.shape[0]
    links = (parent_row[:, None] == jnp.arange(span, dtype=jnp.int32)[None, :]).astype(jnp.float32)
    reach = jnp.eye(span, dtype=jnp.float32) + links
    for _ in range(span.bit_length()):
        reach = jnp.minimum(jnp.dot(reach, reach, precision=lax.Precision.HIGHEST), 1.0)
    return reach


def attend_kernel(length_ref, query_ref, fresh_ref, keys_ref, reach_ref, value_ref, out_weight_ref, attn_ref):
    drafts = fresh_ref.shape[0]
    heads = value_ref.shape[0]
    lines = drafts * heads
    query, fresh, keys = query_ref[...], fresh_ref[...], keys_ref[...]
    line = lax.broadcasted_iota(jnp.int32, (lines, drafts), 0)
    first = lax.broadcasted_iota(jnp.int32, (lines, drafts), 1) * heads
    owner = ((line >= first) & (line < first + heads)).astype(jnp.float32)
    reach = jnp.dot(owner, reach_ref[...], preferred_element_type=jnp.float32)
    stored = jnp.dot(query, keys, preferred_element_type=jnp.float32) * score_scale
    where = lax.broadcasted_iota(jnp.int32, stored.shape, 1)
    stored = jnp.where(where < length_ref[0], stored, far_below)
    own = jnp.where(reach > 0.5, dot_nt(query, fresh) * score_scale, far_below)
    top = jnp.maximum(
        jnp.max(stored, axis=1, keepdims=True), jnp.max(own, axis=1, keepdims=True)
    )
    stored = jnp.exp(stored - top)
    own = jnp.exp(own - top)
    total = jnp.sum(stored, axis=1, keepdims=True) + jnp.sum(own, axis=1, keepdims=True)
    acc = dot_nt(stored.astype(jnp.bfloat16), keys[:LATENT]) + jnp.dot(
        own.astype(jnp.bfloat16), fresh[:, :LATENT], preferred_element_type=jnp.float32
    )
    context = (acc / total).astype(jnp.bfloat16)
    row = lax.broadcasted_iota(jnp.int32, (drafts, lines), 0) * heads
    column = lax.broadcasted_iota(jnp.int32, (drafts, lines), 1)
    outs = []
    for head in range(heads):
        select = (column == row + head).astype(jnp.bfloat16)
        one = jnp.dot(select, context, preferred_element_type=jnp.float32).astype(jnp.bfloat16)
        outs.append(
            jnp.dot(one, value_ref[head], preferred_element_type=jnp.float32).astype(jnp.bfloat16)
        )
    attn_ref[...] = jnp.dot(
        jnp.concatenate(outs, axis=1), out_weight_ref[...], preferred_element_type=jnp.float32
    )


def attend_slot(query, fresh, piece, length, parent_row, value_weight, out_weight):
    drafts, heads, width = query.shape
    vmem = pl.BlockSpec(memory_space=pltpu.VMEM)
    return pl.pallas_call(
        attend_kernel,
        out_shape=jax.ShapeDtypeStruct((drafts, out_weight.shape[1]), jnp.float32),
        in_specs=[pl.BlockSpec(memory_space=pltpu.SMEM)] + [vmem] * 6,
        out_specs=vmem,
        compiler_params=pltpu.CompilerParams(vmem_limit_bytes=VMEM_LIMIT),
    )(
        length.reshape(1),
        query.reshape(drafts * heads, width),
        fresh,
        piece.T,
        ancestors(parent_row),
        value_weight,
        out_weight,
    )


class Place:
    def __init__(self, n_req, n_blk):
        self.depth = n_req // 4
        self.n_blk = n_blk
        req = lax.axis_index("req")
        self.blk = lax.axis_index("blk")
        self.z = req // 4
        self.y = (req // 2) % 2
        self.x = req % 2
        self.swap = self.blk % 2
        self.a = self.y * (1 - self.swap) + self.x * self.swap
        self.b = self.x * (1 - self.swap) + self.y * self.swap
        self.home = self.group(self.a, self.b)

    def group(self, a, b):
        return a * (2 - self.swap) + b * (1 + self.swap)

    def device(self, z, a, b):
        return (z * 4 + self.group(a, b), self.blk)

    def far(self, step):
        return (self.z + step) % self.depth

    def a_side(self):
        return self.device(self.z, 1 - self.a, self.b)

    def b_side(self):
        return self.device(self.z, self.a, 1 - self.b)

    def z_side(self, step):
        return self.device(self.far(step), self.a, self.b)

    def sibling_blk(self, step):
        return (self.blk + step) % self.n_blk

    def sibling(self, step):
        return (self.z * 4 + self.home, self.sibling_blk(step))

    def greet(self):
        barrier = pltpu.get_barrier_semaphore()
        others = [self.a_side(), self.b_side()]
        others += [self.z_side(step) for step in range(1, self.depth)]
        others += [self.sibling(step) for step in range(1, self.n_blk)]
        for other in others:
            pl.semaphore_signal(barrier, inc=1, device_id=other, device_id_type=MESH)
        pl.semaphore_wait(barrier, len(others))


def send(src, dst, send_sem, recv_sem, target):
    return pltpu.make_async_remote_copy(
        src_ref=src,
        dst_ref=dst,
        send_sem=send_sem,
        recv_sem=recv_sem,
        device_id=target,
        device_id_type=MESH,
    )


def gather_kernel(
    n_req,
    n_blk,
    attn_ref,
    res_ref,
    gain_ref,
    mid_ref,
    rows_ref,
    outbox,
    inbox,
    box_send,
    box_recv,
    z_send,
    a_send,
    b_send,
    land,
    sib_send,
    sib_recv,
):
    at = Place(n_req, n_blk)
    depth, blk, home = at.depth, at.blk, at.home
    outbox[...] = attn_ref[...].astype(jnp.bfloat16)
    at.greet()
    swaps = []
    for step in range(1, n_blk):
        copy = send(
            outbox.at[at.sibling_blk(step)],
            inbox.at[step - 1],
            box_send.at[step - 1],
            box_recv.at[step - 1],
            at.sibling(step),
        )
        copy.start()
        swaps.append(copy)
    mid = res_ref[blk].astype(jnp.float32) + attn_ref[blk]
    for step in range(1, n_blk):
        swaps[step - 1].wait_recv()
        mid = mid + inbox[step - 1].astype(jnp.float32)
    mid_ref[...] = mid
    scale = lax.rsqrt(jnp.mean(mid * mid, axis=1, keepdims=True) + norm_eps)
    rows_ref[blk, home, at.z] = (mid * scale * gain_ref[...].astype(jnp.float32)).astype(jnp.bfloat16)

    waits = []

    def forward(group, z, send_sem, target):
        piece = rows_ref.at[blk, group, z]
        copy = send(piece, piece, send_sem, land.at[group, z], target)
        copy.start()
        waits.append(copy)

    def landed(group, z):
        piece = rows_ref.at[blk, group, z]
        send(piece, piece, z_send.at[0], land.at[group, z], at.a_side()).wait_recv()

    def share(group):
        for step in range(1, n_blk):
            block = rows_ref.at[blk, group]
            copy = send(
                block, block, sib_send.at[step - 1, group], sib_recv.at[step - 1, group], at.sibling(step)
            )
            copy.start()
            waits.append(copy)

    for step in range(1, depth):
        forward(home, at.z, z_send.at[step - 1], at.z_side(step))
    forward(home, at.z, b_send.at[0, 0], at.b_side())
    forward(home, at.z, a_send.at[0], at.a_side())
    for step in range(1, depth):
        z = at.far(step)
        landed(home, z)
        forward(home, z, b_send.at[0, step], at.b_side())
        forward(home, z, a_send.at[step], at.a_side())
    share(home)
    over = at.group(1 - at.a, at.b)
    for step in range(depth):
        z = at.far(step)
        landed(over, z)
        forward(over, z, b_send.at[1, step], at.b_side())
    share(over)
    for a in (at.a, 1 - at.a):
        group = at.group(a, 1 - at.b)
        for step in range(depth):
            landed(group, at.far(step))
        share(group)
    for step in range(1, n_blk):
        source = (blk + n_blk - step) % n_blk
        for group in range(4):
            block = rows_ref.at[source, group]
            send(
                block, block, sib_send.at[step - 1, group], sib_recv.at[step - 1, group], at.sibling(step)
            ).wait_recv()
    for copy in waits:
        copy.wait_send()
    for copy in swaps:
        copy.wait_send()


def gather_rows(attn, residual, gain, n_req, n_blk):
    _, rows, width = attn.shape
    depth = n_req // 4
    vmem = pl.BlockSpec(memory_space=pltpu.VMEM)
    dma = pltpu.SemaphoreType.DMA
    sibs = max(n_blk - 1, 1)
    return pl.pallas_call(
        functools.partial(gather_kernel, n_req, n_blk),
        out_shape=(
            jax.ShapeDtypeStruct((rows, width), jnp.float32),
            jax.ShapeDtypeStruct((n_blk, 4, depth, rows, width), jnp.bfloat16),
        ),
        in_specs=[vmem] * 3,
        out_specs=(vmem, vmem),
        scratch_shapes=[
            pltpu.VMEM((n_blk, rows, width), jnp.bfloat16),
            pltpu.VMEM((sibs, rows, width), jnp.bfloat16),
            dma((sibs,)),
            dma((sibs,)),
            dma((depth,)),
            dma((depth,)),
            dma((2, depth)),
            dma((4, depth)),
            dma((sibs, 4)),
            dma((sibs, 4)),
        ],
        compiler_params=pltpu.CompilerParams(
            collective_id=0, has_side_effects=True, vmem_limit_bytes=VMEM_LIMIT
        ),
    )(attn, residual, gain)


def scatter_kernel(
    n_req,
    n_blk,
    part_ref,
    mid_ref,
    out_ref,
    sib_in,
    b_in,
    a_in,
    z_in,
    sums,
    sib_send,
    sib_recv,
    b_send,
    b_recv,
    a_send,
    a_recv,
    z_send,
    z_recv,
):
    at = Place(n_req, n_blk)
    depth, blk = at.depth, at.blk
    at.greet()
    waits = []
    order = [
        at.group(1 - at.a, 1 - at.b),
        at.group(at.a, 1 - at.b),
        at.group(1 - at.a, at.b),
        at.home,
    ]

    def put(src, dst, send_sem, recv_sem, target):
        copy = send(src, dst, send_sem, recv_sem, target)
        copy.start()
        waits.append(copy)

    for k in range(4):
        for step in range(1, n_blk):
            other_swap = at.sibling_blk(step) % 2
            a = at.y * (1 - other_swap) + at.x * other_swap
            b = at.x * (1 - other_swap) + at.y * other_swap
            ta = a if k in (1, 3) else 1 - a
            tb = b if k in (2, 3) else 1 - b
            group = ta * (2 - other_swap) + tb * (1 + other_swap)
            put(
                part_ref.at[at.sibling_blk(step), group],
                sib_in.at[step - 1, k],
                sib_send.at[step - 1, k],
                sib_recv.at[step - 1, k],
                at.sibling(step),
            )

    def wait_sib(k):
        for step in range(1, n_blk):
            box = sib_in.at[step - 1, k]
            send(box, box, sib_send.at[step - 1, k], sib_recv.at[step - 1, k], at.sibling(step)).wait_recv()

    def own(k, z):
        total = part_ref[blk, order[k], z].astype(jnp.float32)
        for step in range(1, n_blk):
            total = total + sib_in[step - 1, k, z].astype(jnp.float32)
        return total

    def await_box(box, send_sem, recv_sem):
        send(box, box, send_sem, recv_sem, at.a_side()).wait_recv()

    steps = list(range(1, depth)) + [0]
    for k in (0, 1):
        wait_sib(k)
        for step in steps:
            z = at.far(step)
            sums[k, step] = own(k, z).astype(jnp.bfloat16)
            put(sums.at[k, step], b_in.at[k, step], b_send.at[k, step], b_recv.at[k, step], at.b_side())
    wait_sib(2)
    for step in steps:
        z = at.far(step)
        total = own(2, z)
        await_box(b_in.at[0, step], b_send.at[0, step], b_recv.at[0, step])
        sums[2, step] = (total + b_in[0, step].astype(jnp.float32)).astype(jnp.bfloat16)
        put(sums.at[2, step], a_in.at[step], a_send.at[step], a_recv.at[step], at.a_side())
    wait_sib(3)
    keep = None
    for step in steps:
        z = at.far(step)
        total = own(3, z)
        await_box(b_in.at[1, step], b_send.at[1, step], b_recv.at[1, step])
        total = total + b_in[1, step].astype(jnp.float32)
        await_box(a_in.at[step], a_send.at[step], a_recv.at[step])
        total = total + a_in[step].astype(jnp.float32)
        if step > 0:
            sums[3, step] = total.astype(jnp.bfloat16)
            put(sums.at[3, step], z_in.at[step - 1], z_send.at[step - 1], z_recv.at[step - 1], at.z_side(step))
        else:
            keep = total
    total = mid_ref[...] + keep
    for step in range(1, depth):
        await_box(z_in.at[step - 1], z_send.at[step - 1], z_recv.at[step - 1])
        total = total + z_in[step - 1].astype(jnp.float32)
    out_ref[...] = total.astype(jnp.bfloat16)
    for copy in waits:
        copy.wait_send()


def scatter_rows(parts, mid, n_req, n_blk):
    _, _, depth, rows, width = parts.shape
    vmem = pl.BlockSpec(memory_space=pltpu.VMEM)
    dma = pltpu.SemaphoreType.DMA
    sibs = max(n_blk - 1, 1)
    far = max(depth - 1, 1)
    box = lambda *dims: pltpu.VMEM(dims + (rows, width), jnp.bfloat16)
    return pl.pallas_call(
        functools.partial(scatter_kernel, n_req, n_blk),
        out_shape=jax.ShapeDtypeStruct((rows, width), jnp.bfloat16),
        in_specs=[vmem] * 2,
        out_specs=vmem,
        scratch_shapes=[
            box(sibs, 4, depth),
            box(2, depth),
            box(depth),
            box(far),
            box(4, depth),
            dma((sibs, 4)),
            dma((sibs, 4)),
            dma((2, depth)),
            dma((2, depth)),
            dma((depth,)),
            dma((depth,)),
            dma((far,)),
            dma((far,)),
        ],
        compiler_params=pltpu.CompilerParams(
            collective_id=1, has_side_effects=True, vmem_limit_bytes=VMEM_LIMIT
        ),
    )(parts, mid)


def dot_nt(left, right):
    return lax.dot_general(left, right, (((1,), (1,)), ((), ())), preferred_element_type=jnp.float32)


def whole_kernel(
    placement_ref,
    lengths_ref,
    accepted_ref,
    parents_hbm,
    ids_hbm,
    gain_hbm,
    router_hbm,
    res_hbm,
    query_hbm,
    fresh_hbm,
    keys_hbm,
    value_hbm,
    out_weight_hbm,
    gate_hbm,
    up_hbm,
    down_hbm,
    out_ref,
    updated_ref,
    parents_ref,
    ids_ref,
    gain_ref,
    router_ref,
    res_ref,
    query_ref,
    fresh_ref,
    keys_ref,
    value_ref,
    out_weight_ref,
    gate_ref,
    up_ref,
    down_ref,
    gate_t,
    up_t,
    attn_ref,
    mid_ref,
    keep_ref,
    outbox,
    inbox,
    rows_ref,
    flat,
    x_ref,
    act_ref,
    named_ref,
    part_ref,
    b_in,
    a_in,
    z_in,
    over_sum,
    home_sum,
    local_sem,
    value_sem,
    swap_send,
    swap_recv,
    gz_send,
    ga_send,
    gb_send,
    land,
    rb_send,
    rb_recv,
    ra_send,
    ra_recv,
    rz_send,
    rz_recv,
):
    at = Place(4 * DEPTH, 2)
    blk, z, home = at.blk, at.z, at.home
    over = at.group(1 - at.a, at.b)
    side = at.group(at.a, 1 - at.b)
    far = at.group(1 - at.a, 1 - at.b)
    req = lax.axis_index("req")
    planes = [z, z + 1 - 2 * (z % 2), 2 - z // 2, 3 - 3 * (z // 2)]
    sibling = at.sibling(1)
    peers = [None] + [at.device(plane, at.a, at.b) for plane in planes[1:]]
    lines = query_ref.shape[0]
    drafts = fresh_ref.shape[0]
    heads = lines // drafts
    rows = mid_ref.shape[0]
    shard = keys_ref.shape[2]
    hidden = gate_ref.shape[1]
    waits = []

    barrier = pltpu.get_barrier_semaphore()
    partners = [sibling, at.a_side(), at.b_side()] + peers[1:]
    for partner in partners:
        pl.semaphore_signal(barrier, inc=1, device_id=partner, device_id_type=MESH)

    moves = [
        (query_hbm, query_ref),
        (keys_hbm, keys_ref.at[0]),
        (fresh_hbm, fresh_ref),
        (parents_hbm, parents_ref),
        (out_weight_hbm, out_weight_ref),
        (res_hbm, res_ref),
        (gain_hbm, gain_ref),
        (ids_hbm, ids_ref),
        (router_hbm, router_ref),
        (gate_hbm, gate_ref.at[0]),
        (up_hbm, up_ref.at[0]),
        (down_hbm, down_ref.at[0]),
    ]
    loads = [pltpu.make_async_copy(src, dst, local_sem.at[i]) for i, (src, dst) in enumerate(moves)]
    (
        query_load,
        keys_load,
        fresh_load,
        parents_load,
        out_weight_load,
        res_load,
        gain_load,
        ids_load,
        router_load,
        gate_load,
        up_load,
        down_load,
    ) = loads
    value_loads = [
        pltpu.make_async_copy(value_hbm.at[head], value_ref.at[:, pl.ds(head * 128, 128)], value_sem.at[head])
        for head in range(heads)
    ]
    for load in loads[:4] + value_loads + loads[4:]:
        load.start()

    def put(src, dst, send_sem, recv_sem, target):
        copy = send(src, dst, send_sem, recv_sem, target)
        copy.start()
        waits.append(copy)

    def await_box(box, send_sem, recv_sem):
        send(box, box, send_sem, recv_sem, sibling).wait_recv()

    swaps = [
        (keys_hbm, keys_ref.at[1]),
        (gate_hbm, gate_ref.at[1]),
        (up_hbm, up_ref.at[1]),
        (down_hbm, down_ref.at[1]),
    ]

    def swap(i):
        put(swaps[i][0], swaps[i][1], swap_send.at[i], swap_recv.at[i], sibling)

    def swapped(i):
        await_box(swaps[i][1], swap_send.at[i], swap_recv.at[i])

    request = placement_ref[req]
    length = lengths_ref[request]

    parents_load.wait()
    parent_row = parents_ref[pl.ds(request, 1), :]
    upper = lax.broadcasted_iota(jnp.int32, (drafts, drafts), 0)
    lower = lax.broadcasted_iota(jnp.int32, (drafts, drafts), 1)
    reach = (parent_row == upper).astype(jnp.float32) + (upper == lower).astype(jnp.float32)
    for _ in range(drafts.bit_length()):
        half = reach.astype(jnp.bfloat16)
        reach = jnp.minimum(jnp.dot(half, half, preferred_element_type=jnp.float32), 1.0)
    line = lax.broadcasted_iota(jnp.int32, (lines, drafts), 0)
    first = lax.broadcasted_iota(jnp.int32, (lines, drafts), 1) * heads
    owner = ((line >= first) & (line < first + heads)).astype(jnp.float32).astype(jnp.bfloat16)
    seen = dot_nt(owner, reach.astype(jnp.bfloat16))

    pl.semaphore_wait(barrier, len(partners))
    for i in range(4):
        swap(i)

    query_load.wait()
    fresh_load.wait()
    query, fresh = query_ref[...], fresh_ref[...]
    own = jnp.where(seen > 0.5, dot_nt(query, fresh) * score_scale, far_below)
    place = lax.broadcasted_iota(jnp.int32, (lines, shard), 1)

    def scores(i, start):
        stored = jnp.dot(query, keys_ref[i], preferred_element_type=jnp.float32) * score_scale
        return jnp.where(place + start < length, stored, far_below)

    keys_load.wait()
    near = scores(0, blk * shard)
    swapped(0)
    apart = scores(1, (1 - blk) * shard)
    top = jnp.maximum(
        jnp.maximum(jnp.max(near, axis=1, keepdims=True), jnp.max(apart, axis=1, keepdims=True)),
        jnp.max(own, axis=1, keepdims=True),
    )
    near, apart, own = jnp.exp(near - top), jnp.exp(apart - top), jnp.exp(own - top)
    total = (
        jnp.sum(near, axis=1, keepdims=True)
        + jnp.sum(apart, axis=1, keepdims=True)
        + jnp.sum(own, axis=1, keepdims=True)
    )
    acc = (
        dot_nt(near.astype(jnp.bfloat16), keys_ref[0, :LATENT])
        + dot_nt(apart.astype(jnp.bfloat16), keys_ref[1, :LATENT])
        + jnp.dot(own.astype(jnp.bfloat16), fresh[:, :LATENT], preferred_element_type=jnp.float32)
    )
    context = (acc * (1.0 / total)).astype(jnp.bfloat16)
    for load in value_loads:
        load.wait()
    every = jnp.dot(context, value_ref[...], preferred_element_type=jnp.float32)
    head_of = lax.broadcasted_iota(jnp.int32, every.shape, 0) % heads
    column_head = lax.broadcasted_iota(jnp.int32, every.shape, 1) // 128
    every = jnp.where(head_of == column_head, every, 0.0).astype(jnp.bfloat16)
    row = lax.broadcasted_iota(jnp.int32, (drafts, lines), 0) * heads
    column = lax.broadcasted_iota(jnp.int32, (drafts, lines), 1)
    gather = ((column >= row) & (column < row + heads)).astype(jnp.float32).astype(jnp.bfloat16)
    head_out = jnp.dot(gather, every, preferred_element_type=jnp.float32).astype(jnp.bfloat16)
    out_weight_load.wait()
    attn = jnp.dot(head_out, out_weight_ref[...], preferred_element_type=jnp.float32)
    attn_ref[0] = attn[:rows]
    attn_ref[1] = attn[rows:]
    outbox[...] = attn_ref[1 - blk].astype(jnp.bfloat16)
    put(outbox, inbox, swap_send.at[4], swap_recv.at[4], sibling)
    res_load.wait()
    gain_load.wait()
    mid = res_ref[blk].astype(jnp.float32) + attn_ref[blk]
    await_box(inbox, swap_send.at[4], swap_recv.at[4])
    mid = mid + inbox[...].astype(jnp.float32)
    mid_ref[...] = mid
    scale = lax.rsqrt(jnp.mean(mid * mid, axis=1, keepdims=True) + norm_eps)
    rows_ref[z, home] = (mid * scale * gain_ref[...].astype(jnp.float32).reshape(1, -1)).astype(jnp.bfloat16)

    def forward(plane, group, send_sem, target):
        piece = rows_ref.at[plane, group]
        put(piece, piece, send_sem, land.at[plane, group], target)

    def landed(plane, group):
        await_box(rows_ref.at[plane, group], gz_send.at[0], land.at[plane, group])

    def spread_home(k):
        if k > 0:
            landed(planes[k], home)
        forward(planes[k], home, gb_send.at[0, k], at.b_side())
        forward(planes[k], home, ga_send.at[k], at.a_side())

    def spread_over(k):
        landed(planes[k], over)
        forward(planes[k], over, gb_send.at[1, k], at.b_side())

    forward(z, home, gz_send.at[1], peers[1])
    spread_home(0)
    forward(z, home, gz_send.at[2], peers[2])
    forward(z, home, gz_send.at[3], peers[3])

    pick_draft = lax.broadcasted_iota(jnp.int32, (drafts, shard), 0)
    pick_place = lax.broadcasted_iota(jnp.int32, (drafts, shard), 1)
    picked = jnp.zeros((drafts, shard), jnp.float32)
    for i in range(accepted_ref.shape[0]):
        target = length + i - blk * shard
        picked = jnp.where((pick_draft == accepted_ref[i, request]) & (pick_place == target), 1.0, picked)
    hit = jnp.max(picked, axis=0, keepdims=True)
    written = lax.dot_general(
        fresh, picked.astype(jnp.bfloat16), (((0,), (0,)), ((), ())), preferred_element_type=jnp.float32
    )
    updated_ref[...] = jnp.where(hit > 0.5, written, keys_ref[0].astype(jnp.float32)).astype(jnp.bfloat16)

    ids_load.wait()
    experts = router_ref.shape[0]
    expert_at = lax.broadcasted_iota(jnp.int32, (experts, drafts), 0)
    seat = (
        lax.broadcasted_iota(jnp.int32, (rows, drafts), 1)
        == lax.broadcasted_iota(jnp.int32, (rows, drafts), 0) + blk * rows
    ).astype(jnp.float32).astype(jnp.bfloat16)
    for k in range(DEPTH):
        for group in range(4):
            asked = placement_ref[planes[k] * 4 + group]
            names = jnp.zeros((experts, drafts), jnp.float32)
            for j in range(TOP):
                names = jnp.where(ids_ref[j, pl.ds(asked, 1), :] == expert_at, 1.0, names)
            named_ref[k, pl.ds(group * rows, rows), :] = dot_nt(seat, names.astype(jnp.bfloat16))

    def turn(i):
        for source, dest in ((gate_ref, gate_t), (up_ref, up_t)):
            for c in range(source.shape[2] // 256):
                dest[i, pl.ds(c * 256, 256), :] = source[i, :, pl.ds(c * 256, 256)].T

    def load_rows(k):
        for group in range(4):
            flat[pl.ds(group * rows, rows), :] = rows_ref[planes[k], group].astype(jnp.float32)
        x_ref[...] = flat[...].astype(jnp.bfloat16)

    def gate_of(k):
        chosen = named_ref[k] * jax.nn.sigmoid(dot_nt(x_ref[...], router_ref[...]))
        mine = lax.broadcasted_iota(jnp.int32, chosen.shape, 1) == req
        return (
            route_scale
            * jnp.sum(jnp.where(mine, chosen, 0.0), axis=1, keepdims=True)
            / jnp.sum(chosen, axis=1, keepdims=True)
        )

    def expand(i):
        x = x_ref[...]
        act_ref[i] = (
            jax.nn.silu(jnp.dot(x, gate_t[i], preferred_element_type=jnp.float32))
            * jnp.dot(x, up_t[i], preferred_element_type=jnp.float32)
        ).astype(jnp.bfloat16)

    def contract(k, gate):
        flat[...] = (
            jnp.dot(act_ref[0], down_ref[0], preferred_element_type=jnp.float32)
            + jnp.dot(act_ref[1], down_ref[1], preferred_element_type=jnp.float32)
        ) * gate
        for group in range(4):
            part_ref[k, group] = flat[pl.ds(group * rows, rows), :].astype(jnp.bfloat16)
        put(part_ref.at[k, far], b_in.at[0, k], rb_send.at[0, k], rb_recv.at[0, k], at.b_side())
        put(part_ref.at[k, side], b_in.at[1, k], rb_send.at[1, k], rb_recv.at[1, k], at.b_side())

    def sum_over(k):
        await_box(b_in.at[0, k], rb_send.at[0, k], rb_recv.at[0, k])
        over_sum[k] = (part_ref[k, over].astype(jnp.float32) + b_in[0, k].astype(jnp.float32)).astype(jnp.bfloat16)
        put(over_sum.at[k], a_in.at[k], ra_send.at[k], ra_recv.at[k], at.a_side())

    def sum_home(k):
        await_box(b_in.at[1, k], rb_send.at[1, k], rb_recv.at[1, k])
        here = part_ref[k, home].astype(jnp.float32) + b_in[1, k].astype(jnp.float32)
        await_box(a_in.at[k], ra_send.at[k], ra_recv.at[k])
        here = here + a_in[k].astype(jnp.float32)
        if k > 0:
            home_sum[k] = here.astype(jnp.bfloat16)
            put(home_sum.at[k], z_in.at[z], rz_send.at[k], rz_recv.at[z], peers[k])
        else:
            keep_ref[...] = mid_ref[...] + here

    def settle(k):
        landed(planes[k], side)
        landed(planes[k], far)
        load_rows(k)
        return gate_of(k)

    gate_load.wait()
    up_load.wait()
    turn(0)
    router_load.wait()
    spread_over(0)
    spread_home(1)
    spread_home(2)
    swapped(1)
    swapped(2)
    turn(1)
    gate = settle(0)
    expand(0)
    spread_over(1)
    expand(1)
    spread_home(3)
    down_load.wait()
    swapped(3)
    contract(0, gate)
    spread_over(2)
    gate = settle(1)
    expand(0)
    spread_over(3)
    expand(1)
    contract(1, gate)
    sum_over(0)
    gate = settle(2)
    expand(0)
    expand(1)
    contract(2, gate)
    sum_home(0)
    gate = settle(3)
    expand(0)
    sum_over(1)
    expand(1)
    contract(3, gate)
    sum_over(2)
    sum_home(1)
    sum_over(3)
    sum_home(2)
    sum_home(3)
    result = keep_ref[...]
    for k in range(1, DEPTH):
        await_box(z_in.at[planes[k]], rz_send.at[k], rz_recv.at[planes[k]])
        result = result + z_in[planes[k]].astype(jnp.float32)
    out_ref[...] = result.astype(jnp.bfloat16)
    for copy in waits:
        copy.wait_send()


def whole_layer(
    residual,
    query,
    fresh,
    keys,
    lengths,
    placement,
    parents,
    accepted,
    expert_ids,
    value_weight,
    out_weight,
    gain,
    router_weight,
    gate_weight,
    up_weight,
    down_weight,
):
    n_blk, rows, width = residual.shape
    hidden = gate_weight.shape[0]
    shard = keys.shape[1]
    lines = query.shape[0]
    heads = value_weight.shape[0]
    experts = router_weight.shape[0]
    smem = pl.BlockSpec(memory_space=pltpu.SMEM)
    hbm = pl.BlockSpec(memory_space=pl.ANY)
    vmem = pl.BlockSpec(memory_space=pltpu.VMEM)
    dma = pltpu.SemaphoreType.DMA
    like = lambda a: pltpu.VMEM(a.shape, a.dtype)
    pair = lambda a: pltpu.VMEM((2,) + a.shape, a.dtype)
    box = lambda *dims: pltpu.VMEM(dims + (rows, width), jnp.bfloat16)
    f32 = lambda *dims: pltpu.VMEM(dims, jnp.float32)
    return pl.pallas_call(
        whole_kernel,
        out_shape=(pltpu.VMEM((rows, width), jnp.bfloat16), pltpu.VMEM(keys.shape, jnp.bfloat16)),
        in_specs=[smem] * 3 + [hbm] * 13,
        out_specs=(vmem, vmem),
        scratch_shapes=[
            like(parents),
            like(expert_ids),
            like(gain),
            like(router_weight),
            like(residual),
            like(query),
            like(fresh),
            pair(keys),
            pltpu.VMEM((value_weight.shape[1], heads * value_weight.shape[2]), jnp.bfloat16),
            like(out_weight),
            pair(gate_weight),
            pair(up_weight),
            pair(down_weight),
            pltpu.VMEM((2, width, hidden), jnp.bfloat16),
            pltpu.VMEM((2, width, hidden), jnp.bfloat16),
            f32(n_blk, rows, width),
            f32(rows, width),
            f32(rows, width),
            box(),
            box(),
            box(DEPTH, 4),
            f32(4 * rows, width),
            pltpu.VMEM((4 * rows, width), jnp.bfloat16),
            pltpu.VMEM((2, 4 * rows, hidden), jnp.bfloat16),
            f32(DEPTH, 4 * rows, experts),
            box(DEPTH, 4),
            box(2, DEPTH),
            box(DEPTH),
            box(DEPTH),
            box(DEPTH),
            box(DEPTH),
            dma((12,)),
            dma((heads,)),
            dma((5,)),
            dma((5,)),
            dma((DEPTH,)),
            dma((DEPTH,)),
            dma((2, DEPTH)),
            dma((DEPTH, 4)),
            dma((2, DEPTH)),
            dma((2, DEPTH)),
            dma((DEPTH,)),
            dma((DEPTH,)),
            dma((DEPTH,)),
            dma((DEPTH,)),
        ],
        compiler_params=pltpu.CompilerParams(
            collective_id=2, has_side_effects=True, vmem_limit_bytes=VMEM_LIMIT
        ),
    )(
        placement,
        lengths,
        accepted,
        parents,
        expert_ids,
        gain,
        router_weight,
        residual,
        query,
        fresh,
        keys,
        value_weight,
        out_weight,
        gate_weight,
        up_weight,
        down_weight,
    )


def on_device(
    residual,
    queries,
    new_latents,
    latent_cache,
    lengths,
    placement,
    parents,
    accepted,
    expert_ids,
    value_weight,
    out_weight,
    norm_gain,
    router_weight,
    gate_weight,
    up_weight,
    down_weight,
):
    req = lax.axis_index("req")
    block_index = lax.axis_index("blk")
    n_req = lax.axis_size("req")
    n_blk = lax.axis_size("blk")
    drafts = residual.shape[1]
    width = residual.shape[2]
    shard_len = latent_cache.shape[1]
    experts = router_weight.shape[1]
    rows_here = drafts // n_blk
    depth = n_req // 4
    if n_req == 4 * DEPTH and n_blk == 2 and n_blk * n_req * rows_here <= FUSED_ROWS:
        layer_out, updated = whole_layer(
            residual[0].reshape(n_blk, rows_here, width),
            queries[0].reshape(drafts * queries.shape[2], queries.shape[3]),
            new_latents[0],
            latent_cache[0].T,
            lengths,
            placement,
            parents,
            accepted.T,
            expert_ids.transpose(2, 0, 1),
            value_weight,
            out_weight,
            norm_gain,
            router_weight.T,
            gate_weight[0].T,
            up_weight[0].T,
            down_weight[0],
        )
        return (layer_out[None], updated.T[None])

    request = lax.dynamic_index_in_dim(placement, req, 0, keepdims=False)
    length = lax.dynamic_index_in_dim(lengths, request, 0, keepdims=False)
    parent_row = lax.dynamic_index_in_dim(parents, request, 0, keepdims=False)
    taken = lax.dynamic_index_in_dim(accepted, request, 0, keepdims=False)

    named = jnp.any(
        expert_ids[:, :, :, None] == jnp.arange(experts, dtype=jnp.int32), axis=2
    ).astype(jnp.bfloat16)
    seat = (placement[:, None] == jnp.arange(n_req, dtype=jnp.int32)[None, :]).astype(jnp.bfloat16)
    named = jnp.einsum("sr,rte->ste", seat, named, preferred_element_type=jnp.float32)
    named = named.reshape(depth, 4, n_blk, rows_here, experts)

    piece = lax.all_gather(latent_cache[0], "blk", axis=0, tiled=True)
    attn = attend_slot(
        queries[0], new_latents[0], piece, length, parent_row, value_weight, out_weight
    )
    attn = attn.reshape(n_blk, rows_here, width)
    home_rows = residual.reshape(n_blk, rows_here, width)
    gain = norm_gain.reshape(1, width)
    mid, gathered = gather_rows(attn, home_rows, gain, n_req, n_blk)
    rows = gathered.reshape(n_req * drafts, width)
    score_e = jax.nn.sigmoid(jnp.dot(rows, router_weight, preferred_element_type=jnp.float32))
    chosen = named.transpose(2, 1, 0, 3, 4).reshape(n_req * drafts, experts) * score_e
    mine = jnp.arange(experts, dtype=jnp.int32)[None, :] == req
    gate = (
        route_scale
        * jnp.sum(jnp.where(mine, chosen, 0.0), axis=1, keepdims=True)
        / jnp.sum(chosen, axis=1, keepdims=True)
    )
    act = (
        jax.nn.silu(jnp.dot(rows, gate_weight[0], preferred_element_type=jnp.float32))
        * jnp.dot(rows, up_weight[0], preferred_element_type=jnp.float32)
    ).astype(jnp.bfloat16)
    parts = jnp.dot(act, down_weight[0], preferred_element_type=jnp.float32) * gate
    parts = parts.astype(jnp.bfloat16).reshape(n_blk, 4, depth, rows_here, width)
    layer_out = scatter_rows(parts, mid, n_req, n_blk)

    stored = latent_cache[0]
    chosen_rows = new_latents[0][taken]
    targets = length + jnp.arange(taken.shape[0], dtype=jnp.int32) - block_index * shard_len
    hit = jnp.arange(shard_len, dtype=jnp.int32)[:, None] == targets[None, :]
    written = jnp.dot(
        hit.astype(jnp.bfloat16), chosen_rows, preferred_element_type=jnp.float32
    ).astype(jnp.bfloat16)
    updated = jnp.where(jnp.any(hit, axis=1)[:, None], written, stored)
    return (layer_out[None], updated[None])


def solution(mesh):
    return jax.shard_map(
        on_device,
        mesh=mesh,
        in_specs=(
            P("req", None, None),
            P("req", None, "blk", None),
            P("req", None, None),
            P("req", "blk", None),
            P(),
            P(),
            P(),
            P(),
            P(),
            P("blk", None, None),
            P("blk", None),
            P(),
            P(),
            P("req", None, "blk"),
            P("req", None, "blk"),
            P("req", "blk", None),
        ),
        out_specs=(P("req", "blk", None), P("req", "blk", None)),
        check_vma=False,
    )
```

```python
import functools

import jax
import jax.numpy as jnp
from jax import lax
from jax.experimental import pallas as pl
from jax.experimental.pallas import tpu as pltpu
from jax.sharding import PartitionSpec as P

LATENT = 512
TOP = 6
MESH = pl.DeviceIdType.MESH
VMEM_LIMIT = 56 * 1024 * 1024
FUSED_ROWS = 1024
DEPTH = 4

score_scale = 0.07216878364870322
route_scale = 2.446
norm_eps = 1e-06
far_below = -1e30


def ancestors(parent_row):
    span = parent_row.shape[0]
    links = (parent_row[:, None] == jnp.arange(span, dtype=jnp.int32)[None, :]).astype(jnp.float32)
    reach = jnp.eye(span, dtype=jnp.float32) + links
    for _ in range(span.bit_length()):
        reach = jnp.minimum(jnp.dot(reach, reach, precision=lax.Precision.HIGHEST), 1.0)
    return reach


def attend_kernel(length_ref, query_ref, fresh_ref, keys_ref, reach_ref, value_ref, out_weight_ref, attn_ref):
    drafts = fresh_ref.shape[0]
    heads = value_ref.shape[0]
    lines = drafts * heads
    query, fresh, keys = query_ref[...], fresh_ref[...], keys_ref[...]
    line = lax.broadcasted_iota(jnp.int32, (lines, drafts), 0)
    first = lax.broadcasted_iota(jnp.int32, (lines, drafts), 1) * heads
    owner = ((line >= first) & (line < first + heads)).astype(jnp.float32)
    reach = jnp.dot(owner, reach_ref[...], preferred_element_type=jnp.float32)
    stored = jnp.dot(query, keys, preferred_element_type=jnp.float32) * score_scale
    where = lax.broadcasted_iota(jnp.int32, stored.shape, 1)
    stored = jnp.where(where < length_ref[0], stored, far_below)
    own = jnp.where(reach > 0.5, dot_nt(query, fresh) * score_scale, far_below)
    top = jnp.maximum(
        jnp.max(stored, axis=1, keepdims=True), jnp.max(own, axis=1, keepdims=True)
    )
    stored = jnp.exp(stored - top)
    own = jnp.exp(own - top)
    total = jnp.sum(stored, axis=1, keepdims=True) + jnp.sum(own, axis=1, keepdims=True)
    acc = dot_nt(stored.astype(jnp.bfloat16), keys[:LATENT]) + jnp.dot(
        own.astype(jnp.bfloat16), fresh[:, :LATENT], preferred_element_type=jnp.float32
    )
    context = (acc / total).astype(jnp.bfloat16)
    row = lax.broadcasted_iota(jnp.int32, (drafts, lines), 0) * heads
    column = lax.broadcasted_iota(jnp.int32, (drafts, lines), 1)
    outs = []
    for head in range(heads):
        select = (column == row + head).astype(jnp.bfloat16)
        one = jnp.dot(select, context, preferred_element_type=jnp.float32).astype(jnp.bfloat16)
        outs.append(
            jnp.dot(one, value_ref[head], preferred_element_type=jnp.float32).astype(jnp.bfloat16)
        )
    attn_ref[...] = jnp.dot(
        jnp.concatenate(outs, axis=1), out_weight_ref[...], preferred_element_type=jnp.float32
    )


def attend_slot(query, fresh, piece, length, parent_row, value_weight, out_weight):
    drafts, heads, width = query.shape
    vmem = pl.BlockSpec(memory_space=pltpu.VMEM)
    return pl.pallas_call(
        attend_kernel,
        out_shape=jax.ShapeDtypeStruct((drafts, out_weight.shape[1]), jnp.float32),
        in_specs=[pl.BlockSpec(memory_space=pltpu.SMEM)] + [vmem] * 6,
        out_specs=vmem,
        compiler_params=pltpu.CompilerParams(vmem_limit_bytes=VMEM_LIMIT),
    )(
        length.reshape(1),
        query.reshape(drafts * heads, width),
        fresh,
        piece.T,
        ancestors(parent_row),
        value_weight,
        out_weight,
    )


class Place:
    def __init__(self, n_req, n_blk):
        self.depth = n_req // 4
        self.n_blk = n_blk
        req = lax.axis_index("req")
        self.blk = lax.axis_index("blk")
        self.z = req // 4
        self.y = (req // 2) % 2
        self.x = req % 2
        self.swap = self.blk % 2
        self.a = self.y * (1 - self.swap) + self.x * self.swap
        self.b = self.x * (1 - self.swap) + self.y * self.swap
        self.home = self.group(self.a, self.b)

    def group(self, a, b):
        return a * (2 - self.swap) + b * (1 + self.swap)

    def device(self, z, a, b):
        return (z * 4 + self.group(a, b), self.blk)

    def far(self, step):
        return (self.z + step) % self.depth

    def a_side(self):
        return self.device(self.z, 1 - self.a, self.b)

    def b_side(self):
        return self.device(self.z, self.a, 1 - self.b)

    def z_side(self, step):
        return self.device(self.far(step), self.a, self.b)

    def sibling_blk(self, step):
        return (self.blk + step) % self.n_blk

    def sibling(self, step):
        return (self.z * 4 + self.home, self.sibling_blk(step))

    def greet(self):
        barrier = pltpu.get_barrier_semaphore()
        others = [self.a_side(), self.b_side()]
        others += [self.z_side(step) for step in range(1, self.depth)]
        others += [self.sibling(step) for step in range(1, self.n_blk)]
        for other in others:
            pl.semaphore_signal(barrier, inc=1, device_id=other, device_id_type=MESH)
        pl.semaphore_wait(barrier, len(others))


def send(src, dst, send_sem, recv_sem, target):
    return pltpu.make_async_remote_copy(
        src_ref=src,
        dst_ref=dst,
        send_sem=send_sem,
        recv_sem=recv_sem,
        device_id=target,
        device_id_type=MESH,
    )


def gather_kernel(
    n_req,
    n_blk,
    attn_ref,
    res_ref,
    gain_ref,
    mid_ref,
    rows_ref,
    outbox,
    inbox,
    box_send,
    box_recv,
    z_send,
    a_send,
    b_send,
    land,
    sib_send,
    sib_recv,
):
    at = Place(n_req, n_blk)
    depth, blk, home = at.depth, at.blk, at.home
    outbox[...] = attn_ref[...].astype(jnp.bfloat16)
    at.greet()
    swaps = []
    for step in range(1, n_blk):
        copy = send(
            outbox.at[at.sibling_blk(step)],
            inbox.at[step - 1],
            box_send.at[step - 1],
            box_recv.at[step - 1],
            at.sibling(step),
        )
        copy.start()
        swaps.append(copy)
    mid = res_ref[blk].astype(jnp.float32) + attn_ref[blk]
    for step in range(1, n_blk):
        swaps[step - 1].wait_recv()
        mid = mid + inbox[step - 1].astype(jnp.float32)
    mid_ref[...] = mid
    scale = lax.rsqrt(jnp.mean(mid * mid, axis=1, keepdims=True) + norm_eps)
    rows_ref[blk, home, at.z] = (mid * scale * gain_ref[...].astype(jnp.float32)).astype(jnp.bfloat16)

    waits = []

    def forward(group, z, send_sem, target):
        piece = rows_ref.at[blk, group, z]
        copy = send(piece, piece, send_sem, land.at[group, z], target)
        copy.start()
        waits.append(copy)

    def landed(group, z):
        piece = rows_ref.at[blk, group, z]
        send(piece, piece, z_send.at[0], land.at[group, z], at.a_side()).wait_recv()

    def share(group):
        for step in range(1, n_blk):
            block = rows_ref.at[blk, group]
            copy = send(
                block, block, sib_send.at[step - 1, group], sib_recv.at[step - 1, group], at.sibling(step)
            )
            copy.start()
            waits.append(copy)

    for step in range(1, depth):
        forward(home, at.z, z_send.at[step - 1], at.z_side(step))
    forward(home, at.z, b_send.at[0, 0], at.b_side())
    forward(home, at.z, a_send.at[0], at.a_side())
    for step in range(1, depth):
        z = at.far(step)
        landed(home, z)
        forward(home, z, b_send.at[0, step], at.b_side())
        forward(home, z, a_send.at[step], at.a_side())
    share(home)
    over = at.group(1 - at.a, at.b)
    for step in range(depth):
        z = at.far(step)
        landed(over, z)
        forward(over, z, b_send.at[1, step], at.b_side())
    share(over)
    for a in (at.a, 1 - at.a):
        group = at.group(a, 1 - at.b)
        for step in range(depth):
            landed(group, at.far(step))
        share(group)
    for step in range(1, n_blk):
        source = (blk + n_blk - step) % n_blk
        for group in range(4):
            block = rows_ref.at[source, group]
            send(
                block, block, sib_send.at[step - 1, group], sib_recv.at[step - 1, group], at.sibling(step)
            ).wait_recv()
    for copy in waits:
        copy.wait_send()
    for copy in swaps:
        copy.wait_send()


def gather_rows(attn, residual, gain, n_req, n_blk):
    _, rows, width = attn.shape
    depth = n_req // 4
    vmem = pl.BlockSpec(memory_space=pltpu.VMEM)
    dma = pltpu.SemaphoreType.DMA
    sibs = max(n_blk - 1, 1)
    return pl.pallas_call(
        functools.partial(gather_kernel, n_req, n_blk),
        out_shape=(
            jax.ShapeDtypeStruct((rows, width), jnp.float32),
            jax.ShapeDtypeStruct((n_blk, 4, depth, rows, width), jnp.bfloat16),
        ),
        in_specs=[vmem] * 3,
        out_specs=(vmem, vmem),
        scratch_shapes=[
            pltpu.VMEM((n_blk, rows, width), jnp.bfloat16),
            pltpu.VMEM((sibs, rows, width), jnp.bfloat16),
            dma((sibs,)),
            dma((sibs,)),
            dma((depth,)),
            dma((depth,)),
            dma((2, depth)),
            dma((4, depth)),
            dma((sibs, 4)),
            dma((sibs, 4)),
        ],
        compiler_params=pltpu.CompilerParams(
            collective_id=0, has_side_effects=True, vmem_limit_bytes=VMEM_LIMIT
        ),
    )(attn, residual, gain)


def scatter_kernel(
    n_req,
    n_blk,
    part_ref,
    mid_ref,
    out_ref,
    sib_in,
    b_in,
    a_in,
    z_in,
    sums,
    sib_send,
    sib_recv,
    b_send,
    b_recv,
    a_send,
    a_recv,
    z_send,
    z_recv,
):
    at = Place(n_req, n_blk)
    depth, blk = at.depth, at.blk
    at.greet()
    waits = []
    order = [
        at.group(1 - at.a, 1 - at.b),
        at.group(at.a, 1 - at.b),
        at.group(1 - at.a, at.b),
        at.home,
    ]

    def put(src, dst, send_sem, recv_sem, target):
        copy = send(src, dst, send_sem, recv_sem, target)
        copy.start()
        waits.append(copy)

    for k in range(4):
        for step in range(1, n_blk):
            other_swap = at.sibling_blk(step) % 2
            a = at.y * (1 - other_swap) + at.x * other_swap
            b = at.x * (1 - other_swap) + at.y * other_swap
            ta = a if k in (1, 3) else 1 - a
            tb = b if k in (2, 3) else 1 - b
            group = ta * (2 - other_swap) + tb * (1 + other_swap)
            put(
                part_ref.at[at.sibling_blk(step), group],
                sib_in.at[step - 1, k],
                sib_send.at[step - 1, k],
                sib_recv.at[step - 1, k],
                at.sibling(step),
            )

    def wait_sib(k):
        for step in range(1, n_blk):
            box = sib_in.at[step - 1, k]
            send(box, box, sib_send.at[step - 1, k], sib_recv.at[step - 1, k], at.sibling(step)).wait_recv()

    def own(k, z):
        total = part_ref[blk, order[k], z].astype(jnp.float32)
        for step in range(1, n_blk):
            total = total + sib_in[step - 1, k, z].astype(jnp.float32)
        return total

    def await_box(box, send_sem, recv_sem):
        send(box, box, send_sem, recv_sem, at.a_side()).wait_recv()

    steps = list(range(1, depth)) + [0]
    for k in (0, 1):
        wait_sib(k)
        for step in steps:
            z = at.far(step)
            sums[k, step] = own(k, z).astype(jnp.bfloat16)
            put(sums.at[k, step], b_in.at[k, step], b_send.at[k, step], b_recv.at[k, step], at.b_side())
    wait_sib(2)
    for step in steps:
        z = at.far(step)
        total = own(2, z)
        await_box(b_in.at[0, step], b_send.at[0, step], b_recv.at[0, step])
        sums[2, step] = (total + b_in[0, step].astype(jnp.float32)).astype(jnp.bfloat16)
        put(sums.at[2, step], a_in.at[step], a_send.at[step], a_recv.at[step], at.a_side())
    wait_sib(3)
    keep = None
    for step in steps:
        z = at.far(step)
        total = own(3, z)
        await_box(b_in.at[1, step], b_send.at[1, step], b_recv.at[1, step])
        total = total + b_in[1, step].astype(jnp.float32)
        await_box(a_in.at[step], a_send.at[step], a_recv.at[step])
        total = total + a_in[step].astype(jnp.float32)
        if step > 0:
            sums[3, step] = total.astype(jnp.bfloat16)
            put(sums.at[3, step], z_in.at[step - 1], z_send.at[step - 1], z_recv.at[step - 1], at.z_side(step))
        else:
            keep = total
    total = mid_ref[...] + keep
    for step in range(1, depth):
        await_box(z_in.at[step - 1], z_send.at[step - 1], z_recv.at[step - 1])
        total = total + z_in[step - 1].astype(jnp.float32)
    out_ref[...] = total.astype(jnp.bfloat16)
    for copy in waits:
        copy.wait_send()


def scatter_rows(parts, mid, n_req, n_blk):
    _, _, depth, rows, width = parts.shape
    vmem = pl.BlockSpec(memory_space=pltpu.VMEM)
    dma = pltpu.SemaphoreType.DMA
    sibs = max(n_blk - 1, 1)
    far = max(depth - 1, 1)
    box = lambda *dims: pltpu.VMEM(dims + (rows, width), jnp.bfloat16)
    return pl.pallas_call(
        functools.partial(scatter_kernel, n_req, n_blk),
        out_shape=jax.ShapeDtypeStruct((rows, width), jnp.bfloat16),
        in_specs=[vmem] * 2,
        out_specs=vmem,
        scratch_shapes=[
            box(sibs, 4, depth),
            box(2, depth),
            box(depth),
            box(far),
            box(4, depth),
            dma((sibs, 4)),
            dma((sibs, 4)),
            dma((2, depth)),
            dma((2, depth)),
            dma((depth,)),
            dma((depth,)),
            dma((far,)),
            dma((far,)),
        ],
        compiler_params=pltpu.CompilerParams(
            collective_id=1, has_side_effects=True, vmem_limit_bytes=VMEM_LIMIT
        ),
    )(parts, mid)


def dot_nt(left, right):
    return lax.dot_general(left, right, (((1,), (1,)), ((), ())), preferred_element_type=jnp.float32)


def whole_kernel(
    placement_ref,
    lengths_ref,
    accepted_ref,
    parents_hbm,
    ids_hbm,
    gain_hbm,
    router_hbm,
    res_hbm,
    query_hbm,
    fresh_hbm,
    keys_hbm,
    value_hbm,
    out_weight_hbm,
    gate_hbm,
    up_hbm,
    down_hbm,
    out_ref,
    updated_ref,
    parents_ref,
    ids_ref,
    gain_ref,
    router_ref,
    res_ref,
    query_ref,
    fresh_ref,
    keys_ref,
    value_ref,
    out_weight_ref,
    gate_ref,
    up_ref,
    down_ref,
    gate_t,
    up_t,
    attn_ref,
    mid_ref,
    keep_ref,
    outbox,
    inbox,
    rows_ref,
    flat,
    x_ref,
    act_ref,
    named_ref,
    part_ref,
    f_in,
    a_in,
    b_in,
    q_in,
    z_in,
    plane_sum,
    home_sum,
    local_sem,
    value_sem,
    swap_send,
    swap_recv,
    gz_send,
    gf_send,
    ga_send,
    gb_send,
    gq_send,
    land,
    rf_send,
    rf_recv,
    ra_send,
    ra_recv,
    rb_send,
    rb_recv,
    rq_send,
    rq_recv,
    rz_send,
    rz_recv,
):
    at = Place(4 * DEPTH, 2)
    blk, z, home = at.blk, at.z, at.home
    over = at.group(1 - at.a, at.b)
    side = at.group(at.a, 1 - at.b)
    far = at.group(1 - at.a, 1 - at.b)
    req = lax.axis_index("req")
    planes = [z, z + 1 - 2 * (z % 2), 2 - z // 2, 3 - 3 * (z // 2)]
    sibling = at.sibling(1)
    peers = [None] + [at.device(plane, at.a, at.b) for plane in planes[1:]]
    lines = query_ref.shape[0]
    drafts = fresh_ref.shape[0]
    heads = lines // drafts
    rows = mid_ref.shape[0]
    shard = keys_ref.shape[2]
    hidden = gate_ref.shape[1]
    waits = []

    barrier = pltpu.get_barrier_semaphore()
    diagonal = at.device(z, 1 - at.a, 1 - at.b)
    partners = [sibling, at.a_side(), at.b_side(), diagonal] + peers[1:]
    for partner in partners:
        pl.semaphore_signal(barrier, inc=1, device_id=partner, device_id_type=MESH)

    moves = [
        (query_hbm, query_ref),
        (keys_hbm, keys_ref.at[0]),
        (fresh_hbm, fresh_ref),
        (parents_hbm, parents_ref),
        (out_weight_hbm, out_weight_ref),
        (res_hbm, res_ref),
        (gain_hbm, gain_ref),
        (ids_hbm, ids_ref),
        (router_hbm, router_ref),
        (gate_hbm, gate_ref.at[0]),
        (up_hbm, up_ref.at[0]),
        (down_hbm, down_ref.at[0]),
    ]
    loads = [pltpu.make_async_copy(src, dst, local_sem.at[i]) for i, (src, dst) in enumerate(moves)]
    (
        query_load,
        keys_load,
        fresh_load,
        parents_load,
        out_weight_load,
        res_load,
        gain_load,
        ids_load,
        router_load,
        gate_load,
        up_load,
        down_load,
    ) = loads
    value_loads = [
        pltpu.make_async_copy(value_hbm.at[head], value_ref.at[:, pl.ds(head * 128, 128)], value_sem.at[head])
        for head in range(heads)
    ]
    for load in loads[:4] + value_loads + loads[4:]:
        load.start()

    def put(src, dst, send_sem, recv_sem, target):
        copy = send(src, dst, send_sem, recv_sem, target)
        copy.start()
        waits.append(copy)

    def await_box(box, send_sem, recv_sem):
        send(box, box, send_sem, recv_sem, sibling).wait_recv()

    swaps = [
        (keys_hbm, keys_ref.at[1]),
        (gate_hbm, gate_ref.at[1]),
        (up_hbm, up_ref.at[1]),
        (down_hbm, down_ref.at[1]),
    ]

    def swap(i):
        put(swaps[i][0], swaps[i][1], swap_send.at[i], swap_recv.at[i], sibling)

    def swapped(i):
        await_box(swaps[i][1], swap_send.at[i], swap_recv.at[i])

    request = placement_ref[req]
    length = lengths_ref[request]

    parents_load.wait()
    parent_row = parents_ref[pl.ds(request, 1), :]
    upper = lax.broadcasted_iota(jnp.int32, (drafts, drafts), 0)
    lower = lax.broadcasted_iota(jnp.int32, (drafts, drafts), 1)
    reach = (parent_row == upper).astype(jnp.float32) + (upper == lower).astype(jnp.float32)
    for _ in range(drafts.bit_length()):
        half = reach.astype(jnp.bfloat16)
        reach = jnp.minimum(jnp.dot(half, half, preferred_element_type=jnp.float32), 1.0)
    line = lax.broadcasted_iota(jnp.int32, (lines, drafts), 0)
    first = lax.broadcasted_iota(jnp.int32, (lines, drafts), 1) * heads
    owner = ((line >= first) & (line < first + heads)).astype(jnp.float32).astype(jnp.bfloat16)
    seen = dot_nt(owner, reach.astype(jnp.bfloat16))

    pl.semaphore_wait(barrier, len(partners))
    for i in range(4):
        swap(i)

    query_load.wait()
    fresh_load.wait()
    query, fresh = query_ref[...], fresh_ref[...]
    own = jnp.where(seen > 0.5, dot_nt(query, fresh) * score_scale, far_below)
    place = lax.broadcasted_iota(jnp.int32, (lines, shard), 1)

    def scores(i, start):
        stored = jnp.dot(query, keys_ref[i], preferred_element_type=jnp.float32) * score_scale
        return jnp.where(place + start < length, stored, far_below)

    keys_load.wait()
    near = scores(0, blk * shard)
    swapped(0)
    apart = scores(1, (1 - blk) * shard)
    top = jnp.maximum(
        jnp.maximum(jnp.max(near, axis=1, keepdims=True), jnp.max(apart, axis=1, keepdims=True)),
        jnp.max(own, axis=1, keepdims=True),
    )
    near, apart, own = jnp.exp(near - top), jnp.exp(apart - top), jnp.exp(own - top)
    total = (
        jnp.sum(near, axis=1, keepdims=True)
        + jnp.sum(apart, axis=1, keepdims=True)
        + jnp.sum(own, axis=1, keepdims=True)
    )
    acc = (
        dot_nt(near.astype(jnp.bfloat16), keys_ref[0, :LATENT])
        + dot_nt(apart.astype(jnp.bfloat16), keys_ref[1, :LATENT])
        + jnp.dot(own.astype(jnp.bfloat16), fresh[:, :LATENT], preferred_element_type=jnp.float32)
    )
    context = (acc * (1.0 / total)).astype(jnp.bfloat16)
    for load in value_loads:
        load.wait()
    every = jnp.dot(context, value_ref[...], preferred_element_type=jnp.float32)
    head_of = lax.broadcasted_iota(jnp.int32, every.shape, 0) % heads
    column_head = lax.broadcasted_iota(jnp.int32, every.shape, 1) // 128
    every = jnp.where(head_of == column_head, every, 0.0).astype(jnp.bfloat16)
    row = lax.broadcasted_iota(jnp.int32, (drafts, lines), 0) * heads
    column = lax.broadcasted_iota(jnp.int32, (drafts, lines), 1)
    gather = ((column >= row) & (column < row + heads)).astype(jnp.float32).astype(jnp.bfloat16)
    head_out = jnp.dot(gather, every, preferred_element_type=jnp.float32).astype(jnp.bfloat16)
    out_weight_load.wait()
    attn = jnp.dot(head_out, out_weight_ref[...], preferred_element_type=jnp.float32)
    attn_ref[0] = attn[:rows]
    attn_ref[1] = attn[rows:]
    outbox[...] = attn_ref[1 - blk].astype(jnp.bfloat16)
    put(outbox, inbox, swap_send.at[4], swap_recv.at[4], sibling)
    res_load.wait()
    gain_load.wait()
    mid = res_ref[blk].astype(jnp.float32) + attn_ref[blk]
    await_box(inbox, swap_send.at[4], swap_recv.at[4])
    mid = mid + inbox[...].astype(jnp.float32)
    mid_ref[...] = mid
    scale = lax.rsqrt(jnp.mean(mid * mid, axis=1, keepdims=True) + norm_eps)
    rows_ref[z, home] = (mid * scale * gain_ref[...].astype(jnp.float32).reshape(1, -1)).astype(jnp.bfloat16)

    def forward(plane, group, send_sem, target):
        piece = rows_ref.at[plane, group]
        put(piece, piece, send_sem, land.at[plane, group], target)

    def landed(plane, group):
        await_box(rows_ref.at[plane, group], gz_send.at[0], land.at[plane, group])

    def spread(k):
        if k > 0:
            landed(planes[k], home)
        forward(planes[k], home, gf_send.at[k], diagonal)
        forward(planes[k], home, ga_send.at[k], at.a_side())
        forward(planes[k], home, gb_send.at[k], at.b_side())

    def spread_plane():
        for i, group in enumerate((over, side, far)):
            landed(z, group)
            forward(z, group, gq_send.at[i], peers[1])

    forward(z, home, gz_send.at[3], peers[3])
    forward(z, home, gz_send.at[2], peers[2])
    spread(0)
    forward(z, home, gz_send.at[1], peers[1])

    pick_draft = lax.broadcasted_iota(jnp.int32, (drafts, shard), 0)
    pick_place = lax.broadcasted_iota(jnp.int32, (drafts, shard), 1)
    picked = jnp.zeros((drafts, shard), jnp.float32)
    for i in range(accepted_ref.shape[0]):
        target = length + i - blk * shard
        picked = jnp.where((pick_draft == accepted_ref[i, request]) & (pick_place == target), 1.0, picked)
    hit = jnp.max(picked, axis=0, keepdims=True)
    written = lax.dot_general(
        fresh, picked.astype(jnp.bfloat16), (((0,), (0,)), ((), ())), preferred_element_type=jnp.float32
    )
    updated_ref[...] = jnp.where(hit > 0.5, written, keys_ref[0].astype(jnp.float32)).astype(jnp.bfloat16)

    ids_load.wait()
    experts = router_ref.shape[0]
    expert_at = lax.broadcasted_iota(jnp.int32, (experts, drafts), 0)
    seat = (
        lax.broadcasted_iota(jnp.int32, (rows, drafts), 1)
        == lax.broadcasted_iota(jnp.int32, (rows, drafts), 0) + blk * rows
    ).astype(jnp.float32).astype(jnp.bfloat16)
    for k in range(DEPTH):
        for group in range(4):
            asked = placement_ref[planes[k] * 4 + group]
            names = jnp.zeros((experts, drafts), jnp.float32)
            for j in range(TOP):
                names = jnp.where(ids_ref[j, pl.ds(asked, 1), :] == expert_at, 1.0, names)
            named_ref[k, pl.ds(group * rows, rows), :] = dot_nt(seat, names.astype(jnp.bfloat16))

    def turn(i):
        for source, dest in ((gate_ref, gate_t), (up_ref, up_t)):
            for c in range(source.shape[2] // 256):
                dest[i, pl.ds(c * 256, 256), :] = source[i, :, pl.ds(c * 256, 256)].T

    def load_rows(k):
        for group in range(4):
            flat[pl.ds(group * rows, rows), :] = rows_ref[planes[k], group].astype(jnp.float32)
        x_ref[...] = flat[...].astype(jnp.bfloat16)

    def gate_of(k):
        chosen = named_ref[k] * jax.nn.sigmoid(dot_nt(x_ref[...], router_ref[...]))
        mine = lax.broadcasted_iota(jnp.int32, chosen.shape, 1) == req
        return (
            route_scale
            * jnp.sum(jnp.where(mine, chosen, 0.0), axis=1, keepdims=True)
            / jnp.sum(chosen, axis=1, keepdims=True)
        )

    def expand(i):
        x = x_ref[...]
        act_ref[i] = (
            jax.nn.silu(jnp.dot(x, gate_t[i], preferred_element_type=jnp.float32))
            * jnp.dot(x, up_t[i], preferred_element_type=jnp.float32)
        ).astype(jnp.bfloat16)

    def contract(k, gate):
        flat[...] = (
            jnp.dot(act_ref[0], down_ref[0], preferred_element_type=jnp.float32)
            + jnp.dot(act_ref[1], down_ref[1], preferred_element_type=jnp.float32)
        ) * gate
        for group in range(4):
            part_ref[k, group] = flat[pl.ds(group * rows, rows), :].astype(jnp.bfloat16)

    def return_plane():
        for i, group in enumerate((far, over, side, home)):
            put(part_ref.at[1, group], q_in.at[i], rq_send.at[i], rq_recv.at[i], peers[1])

    def return_far(k):
        put(part_ref.at[k, far], f_in.at[k], rf_send.at[k], rf_recv.at[k], diagonal)
        put(part_ref.at[k, over], a_in.at[k], ra_send.at[k], ra_recv.at[k], at.a_side())
        put(part_ref.at[k, side], b_in.at[k], rb_send.at[k], rb_recv.at[k], at.b_side())

    def plane_total(i, group):
        await_box(q_in.at[i], rq_send.at[i], rq_recv.at[i])
        return part_ref[0, group].astype(jnp.float32) + q_in[i].astype(jnp.float32)

    def return_own():
        plane_sum[0] = plane_total(0, far).astype(jnp.bfloat16)
        put(plane_sum.at[0], f_in.at[0], rf_send.at[0], rf_recv.at[0], diagonal)
        plane_sum[1] = plane_total(1, over).astype(jnp.bfloat16)
        put(plane_sum.at[1], a_in.at[0], ra_send.at[0], ra_recv.at[0], at.a_side())
        plane_sum[2] = plane_total(2, side).astype(jnp.bfloat16)
        put(plane_sum.at[2], b_in.at[0], rb_send.at[0], rb_recv.at[0], at.b_side())
        keep_ref[...] = mid_ref[...] + plane_total(3, home)

    def sum_home(k, here):
        for box, send_sem, recv_sem in ((f_in, rf_send, rf_recv), (a_in, ra_send, ra_recv), (b_in, rb_send, rb_recv)):
            await_box(box.at[k], send_sem.at[k], recv_sem.at[k])
            here = here + box[k].astype(jnp.float32)
        return here

    def return_home(k):
        home_sum[k] = sum_home(k, part_ref[k, home].astype(jnp.float32)).astype(jnp.bfloat16)
        put(home_sum.at[k], z_in.at[z], rz_send.at[k], rz_recv.at[z], peers[k])

    def settle(k):
        if k == 1:
            landed(planes[k], home)
        if k > 0:
            for group in (over, side, far):
                landed(planes[k], group)
        load_rows(k)
        return gate_of(k)

    gate_load.wait()
    up_load.wait()
    turn(0)
    router_load.wait()
    spread(2)
    spread_plane()
    spread(3)
    swapped(1)
    swapped(2)
    turn(1)
    gate = settle(0)
    expand(0)
    expand(1)
    down_load.wait()
    swapped(3)
    contract(0, gate)
    for k in range(1, DEPTH):
        gate = settle(k)
        expand(0)
        expand(1)
        contract(k, gate)
        if k == 1:
            return_plane()
        else:
            return_far(k)
    return_own()
    return_home(2)
    return_home(3)
    result = sum_home(0, keep_ref[...])
    for k in range(2, DEPTH):
        await_box(z_in.at[planes[k]], rz_send.at[k], rz_recv.at[planes[k]])
        result = result + z_in[planes[k]].astype(jnp.float32)
    out_ref[...] = result.astype(jnp.bfloat16)
    for copy in waits:
        copy.wait_send()


def whole_layer(
    residual,
    query,
    fresh,
    keys,
    lengths,
    placement,
    parents,
    accepted,
    expert_ids,
    value_weight,
    out_weight,
    gain,
    router_weight,
    gate_weight,
    up_weight,
    down_weight,
):
    n_blk, rows, width = residual.shape
    hidden = gate_weight.shape[0]
    shard = keys.shape[1]
    lines = query.shape[0]
    heads = value_weight.shape[0]
    experts = router_weight.shape[0]
    smem = pl.BlockSpec(memory_space=pltpu.SMEM)
    hbm = pl.BlockSpec(memory_space=pl.ANY)
    vmem = pl.BlockSpec(memory_space=pltpu.VMEM)
    dma = pltpu.SemaphoreType.DMA
    like = lambda a: pltpu.VMEM(a.shape, a.dtype)
    pair = lambda a: pltpu.VMEM((2,) + a.shape, a.dtype)
    box = lambda *dims: pltpu.VMEM(dims + (rows, width), jnp.bfloat16)
    f32 = lambda *dims: pltpu.VMEM(dims, jnp.float32)
    return pl.pallas_call(
        whole_kernel,
        out_shape=(pltpu.VMEM((rows, width), jnp.bfloat16), pltpu.VMEM(keys.shape, jnp.bfloat16)),
        in_specs=[smem] * 3 + [hbm] * 13,
        out_specs=(vmem, vmem),
        scratch_shapes=[
            like(parents),
            like(expert_ids),
            like(gain),
            like(router_weight),
            like(residual),
            like(query),
            like(fresh),
            pair(keys),
            pltpu.VMEM((value_weight.shape[1], heads * value_weight.shape[2]), jnp.bfloat16),
            like(out_weight),
            pair(gate_weight),
            pair(up_weight),
            pair(down_weight),
            pltpu.VMEM((2, width, hidden), jnp.bfloat16),
            pltpu.VMEM((2, width, hidden), jnp.bfloat16),
            f32(n_blk, rows, width),
            f32(rows, width),
            f32(rows, width),
            box(),
            box(),
            box(DEPTH, 4),
            f32(4 * rows, width),
            pltpu.VMEM((4 * rows, width), jnp.bfloat16),
            pltpu.VMEM((2, 4 * rows, hidden), jnp.bfloat16),
            f32(DEPTH, 4 * rows, experts),
            box(DEPTH, 4),
            box(DEPTH),
            box(DEPTH),
            box(DEPTH),
            box(4),
            box(DEPTH),
            box(3),
            box(DEPTH),
            dma((12,)),
            dma((heads,)),
            dma((5,)),
            dma((5,)),
            dma((DEPTH,)),
            dma((DEPTH,)),
            dma((DEPTH,)),
            dma((DEPTH,)),
            dma((3,)),
            dma((DEPTH, 4)),
            dma((DEPTH,)),
            dma((DEPTH,)),
            dma((DEPTH,)),
            dma((DEPTH,)),
            dma((DEPTH,)),
            dma((DEPTH,)),
            dma((4,)),
            dma((4,)),
            dma((DEPTH,)),
            dma((DEPTH,)),
        ],
        compiler_params=pltpu.CompilerParams(
            collective_id=2, has_side_effects=True, vmem_limit_bytes=VMEM_LIMIT
        ),
    )(
        placement,
        lengths,
        accepted,
        parents,
        expert_ids,
        gain,
        router_weight,
        residual,
        query,
        fresh,
        keys,
        value_weight,
        out_weight,
        gate_weight,
        up_weight,
        down_weight,
    )


def on_device(
    residual,
    queries,
    new_latents,
    latent_cache,
    lengths,
    placement,
    parents,
    accepted,
    expert_ids,
    value_weight,
    out_weight,
    norm_gain,
    router_weight,
    gate_weight,
    up_weight,
    down_weight,
):
    req = lax.axis_index("req")
    block_index = lax.axis_index("blk")
    n_req = lax.axis_size("req")
    n_blk = lax.axis_size("blk")
    drafts = residual.shape[1]
    width = residual.shape[2]
    shard_len = latent_cache.shape[1]
    experts = router_weight.shape[1]
    rows_here = drafts // n_blk
    depth = n_req // 4
    if n_req == 4 * DEPTH and n_blk == 2 and n_blk * n_req * rows_here <= FUSED_ROWS:
        layer_out, updated = whole_layer(
            residual[0].reshape(n_blk, rows_here, width),
            queries[0].reshape(drafts * queries.shape[2], queries.shape[3]),
            new_latents[0],
            latent_cache[0].T,
            lengths,
            placement,
            parents,
            accepted.T,
            expert_ids.transpose(2, 0, 1),
            value_weight,
            out_weight,
            norm_gain,
            router_weight.T,
            gate_weight[0].T,
            up_weight[0].T,
            down_weight[0],
        )
        return (layer_out[None], updated.T[None])

    request = lax.dynamic_index_in_dim(placement, req, 0, keepdims=False)
    length = lax.dynamic_index_in_dim(lengths, request, 0, keepdims=False)
    parent_row = lax.dynamic_index_in_dim(parents, request, 0, keepdims=False)
    taken = lax.dynamic_index_in_dim(accepted, request, 0, keepdims=False)

    named = jnp.any(
        expert_ids[:, :, :, None] == jnp.arange(experts, dtype=jnp.int32), axis=2
    ).astype(jnp.bfloat16)
    seat = (placement[:, None] == jnp.arange(n_req, dtype=jnp.int32)[None, :]).astype(jnp.bfloat16)
    named = jnp.einsum("sr,rte->ste", seat, named, preferred_element_type=jnp.float32)
    named = named.reshape(depth, 4, n_blk, rows_here, experts)

    piece = lax.all_gather(latent_cache[0], "blk", axis=0, tiled=True)
    attn = attend_slot(
        queries[0], new_latents[0], piece, length, parent_row, value_weight, out_weight
    )
    attn = attn.reshape(n_blk, rows_here, width)
    home_rows = residual.reshape(n_blk, rows_here, width)
    gain = norm_gain.reshape(1, width)
    mid, gathered = gather_rows(attn, home_rows, gain, n_req, n_blk)
    rows = gathered.reshape(n_req * drafts, width)
    score_e = jax.nn.sigmoid(jnp.dot(rows, router_weight, preferred_element_type=jnp.float32))
    chosen = named.transpose(2, 1, 0, 3, 4).reshape(n_req * drafts, experts) * score_e
    mine = jnp.arange(experts, dtype=jnp.int32)[None, :] == req
    gate = (
        route_scale
        * jnp.sum(jnp.where(mine, chosen, 0.0), axis=1, keepdims=True)
        / jnp.sum(chosen, axis=1, keepdims=True)
    )
    act = (
        jax.nn.silu(jnp.dot(rows, gate_weight[0], preferred_element_type=jnp.float32))
        * jnp.dot(rows, up_weight[0], preferred_element_type=jnp.float32)
    ).astype(jnp.bfloat16)
    parts = jnp.dot(act, down_weight[0], preferred_element_type=jnp.float32) * gate
    parts = parts.astype(jnp.bfloat16).reshape(n_blk, 4, depth, rows_here, width)
    layer_out = scatter_rows(parts, mid, n_req, n_blk)

    stored = latent_cache[0]
    chosen_rows = new_latents[0][taken]
    targets = length + jnp.arange(taken.shape[0], dtype=jnp.int32) - block_index * shard_len
    hit = jnp.arange(shard_len, dtype=jnp.int32)[:, None] == targets[None, :]
    written = jnp.dot(
        hit.astype(jnp.bfloat16), chosen_rows, preferred_element_type=jnp.float32
    ).astype(jnp.bfloat16)
    updated = jnp.where(jnp.any(hit, axis=1)[:, None], written, stored)
    return (layer_out[None], updated[None])


def solution(mesh):
    return jax.shard_map(
        on_device,
        mesh=mesh,
        in_specs=(
            P("req", None, None),
            P("req", None, "blk", None),
            P("req", None, None),
            P("req", "blk", None),
            P(),
            P(),
            P(),
            P(),
            P(),
            P("blk", None, None),
            P("blk", None),
            P(),
            P(),
            P("req", None, "blk"),
            P("req", None, "blk"),
            P("req", "blk", None),
        ),
        out_specs=(P("req", "blk", None), P("req", "blk", None)),
        check_vma=False,
    )
```

```python
import functools

import jax
import jax.numpy as jnp
from jax import lax
from jax.experimental import pallas as pl
from jax.experimental.pallas import tpu as pltpu
from jax.sharding import PartitionSpec as P

LATENT = 512
TOP = 6
MESH = pl.DeviceIdType.MESH
VMEM_LIMIT = 56 * 1024 * 1024
FUSED_ROWS = 1024
DEPTH = 4

score_scale = 0.07216878364870322
route_scale = 2.446
norm_eps = 1e-06
far_below = -1e30


def ancestors(parent_row):
    span = parent_row.shape[0]
    links = (parent_row[:, None] == jnp.arange(span, dtype=jnp.int32)[None, :]).astype(jnp.float32)
    reach = jnp.eye(span, dtype=jnp.float32) + links
    for _ in range(span.bit_length()):
        reach = jnp.minimum(jnp.dot(reach, reach, precision=lax.Precision.HIGHEST), 1.0)
    return reach


def attend_kernel(length_ref, query_ref, fresh_ref, keys_ref, reach_ref, value_ref, out_weight_ref, attn_ref):
    drafts = fresh_ref.shape[0]
    heads = value_ref.shape[0]
    lines = drafts * heads
    query, fresh, keys = query_ref[...], fresh_ref[...], keys_ref[...]
    line = lax.broadcasted_iota(jnp.int32, (lines, drafts), 0)
    first = lax.broadcasted_iota(jnp.int32, (lines, drafts), 1) * heads
    owner = ((line >= first) & (line < first + heads)).astype(jnp.float32)
    reach = jnp.dot(owner, reach_ref[...], preferred_element_type=jnp.float32)
    stored = jnp.dot(query, keys, preferred_element_type=jnp.float32) * score_scale
    where = lax.broadcasted_iota(jnp.int32, stored.shape, 1)
    stored = jnp.where(where < length_ref[0], stored, far_below)
    own = jnp.where(reach > 0.5, dot_nt(query, fresh) * score_scale, far_below)
    top = jnp.maximum(
        jnp.max(stored, axis=1, keepdims=True), jnp.max(own, axis=1, keepdims=True)
    )
    stored = jnp.exp(stored - top)
    own = jnp.exp(own - top)
    total = jnp.sum(stored, axis=1, keepdims=True) + jnp.sum(own, axis=1, keepdims=True)
    acc = dot_nt(stored.astype(jnp.bfloat16), keys[:LATENT]) + jnp.dot(
        own.astype(jnp.bfloat16), fresh[:, :LATENT], preferred_element_type=jnp.float32
    )
    context = (acc / total).astype(jnp.bfloat16)
    row = lax.broadcasted_iota(jnp.int32, (drafts, lines), 0) * heads
    column = lax.broadcasted_iota(jnp.int32, (drafts, lines), 1)
    outs = []
    for head in range(heads):
        select = (column == row + head).astype(jnp.bfloat16)
        one = jnp.dot(select, context, preferred_element_type=jnp.float32).astype(jnp.bfloat16)
        outs.append(
            jnp.dot(one, value_ref[head], preferred_element_type=jnp.float32).astype(jnp.bfloat16)
        )
    attn_ref[...] = jnp.dot(
        jnp.concatenate(outs, axis=1), out_weight_ref[...], preferred_element_type=jnp.float32
    )


def attend_slot(query, fresh, piece, length, parent_row, value_weight, out_weight):
    drafts, heads, width = query.shape
    vmem = pl.BlockSpec(memory_space=pltpu.VMEM)
    return pl.pallas_call(
        attend_kernel,
        out_shape=jax.ShapeDtypeStruct((drafts, out_weight.shape[1]), jnp.float32),
        in_specs=[pl.BlockSpec(memory_space=pltpu.SMEM)] + [vmem] * 6,
        out_specs=vmem,
        compiler_params=pltpu.CompilerParams(vmem_limit_bytes=VMEM_LIMIT),
    )(
        length.reshape(1),
        query.reshape(drafts * heads, width),
        fresh,
        piece.T,
        ancestors(parent_row),
        value_weight,
        out_weight,
    )


class Place:
    def __init__(self, n_req, n_blk):
        self.depth = n_req // 4
        self.n_blk = n_blk
        req = lax.axis_index("req")
        self.blk = lax.axis_index("blk")
        self.z = req // 4
        self.y = (req // 2) % 2
        self.x = req % 2
        self.swap = self.blk % 2
        self.a = self.y * (1 - self.swap) + self.x * self.swap
        self.b = self.x * (1 - self.swap) + self.y * self.swap
        self.home = self.group(self.a, self.b)

    def group(self, a, b):
        return a * (2 - self.swap) + b * (1 + self.swap)

    def device(self, z, a, b):
        return (z * 4 + self.group(a, b), self.blk)

    def far(self, step):
        return (self.z + step) % self.depth

    def a_side(self):
        return self.device(self.z, 1 - self.a, self.b)

    def b_side(self):
        return self.device(self.z, self.a, 1 - self.b)

    def z_side(self, step):
        return self.device(self.far(step), self.a, self.b)

    def sibling_blk(self, step):
        return (self.blk + step) % self.n_blk

    def sibling(self, step):
        return (self.z * 4 + self.home, self.sibling_blk(step))

    def greet(self):
        barrier = pltpu.get_barrier_semaphore()
        others = [self.a_side(), self.b_side()]
        others += [self.z_side(step) for step in range(1, self.depth)]
        others += [self.sibling(step) for step in range(1, self.n_blk)]
        for other in others:
            pl.semaphore_signal(barrier, inc=1, device_id=other, device_id_type=MESH)
        pl.semaphore_wait(barrier, len(others))


def send(src, dst, send_sem, recv_sem, target):
    return pltpu.make_async_remote_copy(
        src_ref=src,
        dst_ref=dst,
        send_sem=send_sem,
        recv_sem=recv_sem,
        device_id=target,
        device_id_type=MESH,
    )


def gather_kernel(
    n_req,
    n_blk,
    attn_ref,
    res_ref,
    gain_ref,
    mid_ref,
    rows_ref,
    outbox,
    inbox,
    box_send,
    box_recv,
    z_send,
    a_send,
    b_send,
    land,
    sib_send,
    sib_recv,
):
    at = Place(n_req, n_blk)
    depth, blk, home = at.depth, at.blk, at.home
    outbox[...] = attn_ref[...].astype(jnp.bfloat16)
    at.greet()
    swaps = []
    for step in range(1, n_blk):
        copy = send(
            outbox.at[at.sibling_blk(step)],
            inbox.at[step - 1],
            box_send.at[step - 1],
            box_recv.at[step - 1],
            at.sibling(step),
        )
        copy.start()
        swaps.append(copy)
    mid = res_ref[blk].astype(jnp.float32) + attn_ref[blk]
    for step in range(1, n_blk):
        swaps[step - 1].wait_recv()
        mid = mid + inbox[step - 1].astype(jnp.float32)
    mid_ref[...] = mid
    scale = lax.rsqrt(jnp.mean(mid * mid, axis=1, keepdims=True) + norm_eps)
    rows_ref[blk, home, at.z] = (mid * scale * gain_ref[...].astype(jnp.float32)).astype(jnp.bfloat16)

    waits = []

    def forward(group, z, send_sem, target):
        piece = rows_ref.at[blk, group, z]
        copy = send(piece, piece, send_sem, land.at[group, z], target)
        copy.start()
        waits.append(copy)

    def landed(group, z):
        piece = rows_ref.at[blk, group, z]
        send(piece, piece, z_send.at[0], land.at[group, z], at.a_side()).wait_recv()

    def share(group):
        for step in range(1, n_blk):
            block = rows_ref.at[blk, group]
            copy = send(
                block, block, sib_send.at[step - 1, group], sib_recv.at[step - 1, group], at.sibling(step)
            )
            copy.start()
            waits.append(copy)

    for step in range(1, depth):
        forward(home, at.z, z_send.at[step - 1], at.z_side(step))
    forward(home, at.z, b_send.at[0, 0], at.b_side())
    forward(home, at.z, a_send.at[0], at.a_side())
    for step in range(1, depth):
        z = at.far(step)
        landed(home, z)
        forward(home, z, b_send.at[0, step], at.b_side())
        forward(home, z, a_send.at[step], at.a_side())
    share(home)
    over = at.group(1 - at.a, at.b)
    for step in range(depth):
        z = at.far(step)
        landed(over, z)
        forward(over, z, b_send.at[1, step], at.b_side())
    share(over)
    for a in (at.a, 1 - at.a):
        group = at.group(a, 1 - at.b)
        for step in range(depth):
            landed(group, at.far(step))
        share(group)
    for step in range(1, n_blk):
        source = (blk + n_blk - step) % n_blk
        for group in range(4):
            block = rows_ref.at[source, group]
            send(
                block, block, sib_send.at[step - 1, group], sib_recv.at[step - 1, group], at.sibling(step)
            ).wait_recv()
    for copy in waits:
        copy.wait_send()
    for copy in swaps:
        copy.wait_send()


def gather_rows(attn, residual, gain, n_req, n_blk):
    _, rows, width = attn.shape
    depth = n_req // 4
    vmem = pl.BlockSpec(memory_space=pltpu.VMEM)
    dma = pltpu.SemaphoreType.DMA
    sibs = max(n_blk - 1, 1)
    return pl.pallas_call(
        functools.partial(gather_kernel, n_req, n_blk),
        out_shape=(
            jax.ShapeDtypeStruct((rows, width), jnp.float32),
            jax.ShapeDtypeStruct((n_blk, 4, depth, rows, width), jnp.bfloat16),
        ),
        in_specs=[vmem] * 3,
        out_specs=(vmem, vmem),
        scratch_shapes=[
            pltpu.VMEM((n_blk, rows, width), jnp.bfloat16),
            pltpu.VMEM((sibs, rows, width), jnp.bfloat16),
            dma((sibs,)),
            dma((sibs,)),
            dma((depth,)),
            dma((depth,)),
            dma((2, depth)),
            dma((4, depth)),
            dma((sibs, 4)),
            dma((sibs, 4)),
        ],
        compiler_params=pltpu.CompilerParams(
            collective_id=0, has_side_effects=True, vmem_limit_bytes=VMEM_LIMIT
        ),
    )(attn, residual, gain)


def scatter_kernel(
    n_req,
    n_blk,
    part_ref,
    mid_ref,
    out_ref,
    sib_in,
    b_in,
    a_in,
    z_in,
    sums,
    sib_send,
    sib_recv,
    b_send,
    b_recv,
    a_send,
    a_recv,
    z_send,
    z_recv,
):
    at = Place(n_req, n_blk)
    depth, blk = at.depth, at.blk
    at.greet()
    waits = []
    order = [
        at.group(1 - at.a, 1 - at.b),
        at.group(at.a, 1 - at.b),
        at.group(1 - at.a, at.b),
        at.home,
    ]

    def put(src, dst, send_sem, recv_sem, target):
        copy = send(src, dst, send_sem, recv_sem, target)
        copy.start()
        waits.append(copy)

    for k in range(4):
        for step in range(1, n_blk):
            other_swap = at.sibling_blk(step) % 2
            a = at.y * (1 - other_swap) + at.x * other_swap
            b = at.x * (1 - other_swap) + at.y * other_swap
            ta = a if k in (1, 3) else 1 - a
            tb = b if k in (2, 3) else 1 - b
            group = ta * (2 - other_swap) + tb * (1 + other_swap)
            put(
                part_ref.at[at.sibling_blk(step), group],
                sib_in.at[step - 1, k],
                sib_send.at[step - 1, k],
                sib_recv.at[step - 1, k],
                at.sibling(step),
            )

    def wait_sib(k):
        for step in range(1, n_blk):
            box = sib_in.at[step - 1, k]
            send(box, box, sib_send.at[step - 1, k], sib_recv.at[step - 1, k], at.sibling(step)).wait_recv()

    def own(k, z):
        total = part_ref[blk, order[k], z].astype(jnp.float32)
        for step in range(1, n_blk):
            total = total + sib_in[step - 1, k, z].astype(jnp.float32)
        return total

    def await_box(box, send_sem, recv_sem):
        send(box, box, send_sem, recv_sem, at.a_side()).wait_recv()

    steps = list(range(1, depth)) + [0]
    for k in (0, 1):
        wait_sib(k)
        for step in steps:
            z = at.far(step)
            sums[k, step] = own(k, z).astype(jnp.bfloat16)
            put(sums.at[k, step], b_in.at[k, step], b_send.at[k, step], b_recv.at[k, step], at.b_side())
    wait_sib(2)
    for step in steps:
        z = at.far(step)
        total = own(2, z)
        await_box(b_in.at[0, step], b_send.at[0, step], b_recv.at[0, step])
        sums[2, step] = (total + b_in[0, step].astype(jnp.float32)).astype(jnp.bfloat16)
        put(sums.at[2, step], a_in.at[step], a_send.at[step], a_recv.at[step], at.a_side())
    wait_sib(3)
    keep = None
    for step in steps:
        z = at.far(step)
        total = own(3, z)
        await_box(b_in.at[1, step], b_send.at[1, step], b_recv.at[1, step])
        total = total + b_in[1, step].astype(jnp.float32)
        await_box(a_in.at[step], a_send.at[step], a_recv.at[step])
        total = total + a_in[step].astype(jnp.float32)
        if step > 0:
            sums[3, step] = total.astype(jnp.bfloat16)
            put(sums.at[3, step], z_in.at[step - 1], z_send.at[step - 1], z_recv.at[step - 1], at.z_side(step))
        else:
            keep = total
    total = mid_ref[...] + keep
    for step in range(1, depth):
        await_box(z_in.at[step - 1], z_send.at[step - 1], z_recv.at[step - 1])
        total = total + z_in[step - 1].astype(jnp.float32)
    out_ref[...] = total.astype(jnp.bfloat16)
    for copy in waits:
        copy.wait_send()


def scatter_rows(parts, mid, n_req, n_blk):
    _, _, depth, rows, width = parts.shape
    vmem = pl.BlockSpec(memory_space=pltpu.VMEM)
    dma = pltpu.SemaphoreType.DMA
    sibs = max(n_blk - 1, 1)
    far = max(depth - 1, 1)
    box = lambda *dims: pltpu.VMEM(dims + (rows, width), jnp.bfloat16)
    return pl.pallas_call(
        functools.partial(scatter_kernel, n_req, n_blk),
        out_shape=jax.ShapeDtypeStruct((rows, width), jnp.bfloat16),
        in_specs=[vmem] * 2,
        out_specs=vmem,
        scratch_shapes=[
            box(sibs, 4, depth),
            box(2, depth),
            box(depth),
            box(far),
            box(4, depth),
            dma((sibs, 4)),
            dma((sibs, 4)),
            dma((2, depth)),
            dma((2, depth)),
            dma((depth,)),
            dma((depth,)),
            dma((far,)),
            dma((far,)),
        ],
        compiler_params=pltpu.CompilerParams(
            collective_id=1, has_side_effects=True, vmem_limit_bytes=VMEM_LIMIT
        ),
    )(parts, mid)


def dot_nt(left, right):
    return lax.dot_general(left, right, (((1,), (1,)), ((), ())), preferred_element_type=jnp.float32)


def whole_kernel(
    placement_ref,
    lengths_ref,
    accepted_ref,
    parents_hbm,
    ids_hbm,
    gain_hbm,
    router_hbm,
    res_hbm,
    query_hbm,
    fresh_hbm,
    keys_hbm,
    value_hbm,
    out_weight_hbm,
    gate_hbm,
    up_hbm,
    down_hbm,
    out_ref,
    updated_ref,
    parents_ref,
    ids_ref,
    gain_ref,
    router_ref,
    res_ref,
    query_ref,
    fresh_ref,
    keys_ref,
    value_ref,
    out_weight_ref,
    gate_ref,
    up_ref,
    down_ref,
    gate_t,
    up_t,
    attn_ref,
    mid_ref,
    keep_ref,
    outbox,
    inbox,
    rows_ref,
    flat,
    x_ref,
    act_ref,
    named_ref,
    part_ref,
    f_in,
    a_in,
    b_in,
    q_in,
    z_in,
    plane_sum,
    home_sum,
    local_sem,
    value_sem,
    swap_send,
    swap_recv,
    gz_send,
    gf_send,
    ga_send,
    gb_send,
    gq_send,
    land,
    rf_send,
    rf_recv,
    ra_send,
    ra_recv,
    rb_send,
    rb_recv,
    rq_send,
    rq_recv,
    rz_send,
    rz_recv,
):
    at = Place(4 * DEPTH, 2)
    blk, z, home = at.blk, at.z, at.home
    over = at.group(1 - at.a, at.b)
    side = at.group(at.a, 1 - at.b)
    far = at.group(1 - at.a, 1 - at.b)
    req = lax.axis_index("req")
    planes = [z, z + 1 - 2 * (z % 2), 2 - z // 2, 3 - 3 * (z // 2)]
    sibling = at.sibling(1)
    peers = [None] + [at.device(plane, at.a, at.b) for plane in planes[1:]]
    lines = query_ref.shape[0]
    drafts = fresh_ref.shape[0]
    heads = lines // drafts
    rows = mid_ref.shape[0]
    shard = keys_ref.shape[2]
    hidden = gate_ref.shape[1]
    waits = []

    barrier = pltpu.get_barrier_semaphore()
    diagonal = at.device(z, 1 - at.a, 1 - at.b)
    partners = [sibling, at.a_side(), at.b_side(), diagonal] + peers[1:]
    for partner in partners:
        pl.semaphore_signal(barrier, inc=1, device_id=partner, device_id_type=MESH)

    moves = [
        (query_hbm, query_ref),
        (keys_hbm, keys_ref.at[0]),
        (fresh_hbm, fresh_ref),
        (parents_hbm, parents_ref),
        (out_weight_hbm, out_weight_ref),
        (res_hbm, res_ref),
        (gain_hbm, gain_ref),
        (ids_hbm, ids_ref),
        (router_hbm, router_ref),
        (gate_hbm, gate_ref.at[0]),
        (up_hbm, up_ref.at[0]),
        (down_hbm, down_ref.at[0]),
    ]
    loads = [pltpu.make_async_copy(src, dst, local_sem.at[i]) for i, (src, dst) in enumerate(moves)]
    (
        query_load,
        keys_load,
        fresh_load,
        parents_load,
        out_weight_load,
        res_load,
        gain_load,
        ids_load,
        router_load,
        gate_load,
        up_load,
        down_load,
    ) = loads
    value_loads = [
        pltpu.make_async_copy(value_hbm.at[head], value_ref.at[:, pl.ds(head * 128, 128)], value_sem.at[head])
        for head in range(heads)
    ]
    for load in loads[:4] + value_loads + loads[4:]:
        load.start()

    def put(src, dst, send_sem, recv_sem, target):
        copy = send(src, dst, send_sem, recv_sem, target)
        copy.start()
        waits.append(copy)

    def await_box(box, send_sem, recv_sem):
        send(box, box, send_sem, recv_sem, sibling).wait_recv()

    swaps = [
        (keys_hbm, keys_ref.at[1]),
        (gate_hbm, gate_ref.at[1]),
        (up_hbm, up_ref.at[1]),
        (down_hbm, down_ref.at[1]),
    ]

    def swap(i):
        put(swaps[i][0], swaps[i][1], swap_send.at[i], swap_recv.at[i], sibling)

    def swapped(i):
        await_box(swaps[i][1], swap_send.at[i], swap_recv.at[i])

    request = placement_ref[req]
    length = lengths_ref[request]

    parents_load.wait()
    parent_row = parents_ref[pl.ds(request, 1), :]
    upper = lax.broadcasted_iota(jnp.int32, (drafts, drafts), 0)
    lower = lax.broadcasted_iota(jnp.int32, (drafts, drafts), 1)
    reach = (parent_row == upper).astype(jnp.float32) + (upper == lower).astype(jnp.float32)
    for _ in range(drafts.bit_length()):
        half = reach.astype(jnp.bfloat16)
        reach = jnp.minimum(jnp.dot(half, half, preferred_element_type=jnp.float32), 1.0)
    line = lax.broadcasted_iota(jnp.int32, (lines, drafts), 0)
    first = lax.broadcasted_iota(jnp.int32, (lines, drafts), 1) * heads
    owner = ((line >= first) & (line < first + heads)).astype(jnp.float32).astype(jnp.bfloat16)
    seen = dot_nt(owner, reach.astype(jnp.bfloat16))

    pl.semaphore_wait(barrier, len(partners))
    for i in range(4):
        swap(i)

    query_load.wait()
    fresh_load.wait()
    query, fresh = query_ref[...], fresh_ref[...]
    own = jnp.where(seen > 0.5, dot_nt(query, fresh) * score_scale, far_below)
    place = lax.broadcasted_iota(jnp.int32, (lines, shard), 1)

    def scores(i, start):
        stored = jnp.dot(query, keys_ref[i], preferred_element_type=jnp.float32) * score_scale
        return jnp.where(place + start < length, stored, far_below)

    keys_load.wait()
    near = scores(0, blk * shard)
    swapped(0)
    apart = scores(1, (1 - blk) * shard)
    top = jnp.maximum(
        jnp.maximum(jnp.max(near, axis=1, keepdims=True), jnp.max(apart, axis=1, keepdims=True)),
        jnp.max(own, axis=1, keepdims=True),
    )
    near, apart, own = jnp.exp(near - top), jnp.exp(apart - top), jnp.exp(own - top)
    total = (
        jnp.sum(near, axis=1, keepdims=True)
        + jnp.sum(apart, axis=1, keepdims=True)
        + jnp.sum(own, axis=1, keepdims=True)
    )
    acc = (
        dot_nt(near.astype(jnp.bfloat16), keys_ref[0, :LATENT])
        + dot_nt(apart.astype(jnp.bfloat16), keys_ref[1, :LATENT])
        + jnp.dot(own.astype(jnp.bfloat16), fresh[:, :LATENT], preferred_element_type=jnp.float32)
    )
    context = (acc * (1.0 / total)).astype(jnp.bfloat16)
    for load in value_loads:
        load.wait()
    every = jnp.dot(context, value_ref[...], preferred_element_type=jnp.float32)
    head_of = lax.broadcasted_iota(jnp.int32, every.shape, 0) % heads
    column_head = lax.broadcasted_iota(jnp.int32, every.shape, 1) // 128
    every = jnp.where(head_of == column_head, every, 0.0).astype(jnp.bfloat16)
    row = lax.broadcasted_iota(jnp.int32, (drafts, lines), 0) * heads
    column = lax.broadcasted_iota(jnp.int32, (drafts, lines), 1)
    gather = ((column >= row) & (column < row + heads)).astype(jnp.float32).astype(jnp.bfloat16)
    head_out = jnp.dot(gather, every, preferred_element_type=jnp.float32).astype(jnp.bfloat16)
    out_weight_load.wait()
    attn = jnp.dot(head_out, out_weight_ref[...], preferred_element_type=jnp.float32)
    attn_ref[0] = attn[:rows]
    attn_ref[1] = attn[rows:]
    outbox[...] = attn_ref[1 - blk].astype(jnp.bfloat16)
    put(outbox, inbox, swap_send.at[4], swap_recv.at[4], sibling)
    res_load.wait()
    gain_load.wait()
    mid = res_ref[blk].astype(jnp.float32) + attn_ref[blk]
    await_box(inbox, swap_send.at[4], swap_recv.at[4])
    mid = mid + inbox[...].astype(jnp.float32)
    mid_ref[...] = mid
    scale = lax.rsqrt(jnp.mean(mid * mid, axis=1, keepdims=True) + norm_eps)
    rows_ref[z, home] = (mid * scale * gain_ref[...].astype(jnp.float32).reshape(1, -1)).astype(jnp.bfloat16)

    def forward(plane, group, send_sem, target):
        piece = rows_ref.at[plane, group]
        put(piece, piece, send_sem, land.at[plane, group], target)

    def landed(plane, group):
        await_box(rows_ref.at[plane, group], gz_send.at[0], land.at[plane, group])

    def spread(k):
        if k > 0:
            landed(planes[k], home)
        forward(planes[k], home, gf_send.at[k], diagonal)
        forward(planes[k], home, ga_send.at[k], at.a_side())
        forward(planes[k], home, gb_send.at[k], at.b_side())

    def spread_plane():
        for i, group in enumerate((over, side, far)):
            landed(z, group)
            forward(z, group, gq_send.at[i], peers[1])

    forward(z, home, gz_send.at[3], peers[3])
    leading = waits.pop()
    spread(0)

    pick_draft = lax.broadcasted_iota(jnp.int32, (drafts, shard), 0)
    pick_place = lax.broadcasted_iota(jnp.int32, (drafts, shard), 1)
    picked = jnp.zeros((drafts, shard), jnp.float32)
    for i in range(accepted_ref.shape[0]):
        target = length + i - blk * shard
        picked = jnp.where((pick_draft == accepted_ref[i, request]) & (pick_place == target), 1.0, picked)
    hit = jnp.max(picked, axis=0, keepdims=True)
    written = lax.dot_general(
        fresh, picked.astype(jnp.bfloat16), (((0,), (0,)), ((), ())), preferred_element_type=jnp.float32
    )
    updated_ref[...] = jnp.where(hit > 0.5, written, keys_ref[0].astype(jnp.float32)).astype(jnp.bfloat16)

    ids_load.wait()
    experts = router_ref.shape[0]
    expert_at = lax.broadcasted_iota(jnp.int32, (experts, drafts), 0)
    seat = (
        lax.broadcasted_iota(jnp.int32, (rows, drafts), 1)
        == lax.broadcasted_iota(jnp.int32, (rows, drafts), 0) + blk * rows
    ).astype(jnp.float32).astype(jnp.bfloat16)
    for k in range(DEPTH):
        for group in range(4):
            asked = placement_ref[planes[k] * 4 + group]
            names = jnp.zeros((experts, drafts), jnp.float32)
            for j in range(TOP):
                names = jnp.where(ids_ref[j, pl.ds(asked, 1), :] == expert_at, 1.0, names)
            named_ref[k, pl.ds(group * rows, rows), :] = dot_nt(seat, names.astype(jnp.bfloat16))

    def turn(i):
        for source, dest in ((gate_ref, gate_t), (up_ref, up_t)):
            for c in range(source.shape[2] // 256):
                dest[i, pl.ds(c * 256, 256), :] = source[i, :, pl.ds(c * 256, 256)].T

    def load_rows(k):
        for group in range(4):
            flat[pl.ds(group * rows, rows), :] = rows_ref[planes[k], group].astype(jnp.float32)
        x_ref[...] = flat[...].astype(jnp.bfloat16)

    def gate_of(k):
        chosen = named_ref[k] * jax.nn.sigmoid(dot_nt(x_ref[...], router_ref[...]))
        mine = lax.broadcasted_iota(jnp.int32, chosen.shape, 1) == req
        return (
            route_scale
            * jnp.sum(jnp.where(mine, chosen, 0.0), axis=1, keepdims=True)
            / jnp.sum(chosen, axis=1, keepdims=True)
        )

    def expand(i):
        x = x_ref[...]
        act_ref[i] = (
            jax.nn.silu(jnp.dot(x, gate_t[i], preferred_element_type=jnp.float32))
            * jnp.dot(x, up_t[i], preferred_element_type=jnp.float32)
        ).astype(jnp.bfloat16)

    def contract(k, gate):
        flat[...] = (
            jnp.dot(act_ref[0], down_ref[0], preferred_element_type=jnp.float32)
            + jnp.dot(act_ref[1], down_ref[1], preferred_element_type=jnp.float32)
        ) * gate
        for group in range(4):
            part_ref[k, group] = flat[pl.ds(group * rows, rows), :].astype(jnp.bfloat16)

    def return_plane():
        for i, group in enumerate((far, over, side, home)):
            put(part_ref.at[1, group], q_in.at[i], rq_send.at[i], rq_recv.at[i], peers[1])

    def return_far(k):
        put(part_ref.at[k, far], f_in.at[k], rf_send.at[k], rf_recv.at[k], diagonal)
        put(part_ref.at[k, over], a_in.at[k], ra_send.at[k], ra_recv.at[k], at.a_side())
        put(part_ref.at[k, side], b_in.at[k], rb_send.at[k], rb_recv.at[k], at.b_side())

    def plane_total(i, group):
        await_box(q_in.at[i], rq_send.at[i], rq_recv.at[i])
        return part_ref[0, group].astype(jnp.float32) + q_in[i].astype(jnp.float32)

    def return_own():
        plane_sum[0] = plane_total(0, far).astype(jnp.bfloat16)
        put(plane_sum.at[0], f_in.at[0], rf_send.at[0], rf_recv.at[0], diagonal)
        plane_sum[1] = plane_total(1, over).astype(jnp.bfloat16)
        put(plane_sum.at[1], a_in.at[0], ra_send.at[0], ra_recv.at[0], at.a_side())
        plane_sum[2] = plane_total(2, side).astype(jnp.bfloat16)
        put(plane_sum.at[2], b_in.at[0], rb_send.at[0], rb_recv.at[0], at.b_side())
        keep_ref[...] = mid_ref[...] + plane_total(3, home)

    def sum_home(k, here):
        for box, send_sem, recv_sem in ((f_in, rf_send, rf_recv), (a_in, ra_send, ra_recv), (b_in, rb_send, rb_recv)):
            await_box(box.at[k], send_sem.at[k], recv_sem.at[k])
            here = here + box[k].astype(jnp.float32)
        return here

    def return_home(k):
        home_sum[k] = sum_home(k, part_ref[k, home].astype(jnp.float32)).astype(jnp.bfloat16)
        put(home_sum.at[k], z_in.at[z], rz_send.at[k], rz_recv.at[z], peers[k])

    def settle(k):
        if k == 1:
            landed(planes[k], home)
        if k > 0:
            for group in (over, side, far):
                landed(planes[k], group)
        load_rows(k)
        return gate_of(k)

    gate_load.wait()
    up_load.wait()
    turn(0)
    router_load.wait()
    leading.wait_send()
    forward(z, home, gz_send.at[2], peers[2])
    forward(z, home, gz_send.at[1], peers[1])
    spread(3)
    spread_plane()
    spread(2)
    swapped(1)
    swapped(2)
    turn(1)
    gate = settle(0)
    expand(0)
    expand(1)
    down_load.wait()
    swapped(3)
    contract(0, gate)
    for k in (1, 3, 2):
        gate = settle(k)
        expand(0)
        expand(1)
        contract(k, gate)
        if k == 1:
            return_plane()
        else:
            return_far(k)
    return_own()
    return_home(3)
    return_home(2)
    result = sum_home(0, keep_ref[...])
    for k in (3, 2):
        await_box(z_in.at[planes[k]], rz_send.at[k], rz_recv.at[planes[k]])
        result = result + z_in[planes[k]].astype(jnp.float32)
    out_ref[...] = result.astype(jnp.bfloat16)
    for copy in waits:
        copy.wait_send()


def whole_layer(
    residual,
    query,
    fresh,
    keys,
    lengths,
    placement,
    parents,
    accepted,
    expert_ids,
    value_weight,
    out_weight,
    gain,
    router_weight,
    gate_weight,
    up_weight,
    down_weight,
):
    n_blk, rows, width = residual.shape
    hidden = gate_weight.shape[0]
    shard = keys.shape[1]
    lines = query.shape[0]
    heads = value_weight.shape[0]
    experts = router_weight.shape[0]
    smem = pl.BlockSpec(memory_space=pltpu.SMEM)
    hbm = pl.BlockSpec(memory_space=pl.ANY)
    vmem = pl.BlockSpec(memory_space=pltpu.VMEM)
    dma = pltpu.SemaphoreType.DMA
    like = lambda a: pltpu.VMEM(a.shape, a.dtype)
    pair = lambda a: pltpu.VMEM((2,) + a.shape, a.dtype)
    box = lambda *dims: pltpu.VMEM(dims + (rows, width), jnp.bfloat16)
    f32 = lambda *dims: pltpu.VMEM(dims, jnp.float32)
    return pl.pallas_call(
        whole_kernel,
        out_shape=(pltpu.VMEM((rows, width), jnp.bfloat16), pltpu.VMEM(keys.shape, jnp.bfloat16)),
        in_specs=[smem] * 3 + [hbm] * 13,
        out_specs=(vmem, vmem),
        scratch_shapes=[
            like(parents),
            like(expert_ids),
            like(gain),
            like(router_weight),
            like(residual),
            like(query),
            like(fresh),
            pair(keys),
            pltpu.VMEM((value_weight.shape[1], heads * value_weight.shape[2]), jnp.bfloat16),
            like(out_weight),
            pair(gate_weight),
            pair(up_weight),
            pair(down_weight),
            pltpu.VMEM((2, width, hidden), jnp.bfloat16),
            pltpu.VMEM((2, width, hidden), jnp.bfloat16),
            f32(n_blk, rows, width),
            f32(rows, width),
            f32(rows, width),
            box(),
            box(),
            box(DEPTH, 4),
            f32(4 * rows, width),
            pltpu.VMEM((4 * rows, width), jnp.bfloat16),
            pltpu.VMEM((2, 4 * rows, hidden), jnp.bfloat16),
            f32(DEPTH, 4 * rows, experts),
            box(DEPTH, 4),
            box(DEPTH),
            box(DEPTH),
            box(DEPTH),
            box(4),
            box(DEPTH),
            box(3),
            box(DEPTH),
            dma((12,)),
            dma((heads,)),
            dma((5,)),
            dma((5,)),
            dma((DEPTH,)),
            dma((DEPTH,)),
            dma((DEPTH,)),
            dma((DEPTH,)),
            dma((3,)),
            dma((DEPTH, 4)),
            dma((DEPTH,)),
            dma((DEPTH,)),
            dma((DEPTH,)),
            dma((DEPTH,)),
            dma((DEPTH,)),
            dma((DEPTH,)),
            dma((4,)),
            dma((4,)),
            dma((DEPTH,)),
            dma((DEPTH,)),
        ],
        compiler_params=pltpu.CompilerParams(
            collective_id=2, has_side_effects=True, vmem_limit_bytes=VMEM_LIMIT
        ),
    )(
        placement,
        lengths,
        accepted,
        parents,
        expert_ids,
        gain,
        router_weight,
        residual,
        query,
        fresh,
        keys,
        value_weight,
        out_weight,
        gate_weight,
        up_weight,
        down_weight,
    )


def on_device(
    residual,
    queries,
    new_latents,
    latent_cache,
    lengths,
    placement,
    parents,
    accepted,
    expert_ids,
    value_weight,
    out_weight,
    norm_gain,
    router_weight,
    gate_weight,
    up_weight,
    down_weight,
):
    req = lax.axis_index("req")
    block_index = lax.axis_index("blk")
    n_req = lax.axis_size("req")
    n_blk = lax.axis_size("blk")
    drafts = residual.shape[1]
    width = residual.shape[2]
    shard_len = latent_cache.shape[1]
    experts = router_weight.shape[1]
    rows_here = drafts // n_blk
    depth = n_req // 4
    if n_req == 4 * DEPTH and n_blk == 2 and n_blk * n_req * rows_here <= FUSED_ROWS:
        layer_out, updated = whole_layer(
            residual[0].reshape(n_blk, rows_here, width),
            queries[0].reshape(drafts * queries.shape[2], queries.shape[3]),
            new_latents[0],
            latent_cache[0].T,
            lengths,
            placement,
            parents,
            accepted.T,
            expert_ids.transpose(2, 0, 1),
            value_weight,
            out_weight,
            norm_gain,
            router_weight.T,
            gate_weight[0].T,
            up_weight[0].T,
            down_weight[0],
        )
        return (layer_out[None], updated.T[None])

    request = lax.dynamic_index_in_dim(placement, req, 0, keepdims=False)
    length = lax.dynamic_index_in_dim(lengths, request, 0, keepdims=False)
    parent_row = lax.dynamic_index_in_dim(parents, request, 0, keepdims=False)
    taken = lax.dynamic_index_in_dim(accepted, request, 0, keepdims=False)

    named = jnp.any(
        expert_ids[:, :, :, None] == jnp.arange(experts, dtype=jnp.int32), axis=2
    ).astype(jnp.bfloat16)
    seat = (placement[:, None] == jnp.arange(n_req, dtype=jnp.int32)[None, :]).astype(jnp.bfloat16)
    named = jnp.einsum("sr,rte->ste", seat, named, preferred_element_type=jnp.float32)
    named = named.reshape(depth, 4, n_blk, rows_here, experts)

    piece = lax.all_gather(latent_cache[0], "blk", axis=0, tiled=True)
    attn = attend_slot(
        queries[0], new_latents[0], piece, length, parent_row, value_weight, out_weight
    )
    attn = attn.reshape(n_blk, rows_here, width)
    home_rows = residual.reshape(n_blk, rows_here, width)
    gain = norm_gain.reshape(1, width)
    mid, gathered = gather_rows(attn, home_rows, gain, n_req, n_blk)
    rows = gathered.reshape(n_req * drafts, width)
    score_e = jax.nn.sigmoid(jnp.dot(rows, router_weight, preferred_element_type=jnp.float32))
    chosen = named.transpose(2, 1, 0, 3, 4).reshape(n_req * drafts, experts) * score_e
    mine = jnp.arange(experts, dtype=jnp.int32)[None, :] == req
    gate = (
        route_scale
        * jnp.sum(jnp.where(mine, chosen, 0.0), axis=1, keepdims=True)
        / jnp.sum(chosen, axis=1, keepdims=True)
    )
    act = (
        jax.nn.silu(jnp.dot(rows, gate_weight[0], preferred_element_type=jnp.float32))
        * jnp.dot(rows, up_weight[0], preferred_element_type=jnp.float32)
    ).astype(jnp.bfloat16)
    parts = jnp.dot(act, down_weight[0], preferred_element_type=jnp.float32) * gate
    parts = parts.astype(jnp.bfloat16).reshape(n_blk, 4, depth, rows_here, width)
    layer_out = scatter_rows(parts, mid, n_req, n_blk)

    stored = latent_cache[0]
    chosen_rows = new_latents[0][taken]
    targets = length + jnp.arange(taken.shape[0], dtype=jnp.int32) - block_index * shard_len
    hit = jnp.arange(shard_len, dtype=jnp.int32)[:, None] == targets[None, :]
    written = jnp.dot(
        hit.astype(jnp.bfloat16), chosen_rows, preferred_element_type=jnp.float32
    ).astype(jnp.bfloat16)
    updated = jnp.where(jnp.any(hit, axis=1)[:, None], written, stored)
    return (layer_out[None], updated[None])


def solution(mesh):
    return jax.shard_map(
        on_device,
        mesh=mesh,
        in_specs=(
            P("req", None, None),
            P("req", None, "blk", None),
            P("req", None, None),
            P("req", "blk", None),
            P(),
            P(),
            P(),
            P(),
            P(),
            P("blk", None, None),
            P("blk", None),
            P(),
            P(),
            P("req", None, "blk"),
            P("req", None, "blk"),
            P("req", "blk", None),
        ),
        out_specs=(P("req", "blk", None), P("req", "blk", None)),
        check_vma=False,
    )
```

```python
import functools

import jax
import jax.numpy as jnp
from jax import lax
from jax.experimental import pallas as pl
from jax.experimental.pallas import tpu as pltpu
from jax.sharding import PartitionSpec as P

LATENT = 512
TOP = 6
MESH = pl.DeviceIdType.MESH
VMEM_LIMIT = 56 * 1024 * 1024
FUSED_ROWS = 1024
DEPTH = 4

score_scale = 0.07216878364870322
route_scale = 2.446
norm_eps = 1e-06
far_below = -1e30


def ancestors(parent_row):
    span = parent_row.shape[0]
    links = (parent_row[:, None] == jnp.arange(span, dtype=jnp.int32)[None, :]).astype(jnp.float32)
    reach = jnp.eye(span, dtype=jnp.float32) + links
    for _ in range(span.bit_length()):
        reach = jnp.minimum(jnp.dot(reach, reach, precision=lax.Precision.HIGHEST), 1.0)
    return reach


def attend_kernel(length_ref, query_ref, fresh_ref, keys_ref, reach_ref, value_ref, out_weight_ref, attn_ref):
    drafts = fresh_ref.shape[0]
    heads = value_ref.shape[0]
    lines = drafts * heads
    query, fresh, keys = query_ref[...], fresh_ref[...], keys_ref[...]
    line = lax.broadcasted_iota(jnp.int32, (lines, drafts), 0)
    first = lax.broadcasted_iota(jnp.int32, (lines, drafts), 1) * heads
    owner = ((line >= first) & (line < first + heads)).astype(jnp.float32)
    reach = jnp.dot(owner, reach_ref[...], preferred_element_type=jnp.float32)
    stored = jnp.dot(query, keys, preferred_element_type=jnp.float32) * score_scale
    where = lax.broadcasted_iota(jnp.int32, stored.shape, 1)
    stored = jnp.where(where < length_ref[0], stored, far_below)
    own = jnp.where(reach > 0.5, dot_nt(query, fresh) * score_scale, far_below)
    top = jnp.maximum(
        jnp.max(stored, axis=1, keepdims=True), jnp.max(own, axis=1, keepdims=True)
    )
    stored = jnp.exp(stored - top)
    own = jnp.exp(own - top)
    total = jnp.sum(stored, axis=1, keepdims=True) + jnp.sum(own, axis=1, keepdims=True)
    acc = dot_nt(stored.astype(jnp.bfloat16), keys[:LATENT]) + jnp.dot(
        own.astype(jnp.bfloat16), fresh[:, :LATENT], preferred_element_type=jnp.float32
    )
    context = (acc / total).astype(jnp.bfloat16)
    row = lax.broadcasted_iota(jnp.int32, (drafts, lines), 0) * heads
    column = lax.broadcasted_iota(jnp.int32, (drafts, lines), 1)
    outs = []
    for head in range(heads):
        select = (column == row + head).astype(jnp.bfloat16)
        one = jnp.dot(select, context, preferred_element_type=jnp.float32).astype(jnp.bfloat16)
        outs.append(
            jnp.dot(one, value_ref[head], preferred_element_type=jnp.float32).astype(jnp.bfloat16)
        )
    attn_ref[...] = jnp.dot(
        jnp.concatenate(outs, axis=1), out_weight_ref[...], preferred_element_type=jnp.float32
    )


def attend_slot(query, fresh, piece, length, parent_row, value_weight, out_weight):
    drafts, heads, width = query.shape
    vmem = pl.BlockSpec(memory_space=pltpu.VMEM)
    return pl.pallas_call(
        attend_kernel,
        out_shape=jax.ShapeDtypeStruct((drafts, out_weight.shape[1]), jnp.float32),
        in_specs=[pl.BlockSpec(memory_space=pltpu.SMEM)] + [vmem] * 6,
        out_specs=vmem,
        compiler_params=pltpu.CompilerParams(vmem_limit_bytes=VMEM_LIMIT),
    )(
        length.reshape(1),
        query.reshape(drafts * heads, width),
        fresh,
        piece.T,
        ancestors(parent_row),
        value_weight,
        out_weight,
    )


class Place:
    def __init__(self, n_req, n_blk):
        self.depth = n_req // 4
        self.n_blk = n_blk
        req = lax.axis_index("req")
        self.blk = lax.axis_index("blk")
        self.z = req // 4
        self.y = (req // 2) % 2
        self.x = req % 2
        self.swap = self.blk % 2
        self.a = self.y * (1 - self.swap) + self.x * self.swap
        self.b = self.x * (1 - self.swap) + self.y * self.swap
        self.home = self.group(self.a, self.b)

    def group(self, a, b):
        return a * (2 - self.swap) + b * (1 + self.swap)

    def device(self, z, a, b):
        return (z * 4 + self.group(a, b), self.blk)

    def far(self, step):
        return (self.z + step) % self.depth

    def a_side(self):
        return self.device(self.z, 1 - self.a, self.b)

    def b_side(self):
        return self.device(self.z, self.a, 1 - self.b)

    def z_side(self, step):
        return self.device(self.far(step), self.a, self.b)

    def sibling_blk(self, step):
        return (self.blk + step) % self.n_blk

    def sibling(self, step):
        return (self.z * 4 + self.home, self.sibling_blk(step))

    def greet(self):
        barrier = pltpu.get_barrier_semaphore()
        others = [self.a_side(), self.b_side()]
        others += [self.z_side(step) for step in range(1, self.depth)]
        others += [self.sibling(step) for step in range(1, self.n_blk)]
        for other in others:
            pl.semaphore_signal(barrier, inc=1, device_id=other, device_id_type=MESH)
        pl.semaphore_wait(barrier, len(others))


def send(src, dst, send_sem, recv_sem, target):
    return pltpu.make_async_remote_copy(
        src_ref=src,
        dst_ref=dst,
        send_sem=send_sem,
        recv_sem=recv_sem,
        device_id=target,
        device_id_type=MESH,
    )


def gather_kernel(
    n_req,
    n_blk,
    attn_ref,
    res_ref,
    gain_ref,
    mid_ref,
    rows_ref,
    outbox,
    inbox,
    box_send,
    box_recv,
    z_send,
    a_send,
    b_send,
    land,
    sib_send,
    sib_recv,
):
    at = Place(n_req, n_blk)
    depth, blk, home = at.depth, at.blk, at.home
    outbox[...] = attn_ref[...].astype(jnp.bfloat16)
    at.greet()
    swaps = []
    for step in range(1, n_blk):
        copy = send(
            outbox.at[at.sibling_blk(step)],
            inbox.at[step - 1],
            box_send.at[step - 1],
            box_recv.at[step - 1],
            at.sibling(step),
        )
        copy.start()
        swaps.append(copy)
    mid = res_ref[blk].astype(jnp.float32) + attn_ref[blk]
    for step in range(1, n_blk):
        swaps[step - 1].wait_recv()
        mid = mid + inbox[step - 1].astype(jnp.float32)
    mid_ref[...] = mid
    scale = lax.rsqrt(jnp.mean(mid * mid, axis=1, keepdims=True) + norm_eps)
    rows_ref[blk, home, at.z] = (mid * scale * gain_ref[...].astype(jnp.float32)).astype(jnp.bfloat16)

    waits = []

    def forward(group, z, send_sem, target):
        piece = rows_ref.at[blk, group, z]
        copy = send(piece, piece, send_sem, land.at[group, z], target)
        copy.start()
        waits.append(copy)

    def landed(group, z):
        piece = rows_ref.at[blk, group, z]
        send(piece, piece, z_send.at[0], land.at[group, z], at.a_side()).wait_recv()

    def share(group):
        for step in range(1, n_blk):
            block = rows_ref.at[blk, group]
            copy = send(
                block, block, sib_send.at[step - 1, group], sib_recv.at[step - 1, group], at.sibling(step)
            )
            copy.start()
            waits.append(copy)

    for step in range(1, depth):
        forward(home, at.z, z_send.at[step - 1], at.z_side(step))
    forward(home, at.z, b_send.at[0, 0], at.b_side())
    forward(home, at.z, a_send.at[0], at.a_side())
    for step in range(1, depth):
        z = at.far(step)
        landed(home, z)
        forward(home, z, b_send.at[0, step], at.b_side())
        forward(home, z, a_send.at[step], at.a_side())
    share(home)
    over = at.group(1 - at.a, at.b)
    for step in range(depth):
        z = at.far(step)
        landed(over, z)
        forward(over, z, b_send.at[1, step], at.b_side())
    share(over)
    for a in (at.a, 1 - at.a):
        group = at.group(a, 1 - at.b)
        for step in range(depth):
            landed(group, at.far(step))
        share(group)
    for step in range(1, n_blk):
        source = (blk + n_blk - step) % n_blk
        for group in range(4):
            block = rows_ref.at[source, group]
            send(
                block, block, sib_send.at[step - 1, group], sib_recv.at[step - 1, group], at.sibling(step)
            ).wait_recv()
    for copy in waits:
        copy.wait_send()
    for copy in swaps:
        copy.wait_send()


def gather_rows(attn, residual, gain, n_req, n_blk):
    _, rows, width = attn.shape
    depth = n_req // 4
    vmem = pl.BlockSpec(memory_space=pltpu.VMEM)
    dma = pltpu.SemaphoreType.DMA
    sibs = max(n_blk - 1, 1)
    return pl.pallas_call(
        functools.partial(gather_kernel, n_req, n_blk),
        out_shape=(
            jax.ShapeDtypeStruct((rows, width), jnp.float32),
            jax.ShapeDtypeStruct((n_blk, 4, depth, rows, width), jnp.bfloat16),
        ),
        in_specs=[vmem] * 3,
        out_specs=(vmem, vmem),
        scratch_shapes=[
            pltpu.VMEM((n_blk, rows, width), jnp.bfloat16),
            pltpu.VMEM((sibs, rows, width), jnp.bfloat16),
            dma((sibs,)),
            dma((sibs,)),
            dma((depth,)),
            dma((depth,)),
            dma((2, depth)),
            dma((4, depth)),
            dma((sibs, 4)),
            dma((sibs, 4)),
        ],
        compiler_params=pltpu.CompilerParams(
            collective_id=0, has_side_effects=True, vmem_limit_bytes=VMEM_LIMIT
        ),
    )(attn, residual, gain)


def scatter_kernel(
    n_req,
    n_blk,
    part_ref,
    mid_ref,
    out_ref,
    sib_in,
    b_in,
    a_in,
    z_in,
    sums,
    sib_send,
    sib_recv,
    b_send,
    b_recv,
    a_send,
    a_recv,
    z_send,
    z_recv,
):
    at = Place(n_req, n_blk)
    depth, blk = at.depth, at.blk
    at.greet()
    waits = []
    order = [
        at.group(1 - at.a, 1 - at.b),
        at.group(at.a, 1 - at.b),
        at.group(1 - at.a, at.b),
        at.home,
    ]

    def put(src, dst, send_sem, recv_sem, target):
        copy = send(src, dst, send_sem, recv_sem, target)
        copy.start()
        waits.append(copy)

    for k in range(4):
        for step in range(1, n_blk):
            other_swap = at.sibling_blk(step) % 2
            a = at.y * (1 - other_swap) + at.x * other_swap
            b = at.x * (1 - other_swap) + at.y * other_swap
            ta = a if k in (1, 3) else 1 - a
            tb = b if k in (2, 3) else 1 - b
            group = ta * (2 - other_swap) + tb * (1 + other_swap)
            put(
                part_ref.at[at.sibling_blk(step), group],
                sib_in.at[step - 1, k],
                sib_send.at[step - 1, k],
                sib_recv.at[step - 1, k],
                at.sibling(step),
            )

    def wait_sib(k):
        for step in range(1, n_blk):
            box = sib_in.at[step - 1, k]
            send(box, box, sib_send.at[step - 1, k], sib_recv.at[step - 1, k], at.sibling(step)).wait_recv()

    def own(k, z):
        total = part_ref[blk, order[k], z].astype(jnp.float32)
        for step in range(1, n_blk):
            total = total + sib_in[step - 1, k, z].astype(jnp.float32)
        return total

    def await_box(box, send_sem, recv_sem):
        send(box, box, send_sem, recv_sem, at.a_side()).wait_recv()

    steps = list(range(1, depth)) + [0]
    for k in (0, 1):
        wait_sib(k)
        for step in steps:
            z = at.far(step)
            sums[k, step] = own(k, z).astype(jnp.bfloat16)
            put(sums.at[k, step], b_in.at[k, step], b_send.at[k, step], b_recv.at[k, step], at.b_side())
    wait_sib(2)
    for step in steps:
        z = at.far(step)
        total = own(2, z)
        await_box(b_in.at[0, step], b_send.at[0, step], b_recv.at[0, step])
        sums[2, step] = (total + b_in[0, step].astype(jnp.float32)).astype(jnp.bfloat16)
        put(sums.at[2, step], a_in.at[step], a_send.at[step], a_recv.at[step], at.a_side())
    wait_sib(3)
    keep = None
    for step in steps:
        z = at.far(step)
        total = own(3, z)
        await_box(b_in.at[1, step], b_send.at[1, step], b_recv.at[1, step])
        total = total + b_in[1, step].astype(jnp.float32)
        await_box(a_in.at[step], a_send.at[step], a_recv.at[step])
        total = total + a_in[step].astype(jnp.float32)
        if step > 0:
            sums[3, step] = total.astype(jnp.bfloat16)
            put(sums.at[3, step], z_in.at[step - 1], z_send.at[step - 1], z_recv.at[step - 1], at.z_side(step))
        else:
            keep = total
    total = mid_ref[...] + keep
    for step in range(1, depth):
        await_box(z_in.at[step - 1], z_send.at[step - 1], z_recv.at[step - 1])
        total = total + z_in[step - 1].astype(jnp.float32)
    out_ref[...] = total.astype(jnp.bfloat16)
    for copy in waits:
        copy.wait_send()


def scatter_rows(parts, mid, n_req, n_blk):
    _, _, depth, rows, width = parts.shape
    vmem = pl.BlockSpec(memory_space=pltpu.VMEM)
    dma = pltpu.SemaphoreType.DMA
    sibs = max(n_blk - 1, 1)
    far = max(depth - 1, 1)
    box = lambda *dims: pltpu.VMEM(dims + (rows, width), jnp.bfloat16)
    return pl.pallas_call(
        functools.partial(scatter_kernel, n_req, n_blk),
        out_shape=jax.ShapeDtypeStruct((rows, width), jnp.bfloat16),
        in_specs=[vmem] * 2,
        out_specs=vmem,
        scratch_shapes=[
            box(sibs, 4, depth),
            box(2, depth),
            box(depth),
            box(far),
            box(4, depth),
            dma((sibs, 4)),
            dma((sibs, 4)),
            dma((2, depth)),
            dma((2, depth)),
            dma((depth,)),
            dma((depth,)),
            dma((far,)),
            dma((far,)),
        ],
        compiler_params=pltpu.CompilerParams(
            collective_id=1, has_side_effects=True, vmem_limit_bytes=VMEM_LIMIT
        ),
    )(parts, mid)


def dot_nt(left, right):
    return lax.dot_general(left, right, (((1,), (1,)), ((), ())), preferred_element_type=jnp.float32)


def whole_kernel(
    placement_ref,
    lengths_ref,
    accepted_ref,
    parents_hbm,
    ids_hbm,
    gain_hbm,
    router_hbm,
    res_hbm,
    query_hbm,
    fresh_hbm,
    keys_hbm,
    value_hbm,
    out_weight_hbm,
    gate_hbm,
    up_hbm,
    down_hbm,
    out_ref,
    updated_ref,
    parents_ref,
    ids_ref,
    gain_ref,
    router_ref,
    res_ref,
    query_ref,
    fresh_ref,
    keys_ref,
    value_ref,
    out_weight_ref,
    gate_ref,
    up_ref,
    down_ref,
    gate_t,
    up_t,
    attn_ref,
    mid_ref,
    keep_ref,
    outbox,
    inbox,
    rows_ref,
    flat,
    x_ref,
    act_ref,
    named_ref,
    part_ref,
    f_in,
    a_in,
    b_in,
    q_in,
    z_in,
    plane_sum,
    home_sum,
    local_sem,
    value_sem,
    swap_send,
    swap_recv,
    gz_send,
    gf_send,
    ga_send,
    gb_send,
    gq_send,
    land,
    rf_send,
    rf_recv,
    ra_send,
    ra_recv,
    rb_send,
    rb_recv,
    rq_send,
    rq_recv,
    rz_send,
    rz_recv,
):
    at = Place(4 * DEPTH, 2)
    blk, z, home = at.blk, at.z, at.home
    over = at.group(1 - at.a, at.b)
    side = at.group(at.a, 1 - at.b)
    far = at.group(1 - at.a, 1 - at.b)
    req = lax.axis_index("req")
    planes = [z, z + 1 - 2 * (z % 2), 2 - z // 2, 3 - 3 * (z // 2)]
    sibling = at.sibling(1)
    peers = [None] + [at.device(plane, at.a, at.b) for plane in planes[1:]]
    lines = query_ref.shape[0]
    drafts = fresh_ref.shape[0]
    heads = lines // drafts
    rows = mid_ref.shape[0]
    shard = keys_ref.shape[2]
    hidden = gate_ref.shape[1]
    waits = []

    barrier = pltpu.get_barrier_semaphore()
    diagonal = at.device(z, 1 - at.a, 1 - at.b)
    partners = [sibling, at.a_side(), at.b_side(), diagonal] + peers[1:]
    for partner in partners:
        pl.semaphore_signal(barrier, inc=1, device_id=partner, device_id_type=MESH)

    moves = [
        (query_hbm, query_ref),
        (keys_hbm, keys_ref.at[0]),
        (fresh_hbm, fresh_ref),
        (parents_hbm, parents_ref),
        (out_weight_hbm, out_weight_ref),
        (res_hbm, res_ref),
        (gain_hbm, gain_ref),
        (ids_hbm, ids_ref),
        (router_hbm, router_ref),
        (gate_hbm, gate_ref.at[0]),
        (up_hbm, up_ref.at[0]),
        (down_hbm, down_ref.at[0]),
    ]
    loads = [pltpu.make_async_copy(src, dst, local_sem.at[i]) for i, (src, dst) in enumerate(moves)]
    (
        query_load,
        keys_load,
        fresh_load,
        parents_load,
        out_weight_load,
        res_load,
        gain_load,
        ids_load,
        router_load,
        gate_load,
        up_load,
        down_load,
    ) = loads
    value_loads = [
        pltpu.make_async_copy(value_hbm.at[head], value_ref.at[:, pl.ds(head * 128, 128)], value_sem.at[head])
        for head in range(heads)
    ]
    for load in loads[:4] + value_loads + loads[4:]:
        load.start()

    def put(src, dst, send_sem, recv_sem, target):
        copy = send(src, dst, send_sem, recv_sem, target)
        copy.start()
        waits.append(copy)

    def await_box(box, send_sem, recv_sem):
        send(box, box, send_sem, recv_sem, sibling).wait_recv()

    swaps = [
        (keys_hbm, keys_ref.at[1]),
        (gate_hbm, gate_ref.at[1]),
        (up_hbm, up_ref.at[1]),
        (down_hbm, down_ref.at[1]),
    ]

    def swap(i):
        put(swaps[i][0], swaps[i][1], swap_send.at[i], swap_recv.at[i], sibling)

    def swapped(i):
        await_box(swaps[i][1], swap_send.at[i], swap_recv.at[i])

    request = placement_ref[req]
    length = lengths_ref[request]

    parents_load.wait()
    parent_row = parents_ref[pl.ds(request, 1), :]
    upper = lax.broadcasted_iota(jnp.int32, (drafts, drafts), 0)
    lower = lax.broadcasted_iota(jnp.int32, (drafts, drafts), 1)
    reach = (parent_row == upper).astype(jnp.float32) + (upper == lower).astype(jnp.float32)
    for _ in range(drafts.bit_length()):
        half = reach.astype(jnp.bfloat16)
        reach = jnp.minimum(jnp.dot(half, half, preferred_element_type=jnp.float32), 1.0)
    line = lax.broadcasted_iota(jnp.int32, (lines, drafts), 0)
    first = lax.broadcasted_iota(jnp.int32, (lines, drafts), 1) * heads
    owner = ((line >= first) & (line < first + heads)).astype(jnp.float32).astype(jnp.bfloat16)
    seen = dot_nt(owner, reach.astype(jnp.bfloat16))

    pl.semaphore_wait(barrier, len(partners))
    for i in range(4):
        swap(i)

    query_load.wait()
    fresh_load.wait()
    query, fresh = query_ref[...], fresh_ref[...]
    own = jnp.where(seen > 0.5, dot_nt(query, fresh) * score_scale, far_below)
    place = lax.broadcasted_iota(jnp.int32, (lines, shard), 1)

    def scores(i, start):
        stored = jnp.dot(query, keys_ref[i], preferred_element_type=jnp.float32) * score_scale
        return jnp.where(place + start < length, stored, far_below)

    keys_load.wait()
    near = scores(0, blk * shard)
    swapped(0)
    apart = scores(1, (1 - blk) * shard)
    top = jnp.maximum(
        jnp.maximum(jnp.max(near, axis=1, keepdims=True), jnp.max(apart, axis=1, keepdims=True)),
        jnp.max(own, axis=1, keepdims=True),
    )
    near, apart, own = jnp.exp(near - top), jnp.exp(apart - top), jnp.exp(own - top)
    total = (
        jnp.sum(near, axis=1, keepdims=True)
        + jnp.sum(apart, axis=1, keepdims=True)
        + jnp.sum(own, axis=1, keepdims=True)
    )
    acc = (
        dot_nt(near.astype(jnp.bfloat16), keys_ref[0, :LATENT])
        + dot_nt(apart.astype(jnp.bfloat16), keys_ref[1, :LATENT])
        + jnp.dot(own.astype(jnp.bfloat16), fresh[:, :LATENT], preferred_element_type=jnp.float32)
    )
    context = (acc * (1.0 / total)).astype(jnp.bfloat16)
    for load in value_loads:
        load.wait()
    every = jnp.dot(context, value_ref[...], preferred_element_type=jnp.float32)
    head_of = lax.broadcasted_iota(jnp.int32, every.shape, 0) % heads
    column_head = lax.broadcasted_iota(jnp.int32, every.shape, 1) // 128
    every = jnp.where(head_of == column_head, every, 0.0).astype(jnp.bfloat16)
    row = lax.broadcasted_iota(jnp.int32, (drafts, lines), 0) * heads
    column = lax.broadcasted_iota(jnp.int32, (drafts, lines), 1)
    gather = ((column >= row) & (column < row + heads)).astype(jnp.float32).astype(jnp.bfloat16)
    head_out = jnp.dot(gather, every, preferred_element_type=jnp.float32).astype(jnp.bfloat16)
    out_weight_load.wait()
    attn = jnp.dot(head_out, out_weight_ref[...], preferred_element_type=jnp.float32)
    attn_ref[0] = attn[:rows]
    attn_ref[1] = attn[rows:]
    outbox[...] = attn_ref[1 - blk].astype(jnp.bfloat16)
    put(outbox, inbox, swap_send.at[4], swap_recv.at[4], sibling)
    res_load.wait()
    gain_load.wait()
    mid = res_ref[blk].astype(jnp.float32) + attn_ref[blk]
    await_box(inbox, swap_send.at[4], swap_recv.at[4])
    mid = mid + inbox[...].astype(jnp.float32)
    mid_ref[...] = mid
    scale = lax.rsqrt(jnp.mean(mid * mid, axis=1, keepdims=True) + norm_eps)
    rows_ref[z, home] = (mid * scale * gain_ref[...].astype(jnp.float32).reshape(1, -1)).astype(jnp.bfloat16)

    def forward(plane, group, send_sem, target):
        piece = rows_ref.at[plane, group]
        put(piece, piece, send_sem, land.at[plane, group], target)

    def landed(plane, group):
        await_box(rows_ref.at[plane, group], gz_send.at[0], land.at[plane, group])

    def spread(k):
        if k > 0:
            landed(planes[k], home)
        forward(planes[k], home, gf_send.at[k], diagonal)
        forward(planes[k], home, ga_send.at[k], at.a_side())
        forward(planes[k], home, gb_send.at[k], at.b_side())

    def spread_plane():
        for i, group in enumerate((over, side, far)):
            landed(z, group)
            forward(z, group, gq_send.at[i], peers[1])

    forward(z, home, gz_send.at[3], peers[3])
    leading = waits.pop()
    spread(0)

    pick_draft = lax.broadcasted_iota(jnp.int32, (drafts, shard), 0)
    pick_place = lax.broadcasted_iota(jnp.int32, (drafts, shard), 1)
    picked = jnp.zeros((drafts, shard), jnp.float32)
    for i in range(accepted_ref.shape[0]):
        target = length + i - blk * shard
        picked = jnp.where((pick_draft == accepted_ref[i, request]) & (pick_place == target), 1.0, picked)
    hit = jnp.max(picked, axis=0, keepdims=True)
    written = lax.dot_general(
        fresh, picked.astype(jnp.bfloat16), (((0,), (0,)), ((), ())), preferred_element_type=jnp.float32
    )
    updated_ref[...] = jnp.where(hit > 0.5, written, keys_ref[0].astype(jnp.float32)).astype(jnp.bfloat16)

    ids_load.wait()
    experts = router_ref.shape[0]
    expert_at = lax.broadcasted_iota(jnp.int32, (experts, drafts), 0)
    seat = (
        lax.broadcasted_iota(jnp.int32, (rows, drafts), 1)
        == lax.broadcasted_iota(jnp.int32, (rows, drafts), 0) + blk * rows
    ).astype(jnp.float32).astype(jnp.bfloat16)
    for k in range(DEPTH):
        for group in range(4):
            asked = placement_ref[planes[k] * 4 + group]
            names = jnp.zeros((experts, drafts), jnp.float32)
            for j in range(TOP):
                names = jnp.where(ids_ref[j, pl.ds(asked, 1), :] == expert_at, 1.0, names)
            named_ref[k, pl.ds(group * rows, rows), :] = dot_nt(seat, names.astype(jnp.bfloat16))

    def turn(i):
        for source, dest in ((gate_ref, gate_t), (up_ref, up_t)):
            for c in range(source.shape[2] // 256):
                dest[i, pl.ds(c * 256, 256), :] = source[i, :, pl.ds(c * 256, 256)].T

    def load_rows(k):
        for group in range(4):
            flat[pl.ds(group * rows, rows), :] = rows_ref[planes[k], group].astype(jnp.float32)
        x_ref[...] = flat[...].astype(jnp.bfloat16)

    def gate_of(k):
        chosen = named_ref[k] * jax.nn.sigmoid(dot_nt(x_ref[...], router_ref[...]))
        mine = lax.broadcasted_iota(jnp.int32, chosen.shape, 1) == req
        return (
            route_scale
            * jnp.sum(jnp.where(mine, chosen, 0.0), axis=1, keepdims=True)
            / jnp.sum(chosen, axis=1, keepdims=True)
        )

    def expand(i):
        x = x_ref[...]
        act_ref[i] = (
            jax.nn.silu(jnp.dot(x, gate_t[i], preferred_element_type=jnp.float32))
            * jnp.dot(x, up_t[i], preferred_element_type=jnp.float32)
        ).astype(jnp.bfloat16)

    def take(k, group):
        start = pl.multiple_of(group * rows, 8)
        part_ref[k, group] = flat[pl.ds(start, rows), :].astype(jnp.bfloat16)

    def contract(k, gate):
        flat[...] = (
            jnp.dot(act_ref[0], down_ref[0], preferred_element_type=jnp.float32)
            + jnp.dot(act_ref[1], down_ref[1], preferred_element_type=jnp.float32)
        ) * gate
        if k == 0:
            for group in range(4):
                take(k, group)

    def return_plane():
        for i, group in enumerate((far, over, side, home)):
            take(1, group)
            put(part_ref.at[1, group], q_in.at[i], rq_send.at[i], rq_recv.at[i], peers[1])

    def return_far(k):
        take(k, far)
        put(part_ref.at[k, far], f_in.at[k], rf_send.at[k], rf_recv.at[k], diagonal)
        take(k, over)
        put(part_ref.at[k, over], a_in.at[k], ra_send.at[k], ra_recv.at[k], at.a_side())
        take(k, side)
        put(part_ref.at[k, side], b_in.at[k], rb_send.at[k], rb_recv.at[k], at.b_side())
        take(k, home)

    def plane_total(i, group):
        await_box(q_in.at[i], rq_send.at[i], rq_recv.at[i])
        return part_ref[0, group].astype(jnp.float32) + q_in[i].astype(jnp.float32)

    def return_own():
        plane_sum[0] = plane_total(0, far).astype(jnp.bfloat16)
        put(plane_sum.at[0], f_in.at[0], rf_send.at[0], rf_recv.at[0], diagonal)
        plane_sum[1] = plane_total(1, over).astype(jnp.bfloat16)
        put(plane_sum.at[1], a_in.at[0], ra_send.at[0], ra_recv.at[0], at.a_side())
        plane_sum[2] = plane_total(2, side).astype(jnp.bfloat16)
        put(plane_sum.at[2], b_in.at[0], rb_send.at[0], rb_recv.at[0], at.b_side())
        keep_ref[...] = mid_ref[...] + plane_total(3, home)

    def sum_home(k, here):
        for box, send_sem, recv_sem in ((f_in, rf_send, rf_recv), (a_in, ra_send, ra_recv), (b_in, rb_send, rb_recv)):
            await_box(box.at[k], send_sem.at[k], recv_sem.at[k])
            here = here + box[k].astype(jnp.float32)
        return here

    def return_home(k):
        home_sum[k] = sum_home(k, part_ref[k, home].astype(jnp.float32)).astype(jnp.bfloat16)
        put(home_sum.at[k], z_in.at[z], rz_send.at[k], rz_recv.at[z], peers[k])

    def settle(k):
        if k == 1:
            landed(planes[k], home)
        if k > 0:
            for group in (over, side, far):
                landed(planes[k], group)
        load_rows(k)
        return gate_of(k)

    gate_load.wait()
    up_load.wait()
    turn(0)
    router_load.wait()
    leading.wait_send()
    forward(z, home, gz_send.at[2], peers[2])
    forward(z, home, gz_send.at[1], peers[1])
    spread(3)
    spread_plane()
    spread(2)
    swapped(1)
    swapped(2)
    turn(1)
    gate = settle(0)
    expand(0)
    expand(1)
    down_load.wait()
    swapped(3)
    contract(0, gate)
    for k in (1, 3, 2):
        gate = settle(k)
        expand(0)
        expand(1)
        contract(k, gate)
        if k == 1:
            return_plane()
        else:
            return_far(k)
    return_own()
    return_home(3)
    return_home(2)
    result = sum_home(0, keep_ref[...])
    for k in (3, 2):
        await_box(z_in.at[planes[k]], rz_send.at[k], rz_recv.at[planes[k]])
        result = result + z_in[planes[k]].astype(jnp.float32)
    out_ref[...] = result.astype(jnp.bfloat16)
    for copy in waits:
        copy.wait_send()


def whole_layer(
    residual,
    query,
    fresh,
    keys,
    lengths,
    placement,
    parents,
    accepted,
    expert_ids,
    value_weight,
    out_weight,
    gain,
    router_weight,
    gate_weight,
    up_weight,
    down_weight,
):
    n_blk, rows, width = residual.shape
    hidden = gate_weight.shape[0]
    shard = keys.shape[1]
    lines = query.shape[0]
    heads = value_weight.shape[0]
    experts = router_weight.shape[0]
    smem = pl.BlockSpec(memory_space=pltpu.SMEM)
    hbm = pl.BlockSpec(memory_space=pl.ANY)
    vmem = pl.BlockSpec(memory_space=pltpu.VMEM)
    dma = pltpu.SemaphoreType.DMA
    like = lambda a: pltpu.VMEM(a.shape, a.dtype)
    pair = lambda a: pltpu.VMEM((2,) + a.shape, a.dtype)
    box = lambda *dims: pltpu.VMEM(dims + (rows, width), jnp.bfloat16)
    f32 = lambda *dims: pltpu.VMEM(dims, jnp.float32)
    return pl.pallas_call(
        whole_kernel,
        out_shape=(pltpu.VMEM((rows, width), jnp.bfloat16), pltpu.VMEM(keys.shape, jnp.bfloat16)),
        in_specs=[smem] * 3 + [hbm] * 13,
        out_specs=(vmem, vmem),
        scratch_shapes=[
            like(parents),
            like(expert_ids),
            like(gain),
            like(router_weight),
            like(residual),
            like(query),
            like(fresh),
            pair(keys),
            pltpu.VMEM((value_weight.shape[1], heads * value_weight.shape[2]), jnp.bfloat16),
            like(out_weight),
            pair(gate_weight),
            pair(up_weight),
            pair(down_weight),
            pltpu.VMEM((2, width, hidden), jnp.bfloat16),
            pltpu.VMEM((2, width, hidden), jnp.bfloat16),
            f32(n_blk, rows, width),
            f32(rows, width),
            f32(rows, width),
            box(),
            box(),
            box(DEPTH, 4),
            f32(4 * rows, width),
            pltpu.VMEM((4 * rows, width), jnp.bfloat16),
            pltpu.VMEM((2, 4 * rows, hidden), jnp.bfloat16),
            f32(DEPTH, 4 * rows, experts),
            box(DEPTH, 4),
            box(DEPTH),
            box(DEPTH),
            box(DEPTH),
            box(4),
            box(DEPTH),
            box(3),
            box(DEPTH),
            dma((12,)),
            dma((heads,)),
            dma((5,)),
            dma((5,)),
            dma((DEPTH,)),
            dma((DEPTH,)),
            dma((DEPTH,)),
            dma((DEPTH,)),
            dma((3,)),
            dma((DEPTH, 4)),
            dma((DEPTH,)),
            dma((DEPTH,)),
            dma((DEPTH,)),
            dma((DEPTH,)),
            dma((DEPTH,)),
            dma((DEPTH,)),
            dma((4,)),
            dma((4,)),
            dma((DEPTH,)),
            dma((DEPTH,)),
        ],
        compiler_params=pltpu.CompilerParams(
            collective_id=2, has_side_effects=True, vmem_limit_bytes=VMEM_LIMIT
        ),
    )(
        placement,
        lengths,
        accepted,
        parents,
        expert_ids,
        gain,
        router_weight,
        residual,
        query,
        fresh,
        keys,
        value_weight,
        out_weight,
        gate_weight,
        up_weight,
        down_weight,
    )


def on_device(
    residual,
    queries,
    new_latents,
    latent_cache,
    lengths,
    placement,
    parents,
    accepted,
    expert_ids,
    value_weight,
    out_weight,
    norm_gain,
    router_weight,
    gate_weight,
    up_weight,
    down_weight,
):
    req = lax.axis_index("req")
    block_index = lax.axis_index("blk")
    n_req = lax.axis_size("req")
    n_blk = lax.axis_size("blk")
    drafts = residual.shape[1]
    width = residual.shape[2]
    shard_len = latent_cache.shape[1]
    experts = router_weight.shape[1]
    rows_here = drafts // n_blk
    depth = n_req // 4
    if n_req == 4 * DEPTH and n_blk == 2 and n_blk * n_req * rows_here <= FUSED_ROWS:
        layer_out, updated = whole_layer(
            residual[0].reshape(n_blk, rows_here, width),
            queries[0].reshape(drafts * queries.shape[2], queries.shape[3]),
            new_latents[0],
            latent_cache[0].T,
            lengths,
            placement,
            parents,
            accepted.T,
            expert_ids.transpose(2, 0, 1),
            value_weight,
            out_weight,
            norm_gain,
            router_weight.T,
            gate_weight[0].T,
            up_weight[0].T,
            down_weight[0],
        )
        return (layer_out[None], updated.T[None])

    request = lax.dynamic_index_in_dim(placement, req, 0, keepdims=False)
    length = lax.dynamic_index_in_dim(lengths, request, 0, keepdims=False)
    parent_row = lax.dynamic_index_in_dim(parents, request, 0, keepdims=False)
    taken = lax.dynamic_index_in_dim(accepted, request, 0, keepdims=False)

    named = jnp.any(
        expert_ids[:, :, :, None] == jnp.arange(experts, dtype=jnp.int32), axis=2
    ).astype(jnp.bfloat16)
    seat = (placement[:, None] == jnp.arange(n_req, dtype=jnp.int32)[None, :]).astype(jnp.bfloat16)
    named = jnp.einsum("sr,rte->ste", seat, named, preferred_element_type=jnp.float32)
    named = named.reshape(depth, 4, n_blk, rows_here, experts)

    piece = lax.all_gather(latent_cache[0], "blk", axis=0, tiled=True)
    attn = attend_slot(
        queries[0], new_latents[0], piece, length, parent_row, value_weight, out_weight
    )
    attn = attn.reshape(n_blk, rows_here, width)
    home_rows = residual.reshape(n_blk, rows_here, width)
    gain = norm_gain.reshape(1, width)
    mid, gathered = gather_rows(attn, home_rows, gain, n_req, n_blk)
    rows = gathered.reshape(n_req * drafts, width)
    score_e = jax.nn.sigmoid(jnp.dot(rows, router_weight, preferred_element_type=jnp.float32))
    chosen = named.transpose(2, 1, 0, 3, 4).reshape(n_req * drafts, experts) * score_e
    mine = jnp.arange(experts, dtype=jnp.int32)[None, :] == req
    gate = (
        route_scale
        * jnp.sum(jnp.where(mine, chosen, 0.0), axis=1, keepdims=True)
        / jnp.sum(chosen, axis=1, keepdims=True)
    )
    act = (
        jax.nn.silu(jnp.dot(rows, gate_weight[0], preferred_element_type=jnp.float32))
        * jnp.dot(rows, up_weight[0], preferred_element_type=jnp.float32)
    ).astype(jnp.bfloat16)
    parts = jnp.dot(act, down_weight[0], preferred_element_type=jnp.float32) * gate
    parts = parts.astype(jnp.bfloat16).reshape(n_blk, 4, depth, rows_here, width)
    layer_out = scatter_rows(parts, mid, n_req, n_blk)

    stored = latent_cache[0]
    chosen_rows = new_latents[0][taken]
    targets = length + jnp.arange(taken.shape[0], dtype=jnp.int32) - block_index * shard_len
    hit = jnp.arange(shard_len, dtype=jnp.int32)[:, None] == targets[None, :]
    written = jnp.dot(
        hit.astype(jnp.bfloat16), chosen_rows, preferred_element_type=jnp.float32
    ).astype(jnp.bfloat16)
    updated = jnp.where(jnp.any(hit, axis=1)[:, None], written, stored)
    return (layer_out[None], updated[None])


def solution(mesh):
    return jax.shard_map(
        on_device,
        mesh=mesh,
        in_specs=(
            P("req", None, None),
            P("req", None, "blk", None),
            P("req", None, None),
            P("req", "blk", None),
            P(),
            P(),
            P(),
            P(),
            P(),
            P("blk", None, None),
            P("blk", None),
            P(),
            P(),
            P("req", None, "blk"),
            P("req", None, "blk"),
            P("req", "blk", None),
        ),
        out_specs=(P("req", "blk", None), P("req", "blk", None)),
        check_vma=False,
    )
```
